32 devices in a mesh: wide: 8 (over z, y), narrow: 4 (over x, core).
Axes of the slice: x: 2, y: 2, z: 4, core: 2. Of those that a mesh axis runs over, the one named last changes fastest.
Arguments:
- cond_fields: bfloat16 [4, 6824, 172], P(None, 'wide'), may hold values from -6 to 6
- target: float32 [4, 6824, 84], P(None, 'wide'), may hold values from -6 to 6
- noise_draw: float32 [4, 6824, 84], P(None, 'wide'), may hold values from -6 to 6
- noise_sigma: float32 [4], replicated, may hold values from 0.3 to 10
- grid_to_mesh: int32 [4096, 8], P('wide'), may hold values from 0 to 6823, as said below
- mesh_edges: int32 [4096, 16], P('wide'), may hold values from -1 to 4095, as said below
- mesh_to_grid: int32 [6824, 3], P('wide'), may hold values from 0 to 4095, as said below
- latitude_row: int32 [6824], P('wide'), may hold values from 0 to 180
- level_index: int32 [84], replicated, may hold values from 0 to 12
- encoder: float32 [256, 512], P('wide', 'narrow'), may hold values from -0.375 to 0.375
- up_proj: float32 [512, 3584], P('wide', 'narrow'), may hold values from -0.25 to 0.25
- down_proj: float32 [2560, 512], P('narrow', 'wide'), may hold values from -0.25 to 0.25
- readout: float32 [512, 86], P(('narrow', 'wide')), may hold values from -1 to 1.5
- encoder_moment: float32 [256, 512], P('wide', 'narrow'), may hold values from -9.536743e-07 to 9.536743e-07
- up_moment: float32 [512, 3584], P('wide', 'narrow'), may hold values from -9.536743e-07 to 9.536743e-07
- down_moment: float32 [2560, 512], P('narrow', 'wide'), may hold values from -9.536743e-07 to 9.536743e-07
- readout_moment: float32 [512, 86], P(('narrow', 'wide')), may hold values from -9.536743e-07 to 9.536743e-07
- encoder_second: float32 [256, 512], P('wide', 'narrow'), may hold values from 1.5056467e-16 to 2.4090348e-15
- up_second: float32 [512, 3584], P('wide', 'narrow'), may hold values from 1.5056467e-16 to 2.4090348e-15
- down_second: float32 [2560, 512], P('narrow', 'wide'), may hold values from 1.5056467e-16 to 2.4090348e-15
- readout_second: float32 [512, 86], P(('narrow', 'wide')), may hold values from 1.5056467e-16 to 2.4090348e-15
- encoder_average: float32 [256, 512], P('wide', 'narrow'), may hold values from -0.375 to 0.375
- up_average: float32 [512, 3584], P('wide', 'narrow'), may hold values from -0.25 to 0.25
- down_average: float32 [2560, 512], P('narrow', 'wide'), may hold values from -0.25 to 0.25
- readout_average: float32 [512, 86], P(('narrow', 'wide')), may hold values from -1 to 1.5
Outputs:
- loss_value: float32 [], replicated
- grad_norm: float32 [], replicated
- next_encoder_moment: float32 [256, 512], P('wide', 'narrow')
- next_encoder_second: float32 [256, 512], P('wide', 'narrow')
- next_encoder: float32 [256, 512], P('wide', 'narrow')
- next_encoder_average: float32 [256, 512], P('wide', 'narrow')
- encoder_copy: bfloat16 [256, 512], P('wide', 'narrow')
- next_up_moment: float32 [512, 3584], P('wide', 'narrow')
- next_up_second: float32 [512, 3584], P('wide', 'narrow')
- next_up_proj: float32 [512, 3584], P('wide', 'narrow')
- next_up_average: float32 [512, 3584], P('wide', 'narrow')
- up_copy: bfloat16 [512, 3584], P('wide', 'narrow')
- next_down_moment: float32 [2560, 512], P('narrow', 'wide')
- next_down_second: float32 [2560, 512], P('narrow', 'wide')
- next_down_proj: float32 [2560, 512], P('narrow', 'wide')
- next_down_average: float32 [2560, 512], P('narrow', 'wide')
- down_copy: bfloat16 [2560, 512], P('narrow', 'wide')
- next_readout_moment: float32 [512, 86], P(('narrow', 'wide'))
- next_readout_second: float32 [512, 86], P(('narrow', 'wide'))
- next_readout: float32 [512, 86], P(('narrow', 'wide'))
- next_readout_average: float32 [512, 86], P(('narrow', 'wide'))
- readout_copy: bfloat16 [512, 86], P(('narrow', 'wide'))
The draws below stay inside these ranges and needn't reach their ends.
Inputs may be any that keep to these rules, and one draw needn't show every extreme that they name: `grid_to_mesh`: row i names grid points of pixel block i // 512, pixels 853 b to 853 (b + 1) - 1. `mesh_edges`: slot 0 of node i is i itself; used slots name nodes j with (j - i) mod 4096 or (i - j) mod 4096 at most 512; unused slots (-1) end a row; a row uses at least 8 slots. `mesh_to_grid`: row p names mesh nodes of node block p // 853, nodes 512 b to 512 (b + 1) - 1.
All inputs are finite; a program needn't handle non-finite values.
Results may differ from the reference program's by a relative error of at most 0.0062.
The reference program's roundings to bfloat16 on the way count: a program that leaves them out, or rounds other values in their place, can miss the bound.
Values may be sent and summed in bfloat16 or wider, within the bound.
No kernel may reach another device: no remote copies, remote signals or barrier semaphores. Data moves between devices by JAX's collectives and lax.ppermute only.
A program may use at most 192 MiB of HBM per device.

```python
import math
import jax
import jax.numpy as jnp
from jax import lax

D = 512
HEADS = 4
HEAD_DIM = 128
FF = 2048
OUT = 84
IN = 256
LEVELS = 13
KM = 16
KG = 8
KD = 3
STEPS_DONE = 7
MB = 4
NODE_DEV = 512
PIX_DEV = 853
NODES = 4096
PIXELS = 6824
FEAT = 128
HID = 512
PARAMS = 3320832
N_WIDE = 8
N_NARROW = 4


def readout_like(key):
    first, second = jax.random.split(key)
    decoder = jnp.clip(jax.random.normal(first, (D, OUT), jnp.float32), -4.0, 4.0) * D ** (-0.5)
    gains = 1.0 + 0.1 * jnp.clip(jax.random.normal(second, (D, 2), jnp.float32), -4.0, 4.0)
    return jnp.concatenate([decoder, gains], axis=1)


def draw_readout(key, part):
    return readout_like(jax.random.fold_in(key, 11))


def draw_readout_average(key, part):
    return readout_like(jax.random.fold_in(key, 12))


def block_pick(key, rows_all, per_block, width, slots):
    rows = jnp.arange(rows_all, dtype=jnp.int32)[:, None]
    slot_ids = jnp.arange(slots, dtype=jnp.int32)[None, :]
    base = rows // per_block * width
    picked = base + jax.random.randint(key, (rows_all, slots), 0, width, dtype=jnp.int32)
    picked = jnp.where((slot_ids == 0) & (rows % per_block == per_block - 1), base + width - 1, picked)
    picked = jnp.where((slot_ids == 0) & (rows % per_block == 0), base, picked)
    return picked.astype(jnp.int32)


def draw_grid_to_mesh(key, part):
    return block_pick(jax.random.fold_in(key, 21), NODES, NODE_DEV, PIX_DEV, KG)


def draw_mesh_to_grid(key, part):
    return block_pick(jax.random.fold_in(key, 22), PIXELS, PIX_DEV, NODE_DEV, KD)


def draw_mesh_edges(key, part):
    first, second = jax.random.split(jax.random.fold_in(key, 23))
    rows = jnp.arange(NODES, dtype=jnp.int32)[:, None]
    slot_ids = jnp.arange(KM, dtype=jnp.int32)[None, :]
    offsets = jax.random.randint(first, (NODES, KM), -NODE_DEV, NODE_DEV + 1, dtype=jnp.int32)
    offsets = jnp.where(slot_ids == 0, 0, offsets)
    neighbour = (rows + offsets + NODES) % NODES
    count = jax.random.randint(second, (NODES, 1), KM // 2, KM + 1, dtype=jnp.int32)
    count = jnp.where(rows == 0, KM // 2, count)
    return jnp.where(slot_ids < count, neighbour, -1).astype(jnp.int32)


def with_ends(drawn, rng, low, top_value):
    shape = drawn.shape
    index_at = [jax.random.randint(jax.random.fold_in(rng, axis), (), 0, shape[axis]) for axis in range(len(shape))]
    drawn = drawn.at[tuple(index_at)].set(low)
    longest = shape.index(max(shape))
    index_at[longest] = (index_at[longest] + 1) % shape[longest]
    return drawn.at[tuple(index_at)].set(top_value)


def levels(rng, extent, cuts, least, top_value):
    level, own = 1.0, jax.random.fold_in(rng, 6)
    for dim, blocks in cuts:
        draws = jnp.exp(jax.random.uniform(jax.random.fold_in(own, dim), (blocks,), jnp.float32, least / len(cuts), top_value / len(cuts)))
        level = level * jnp.repeat(draws, extent[dim] // blocks).reshape([-1 if axis == dim else 1 for axis in range(len(extent))])
    return level


def scatter_about(own_key, shape, scale, limit, cuts=(), held_as=jnp.bfloat16):
    drawn = scale * jax.random.normal(own_key, shape, jnp.float32)
    if cuts:
        drawn = drawn * levels(own_key, shape, cuts, -0.22, 0.18)
    return jnp.clip(drawn, -limit, limit).astype(held_as)


def setup_inputs(seed: int = 0) -> dict:
    seeds = jax.random.split(jax.random.key(seed), 26)
    cond_fields = scatter_about(seeds[0], (MB, PIXELS, IN - OUT), 1.0, 6.0, ((1, 8),))
    target = scatter_about(seeds[1], (MB, PIXELS, OUT), 1.0, 6.0, ((1, 8),), jnp.float32)
    noise_draw = scatter_about(seeds[2], (MB, PIXELS, OUT), 1.0, 6.0, ((1, 8),), jnp.float32)
    noise_sigma = jnp.clip(jnp.exp(jax.random.uniform(seeds[3], (MB,), jnp.float32, math.log(0.3), math.log(10.0))), 0.3, 10.0)
    grid_to_mesh = draw_grid_to_mesh(jax.random.fold_in(seeds[25], 71), 0)
    mesh_edges = draw_mesh_edges(jax.random.fold_in(seeds[25], 71), 0)
    mesh_to_grid = draw_mesh_to_grid(jax.random.fold_in(seeds[25], 71), 0)
    latitude_row = with_ends(jax.random.randint(seeds[7], (PIXELS,), 0, 181), jax.random.fold_in(seeds[7], 1), 0, 180).astype(jnp.int32)
    level_index = with_ends(jax.random.randint(seeds[8], (OUT,), 0, LEVELS), jax.random.fold_in(seeds[8], 1), 0, LEVELS - 1).astype(jnp.int32)
    encoder = scatter_about(seeds[9], (IN, D), IN ** -0.5, 0.375, ((0, 8), (1, 4)), jnp.float32)
    up_proj = scatter_about(seeds[10], (D, 3 * D + FF), D ** -0.5, 0.25, ((0, 8), (1, 4)), jnp.float32)
    down_proj = scatter_about(seeds[11], (D + FF, D), D ** -0.5, 0.25, ((0, 4), (1, 8)), jnp.float32)
    readout = draw_readout(jax.random.fold_in(seeds[25], 71), 0)
    encoder_moment = scatter_about(seeds[13], (IN, D), (0.000111 / PARAMS ** 0.5), 9.5367431640625e-07, ((0, 8), (1, 4)), jnp.float32)
    up_moment = scatter_about(seeds[14], (D, 3 * D + FF), (0.000111 / PARAMS ** 0.5), 9.5367431640625e-07, ((0, 8), (1, 4)), jnp.float32)
    down_moment = scatter_about(seeds[15], (D + FF, D), (0.000111 / PARAMS ** 0.5), 9.5367431640625e-07, ((0, 4), (1, 8)), jnp.float32)
    readout_moment = scatter_about(seeds[16], (D, OUT + 2), (0.000111 / PARAMS ** 0.5), 9.5367431640625e-07, ((0, 32),), jnp.float32)
    encoder_second = jnp.clip(jnp.exp(math.log(2.409034758582931e-15) - 2.7725887 * jax.random.uniform(seeds[17], (IN, D), jnp.float32) ** levels(seeds[17], (IN, D), ((0, 8), (1, 4)), -0.2, 0.2)), 1.5056467241143318e-16, 2.409034758582931e-15)
    up_second = jnp.clip(jnp.exp(math.log(2.409034758582931e-15) - 2.7725887 * jax.random.uniform(seeds[18], (D, 3 * D + FF), jnp.float32) ** levels(seeds[18], (D, 3 * D + FF), ((0, 8), (1, 4)), -0.2, 0.2)), 1.5056467241143318e-16, 2.409034758582931e-15)
    down_second = jnp.clip(jnp.exp(math.log(2.409034758582931e-15) - 2.7725887 * jax.random.uniform(seeds[19], (D + FF, D), jnp.float32) ** levels(seeds[19], (D + FF, D), ((0, 4), (1, 8)), -0.2, 0.2)), 1.5056467241143318e-16, 2.409034758582931e-15)
    readout_second = jnp.clip(jnp.exp(math.log(2.409034758582931e-15) - 2.7725887 * jax.random.uniform(seeds[20], (D, OUT + 2), jnp.float32) ** levels(seeds[20], (D, OUT + 2), ((0, 32),), -0.2, 0.2)), 1.5056467241143318e-16, 2.409034758582931e-15)
    encoder_average = scatter_about(seeds[21], (IN, D), IN ** -0.5, 0.375, ((0, 8), (1, 4)), jnp.float32)
    up_average = scatter_about(seeds[22], (D, 3 * D + FF), D ** -0.5, 0.25, ((0, 8), (1, 4)), jnp.float32)
    down_average = scatter_about(seeds[23], (D + FF, D), D ** -0.5, 0.25, ((0, 4), (1, 8)), jnp.float32)
    readout_average = draw_readout_average(jax.random.fold_in(seeds[25], 71), 0)
    return {"cond_fields": cond_fields, "target": target, "noise_draw": noise_draw, "noise_sigma": noise_sigma, "grid_to_mesh": grid_to_mesh, "mesh_edges": mesh_edges, "mesh_to_grid": mesh_to_grid, "latitude_row": latitude_row, "level_index": level_index, "encoder": encoder, "up_proj": up_proj, "down_proj": down_proj, "readout": readout, "encoder_moment": encoder_moment, "up_moment": up_moment, "down_moment": down_moment, "readout_moment": readout_moment, "encoder_second": encoder_second, "up_second": up_second, "down_second": down_second, "readout_second": readout_second, "encoder_average": encoder_average, "up_average": up_average, "down_average": down_average, "readout_average": readout_average}


HIGH = lax.Precision.HIGHEST
clip_norm = 0.001
beta_one = 0.9
beta_two = 0.999
epsilon = 1e-08
learn_rate = 0.04
weight_decay = 0.1
average_decay = 0.9

@jax.custom_vjp
def low(v):
    return lax.optimization_barrier(v.astype(jnp.bfloat16)).astype(jnp.float32)

@jax.custom_vjp
def low_back(v):
    return v

def low_keep(v):
    return (low(v), None)

def low_pass(kept, grad):
    return (grad,)

def back_keep(v):
    return (v, None)

def back_low(kept, grad):
    return (low(grad),)
low.defvjp(low_keep, low_pass)
low_back.defvjp(back_keep, back_low)

def rounded(value):
    return low_back(low(value))

def matmul(left, right):
    return jnp.dot(left, right, precision=HIGH)

def norm_rows(values, gain):
    center = values - lax.optimization_barrier(jnp.mean(values, axis=-1, keepdims=True))
    inverse = lax.rsqrt(lax.optimization_barrier(jnp.mean(center * center, axis=-1, keepdims=True)) + 1e-05)
    return center * inverse * gain

def attention(query, keys, values, edges):
    valid = edges >= 0
    safe = jnp.where(valid, edges, 0)

    def block(pieces):
        part_query, part_edges, part_valid = pieces
        count = part_query.shape[0]
        near_keys = keys[part_edges].reshape(count, KM, HEADS, HEAD_DIM)
        near_values = values[part_edges].reshape(count, KM, HEADS, HEAD_DIM)
        scores = jnp.einsum('nhd,nkhd->nhk', part_query.reshape(count, HEADS, HEAD_DIM), near_keys, precision=HIGH)
        scores = scores * HEAD_DIM ** (-0.5)
        scores = jnp.where(part_valid[:, None, :], scores, -1e+30)
        top = lax.optimization_barrier(jnp.max(scores, axis=-1, keepdims=True))
        expo = jnp.exp(scores - top)
        probs = expo / lax.optimization_barrier(jnp.sum(expo, axis=-1, keepdims=True))
        return jnp.einsum('nhk,nkhd->nhd', probs, near_values, precision=HIGH).reshape(count, D)
    blocks = (query.reshape(N_WIDE, NODE_DEV, D), safe.reshape(N_WIDE, NODE_DEV, KM), valid.reshape(N_WIDE, NODE_DEV, KM))
    return lax.map(jax.checkpoint(block), blocks).reshape(NODES, D)

def globe_sum(weights, cond, target, noise, sigma, grid_to_mesh, mesh_edges, mesh_to_grid, pix_weight):
    enc_low = low(weights[0])
    up_low = low(weights[1])
    down_low = low(weights[2])
    read_low = low(weights[3])
    grouped = up_low.reshape(D, N_NARROW, 3 * FEAT + HID)
    w_query = grouped[:, :, :FEAT].reshape(D, D)
    w_keys = grouped[:, :, FEAT:2 * FEAT].reshape(D, D)
    w_values = grouped[:, :, 2 * FEAT:3 * FEAT].reshape(D, D)
    w_hidden = grouped[:, :, 3 * FEAT:].reshape(D, FF)
    rows_grouped = down_low.reshape(N_NARROW, FEAT + HID, D)
    w_output = rows_grouped[:, :FEAT].reshape(D, D)
    w_down = rows_grouped[:, FEAT:].reshape(FF, D)
    w_dec = read_low[:, :OUT]
    gain_att = read_low[:, OUT]
    gain_mlp = read_low[:, OUT + 1]
    square = sigma * sigma
    c_in = lax.rsqrt(square + 1.0)
    c_skip = 1.0 / (square + 1.0)
    c_out = sigma * c_in
    noisy = target + sigma * noise
    grid = low(jnp.concatenate([cond, c_in * noisy], axis=1))
    embed = low_back(matmul(grid, enc_low))
    state = embed[grid_to_mesh[:, 0]]
    for slot in range(1, KG):
        state = state + embed[grid_to_mesh[:, slot]]
    state = state / KG
    normed = low(norm_rows(low(state), gain_att))
    query = rounded(matmul(normed, w_query))
    keys = rounded(matmul(normed, w_keys))
    values = rounded(matmul(normed, w_values))
    mixed = low(attention(query, keys, values, mesh_edges))
    state = state + low_back(matmul(mixed, w_output))
    normed = low(norm_rows(low(state), gain_mlp))
    pre = low_back(matmul(normed, w_hidden))
    act = low(jax.nn.silu(pre))
    state = state + low_back(matmul(act, w_down))
    pooled = state[mesh_to_grid[:, 0]]
    for slot in range(1, KD):
        pooled = pooled + state[mesh_to_grid[:, slot]]
    pooled = low(pooled / KD)
    pred = low_back(matmul(pooled, w_dec))
    error = c_skip * noisy + c_out * pred - target
    return jnp.sum((square + 1.0) / square * pix_weight * error * error)

def reference(cond_fields, target, noise_draw, noise_sigma, grid_to_mesh, mesh_edges, mesh_to_grid, latitude_row, level_index, encoder, up_proj, down_proj, readout, encoder_moment, up_moment, down_moment, readout_moment, encoder_second, up_second, down_second, readout_second, encoder_average, up_average, down_average, readout_average):
    lat_weight = jnp.cos((latitude_row.astype(jnp.float32) - 90.0) * (math.pi / 180.0))
    level_weight = (level_index.astype(jnp.float32) + 1.0) / LEVELS
    pix_weight = lat_weight[:, None] * level_weight[None, :]
    total = MB * jnp.sum(pix_weight)

    def full_sum(params):
        result = jnp.zeros((), jnp.float32)
        for globe in range(MB):
            result = result + jax.checkpoint(globe_sum)(params, cond_fields[globe].astype(jnp.float32), target[globe], noise_draw[globe], noise_sigma[globe], grid_to_mesh, mesh_edges, mesh_to_grid, pix_weight)
        return result
    raw, pull = jax.vjp(full_sum, (encoder, up_proj, down_proj, readout))
    grads = pull(jnp.ones((), jnp.float32))[0]
    scaled = [grad / total for grad in grads]
    norm_value = jnp.sqrt(sum((jnp.sum(grad * grad) for grad in scaled)))
    factor = jnp.minimum(1.0, clip_norm / norm_value)
    step = jnp.asarray(STEPS_DONE, jnp.float32)
    fix_one = 1.0 - jnp.power(beta_one, step)
    fix_two = 1.0 - jnp.power(beta_two, step)
    outputs = [raw / total, norm_value]
    states = [(encoder, encoder_moment, encoder_second, encoder_average), (up_proj, up_moment, up_second, up_average), (down_proj, down_moment, down_second, down_average), (readout, readout_moment, readout_second, readout_average)]
    for grad, (weight, moment, second, average) in zip(scaled, states):
        clipped = grad * factor
        moment_new = beta_one * moment + (1.0 - beta_one) * clipped
        second_new = beta_two * second + (1.0 - beta_two) * clipped * clipped
        weight_new = weight - learn_rate * (moment_new / fix_one / (jnp.sqrt(second_new / fix_two) + epsilon) + weight_decay * weight)
        average_new = average_decay * average + (1.0 - average_decay) * weight_new
        outputs.extend([moment_new, second_new, weight_new, average_new, weight_new.astype(jnp.bfloat16)])
    return tuple(outputs)
```

```python
import functools
import math

import jax
import jax.numpy as jnp
from jax import lax
from jax.experimental import pallas as pl
from jax.experimental.pallas import tpu as pltpu
from jax.sharding import PartitionSpec as P

D = 512
HEADS = 4
HEAD_DIM = 128
OUT = 84
IN = 256
LEVELS = 13
KM = 16
KG = 8
KD = 3
STEPS_DONE = 7
MB = 4
GROUPS = 4
HID = 512
ROWS = 8
LINES = 64
EARLY = 512
LATE = 1152
BAND = 256
WINDOW = 1280
NEAR = 1536

clip_norm = 0.001
beta_one = 0.9
beta_two = 0.999
epsilon = 1e-08
learn_rate = 0.04
weight_decay = 0.1
average_decay = 0.9

BF = jnp.bfloat16
F32 = jnp.float32
BIG = 60 * 1024 * 1024


def mm(left, right):
    return jnp.dot(left, right, preferred_element_type=F32)


def mm_nt(left, right):
    return lax.dot_general(left, right, (((1,), (1,)), ((), ())), preferred_element_type=F32)


def mm_tn(left, right):
    return lax.dot_general(left, right, (((0,), (0,)), ((), ())), preferred_element_type=F32)


def split_two(value):
    high = value.astype(BF)
    return high, (value - high.astype(F32)).astype(BF)


def norm_parts(rows_low):
    values = rows_low.astype(F32)
    center = values - jnp.mean(values, axis=-1, keepdims=True)
    inverse = lax.rsqrt(jnp.mean(center * center, axis=-1, keepdims=True) + 1e-05)
    return center * inverse, inverse


def norm_pull(grad_out, normal, inverse, gain):
    scaled = grad_out * gain
    inner = (
        scaled
        - jnp.mean(scaled, axis=-1, keepdims=True)
        - normal * jnp.mean(scaled * normal, axis=-1, keepdims=True)
    )
    return inner * inverse, jnp.sum(grad_out * normal, axis=0, keepdims=True)


def prepare_kernel(grid_ref, pixels_ref, slots_ref, up_ref, across_ref, sums_ref, bias_ref, pool_ref, pull_ref, count_ref):
    nodes = sums_ref.shape[0]
    width = grid_ref.shape[0]
    step = 32

    def count_pixels(i, _):
        at = pl.multiple_of(i * step, step)
        picks = pixels_ref[pl.ds(at, step), :]
        lanes = lax.broadcasted_iota(jnp.int32, (step, width), 1)
        total = jnp.zeros((step, width), jnp.int32)
        for k in range(KG):
            total = total + (picks[:, k : k + 1] == lanes).astype(jnp.int32)
        count_ref[pl.ds(at, step), :] = total.astype(F32).astype(BF)
        return 0

    lax.fori_loop(0, nodes // step, count_pixels, 0)
    sums_ref[...] = mm(count_ref[...], grid_ref[...])

    def count_slots(i, _):
        at = pl.multiple_of(i * step, step)
        band = (i * step) // BAND
        picks = slots_ref[pl.ds(at, step), :] - band * BAND
        lanes = lax.broadcasted_iota(jnp.int32, (step, WINDOW), 1)
        total = jnp.zeros((step, WINDOW), jnp.int32)
        for k in range(KM):
            total = total + (picks[:, k : k + 1] == lanes).astype(jnp.int32)
        bias_ref[pl.ds(at, step), :] = jnp.where(
            total > 0, jnp.log2(total.astype(F32)), -1e30
        )
        return 0

    lax.fori_loop(0, nodes // step, count_slots, 0)

    def count_up(i, _):
        at = pl.multiple_of(i * step, step)
        picks = up_ref[pl.ds(at, step), :]
        lanes = lax.broadcasted_iota(jnp.int32, (step, nodes), 1)
        total = jnp.zeros((step, nodes), jnp.int32)
        for k in range(KD):
            total = total + (picks[:, k : k + 1] == lanes).astype(jnp.int32)
        pool_ref[pl.ds(at, step), :] = total.astype(F32).astype(BF)
        return 0

    lax.fori_loop(0, width // step, count_up, 0)

    def count_across(i, _):
        at = pl.multiple_of(i * step, step)
        rows = lax.broadcasted_iota(jnp.int32, (step, width), 0) + at
        total = jnp.zeros((step, width), jnp.int32)
        for k in range(KD):
            total = total + (across_ref[k : k + 1, :] == rows).astype(jnp.int32)
        pull_ref[pl.ds(at, step), :] = total.astype(F32).astype(BF)
        return 0

    lax.fori_loop(0, nodes // step, count_across, 0)


def prepare(grid, pixel_rows, slot_rows, up_rows, across_rows):
    nodes, width = slot_rows.shape[0], grid.shape[0]
    return pl.pallas_call(
        prepare_kernel,
        out_shape=(
            jax.ShapeDtypeStruct((nodes, IN), F32),
            jax.ShapeDtypeStruct((nodes, WINDOW), F32),
            jax.ShapeDtypeStruct((width, nodes), BF),
            jax.ShapeDtypeStruct((nodes, width), BF),
        ),
        scratch_shapes=[pltpu.VMEM((nodes, width), BF)],
        compiler_params=pltpu.CompilerParams(vmem_limit_bytes=32 * 1024 * 1024),
        cost_estimate=pl.CostEstimate(flops=400_000_000, bytes_accessed=6_000_000, transcendentals=700_000),
        name="prepare",
    )(grid, pixel_rows, slot_rows, up_rows, across_rows)


def copies_of(pairs, sems):
    return [pltpu.make_async_copy(source, target, sems.at[i]) for i, (source, target) in enumerate(pairs)]


def early_weights(early_ref, enc, wq, wkv, dec):
    pairs = []
    for n in range(GROUPS):
        if enc is not None:
            pairs.append((early_ref.at[:, n, 0:32, 384:512], enc.at[:, :, n * 128 : n * 128 + 128]))
        pairs.append((early_ref.at[:, n, :, 0:128], wq.at[:, :, n * 128 : n * 128 + 128]))
        pairs.append((early_ref.at[:, n, :, 128:256], wkv.at[:, :, n * 128 : n * 128 + 128]))
        pairs.append((early_ref.at[:, n, :, 256:384], wkv.at[:, :, 512 + n * 128 : 640 + n * 128]))
        pairs.append((early_ref.at[:, n, 32:48, 384:512], dec.at[n]))
    return pairs


def attend_kernel(
    early_ref, sums_ref, bias_ref,
    state_ref, rows_ref, normed_ref, query_ref, pair_ref, mixed_ref, probs_ref,
    enc, wq, wkv, dec, sems,
):
    copies = copies_of(early_weights(early_ref, enc, wq, wkv, dec), sems)
    for copy in copies:
        copy.start()
    for copy in copies:
        copy.wait()
    gain = dec[...].reshape(D, 128).astype(F32).T[OUT : OUT + 1, :]
    enc_full = enc[...].reshape(IN, D)
    pair_full = wkv[...].reshape(D, 2 * D)
    step = 256

    def encode(i, _):
        at = pl.multiple_of(i * step, step)
        high, low = split_two(sums_ref[pl.ds(at, step), :])
        state = (mm(high, enc_full) + mm(low, enc_full)) * (1.0 / KG)
        rows = state.astype(BF)
        rows_ref[pl.ds(at, step), :] = rows
        normal, _inverse = norm_parts(rows)
        normed = (normal * gain).astype(BF)
        normed_ref[pl.ds(at, step), :] = normed
        pair_ref[pl.ds(at, step), :] = mm(normed, pair_full).astype(BF)

        @pl.when((i >= 2) & (i < 4))
        def _():
            state_ref[pl.ds(pl.multiple_of(at - 512, step), step), :] = state

        return 0

    lax.fori_loop(0, NEAR // step, encode, 0)
    query_ref[...] = mm(normed_ref[512:1024, :], wq[...].reshape(D, D)).astype(BF)
    factor = HEAD_DIM ** (-0.5) * math.log2(math.e)

    def head(h, _):
        lane = pl.multiple_of(h * HEAD_DIM, HEAD_DIM)
        for band in range(2):
            at = band * BAND
            query = query_ref[at : at + BAND, pl.ds(lane, HEAD_DIM)]
            keys = pair_ref[at : at + WINDOW, pl.ds(lane, HEAD_DIM)]
            values = pair_ref[at : at + WINDOW, pl.ds(lane + D, HEAD_DIM)]
            scores = mm_nt(query, keys) * factor + bias_ref[at : at + BAND, :]
            top = jnp.max(scores, axis=-1, keepdims=True)
            expo = jnp.exp2(scores - top)
            inverse = 1.0 / jnp.sum(expo, axis=-1, keepdims=True)
            mixed_ref[at : at + BAND, pl.ds(lane, HEAD_DIM)] = (
                mm(expo.astype(BF), values) * inverse
            ).astype(BF)
            probs_ref[h, at : at + BAND, :] = (expo * inverse).astype(BF)
        return 0

    lax.fori_loop(0, HEADS, head, 0)


def attend(early, sums, bias):
    nodes = bias.shape[0]
    return pl.pallas_call(
        attend_kernel,
        in_specs=[
            pl.BlockSpec(memory_space=pl.ANY),
            pl.BlockSpec(memory_space=pltpu.VMEM),
            pl.BlockSpec(memory_space=pltpu.VMEM),
        ],
        out_shape=(
            jax.ShapeDtypeStruct((nodes, D), F32),
            jax.ShapeDtypeStruct((NEAR, D), BF),
            jax.ShapeDtypeStruct((NEAR, D), BF),
            jax.ShapeDtypeStruct((nodes, D), BF),
            jax.ShapeDtypeStruct((NEAR, 2 * D), BF),
            jax.ShapeDtypeStruct((nodes, D), BF),
            jax.ShapeDtypeStruct((HEADS, nodes, WINDOW), BF),
        ),
        scratch_shapes=[
            pltpu.VMEM((8, 32, D), BF),
            pltpu.VMEM((8, 64, D), BF),
            pltpu.VMEM((8, 64, 2 * D), BF),
            pltpu.VMEM((GROUPS, 8, 16, 128), BF),
            pltpu.SemaphoreType.DMA((20,)),
        ],
        compiler_params=pltpu.CompilerParams(vmem_limit_bytes=BIG),
        cost_estimate=pl.CostEstimate(flops=5_000_000_000, bytes_accessed=18_000_000, transcendentals=3_000_000),
        name="attend",
    )(early, sums, bias)


def feed_kernel(
    place_ref, scalars_ref, late_ref, early_ref, state_ref, mixed_ref, pool_ref, pull_ref, noisy_ref, target_ref, lat_ref, level_ref,
    keep_ref, send_ref, grad_state_ref, grad_mixed_ref, grad_dec_ref, loss_ref,
    w_hid, w_out, w_down, dec, pre_ref, act_ref, grad_pred_ref, sems,
):
    pairs = []
    for n in range(GROUPS):
        pairs.append((late_ref.at[:, n, :, 512:640], w_out.at[:, :, n * 128 : n * 128 + 128]))
        pairs.append((early_ref.at[:, n, 32:48, 384:512], dec.at[n]))
        pairs.append((late_ref.at[:, n, :, 0:512], w_hid.at[:, :, n * HID : (n + 1) * HID]))
        pairs.append((late_ref.at[:, n, :, 640:1152], w_down.at[:, :, n * HID : (n + 1) * HID]))
    copies = copies_of(pairs, sems)
    for copy in copies:
        copy.start()
    for copy in copies:
        copy.wait()
    dec_full = dec[...].reshape(D, 128)
    gain = dec_full.astype(F32).T[OUT + 1 : OUT + 2, :]
    out_full = w_out[...].reshape(D, D)
    mixed = mixed_ref[...]
    state1 = state_ref[...] + mm_nt(mixed, out_full)
    normal, inverse = norm_parts(state1.astype(BF))
    normed = (normal * gain).astype(BF)

    def forward(n, state):
        lane = pl.multiple_of(n * HID, HID)
        pre = mm(normed, w_hid[:, :, pl.ds(lane, HID)].reshape(D, HID))
        pre_ref[n] = pre
        act = (pre / (1.0 + jnp.exp(-pre))).astype(BF)
        act_ref[n] = act
        return state + mm_nt(act, w_down[:, :, pl.ds(lane, HID)].reshape(D, HID))

    state2 = lax.fori_loop(0, GROUPS, forward, state1)
    high, low = split_two(state2)
    pool = pool_ref[...]
    pooled = ((mm(pool, high) + mm(pool, low)) / KD).astype(BF)
    pixels = noisy_ref.shape[0]
    pred = mm(pooled, dec_full)[:pixels, :OUT]
    c_skip, c_out, lam = scalars_ref[0], scalars_ref[1], scalars_ref[2]
    error = c_skip * noisy_ref[...] + c_out * pred - target_ref[...]
    weighted = lam * (lat_ref[...] * level_ref[...])
    loss_ref[...] = jnp.broadcast_to(jnp.sum(weighted * error * error), loss_ref.shape)
    grad_pred_ref[...] = jnp.zeros_like(grad_pred_ref)
    grad_pred_ref[:pixels, :OUT] = 2.0 * c_out * weighted * error
    grad_pred = grad_pred_ref[...].astype(BF)
    grad_dec_ref[...] = mm_tn(grad_pred, pooled)
    up_high, up_low = split_two(mm(pull_ref[...], grad_pred))
    lanes = lax.broadcasted_iota(jnp.int32, (1, 128), 1)
    dec_only = jnp.where(lanes < OUT, dec_full.astype(F32), 0.0).astype(BF)
    grad_state2 = (mm_nt(up_high, dec_only) + mm_nt(up_low, dec_only)) / KD
    grad_low = grad_state2.astype(BF)

    own_wide, own_narrow = place_ref[0], place_ref[1]

    def put(out_ref, side, part, first, value):
        done = 0
        while done < value.shape[1]:
            colour, column = divmod(first + done, 384)
            count = min(384 - column, value.shape[1] - done)
            for w in range(8):
                out_ref[colour, part, w ^ own_wide, :, column : column + count] = value[
                    w * LINES : (w + 1) * LINES, done : done + count
                ]
            done += count

    def backward(part, grad_n, out_ref, side):
        n = (part * 2 + side) ^ own_narrow
        lane = pl.multiple_of(n * HID, HID)
        act = act_ref[n]
        pre = pre_ref[n]
        put(out_ref, side, part, 640, mm_tn(grad_low, act).astype(BF))
        grad_act = mm(grad_low, w_down[:, :, pl.ds(lane, HID)].reshape(D, HID))
        logistic = 1.0 / (1.0 + jnp.exp(-pre))
        grad_pre = (grad_act * logistic * (1.0 + pre * (1.0 - logistic))).astype(BF)
        put(out_ref, side, part, 0, mm_tn(normed, grad_pre).astype(BF))
        return grad_n + mm_nt(grad_pre, w_hid[:, :, pl.ds(lane, HID)].reshape(D, HID))

    grad_n = jnp.zeros((D, D), F32)
    for side, out_ref in ((1, send_ref), (0, keep_ref)):
        grad_n = lax.fori_loop(0, 2, functools.partial(backward, out_ref=out_ref, side=side), grad_n)
    back, gain_grad = norm_pull(grad_n, normal, inverse, gain)
    grad_dec_ref[OUT + 1 : OUT + 2, :] = gain_grad
    grad_state1 = grad_state2 + back
    grad_state_ref[...] = grad_state1
    grad_low1 = grad_state1.astype(BF)
    act_ref[0] = mixed
    for side, out_ref in ((1, send_ref), (0, keep_ref)):
        for part in range(2):
            lane = pl.multiple_of(((part * 2 + side) ^ own_narrow) * 128, 128)
            put(out_ref, side, part, 512, mm_tn(grad_low1, act_ref[0, :, pl.ds(lane, 128)]).astype(BF))
    grad_mixed_ref[...] = mm(grad_low1, out_full)


def feed(place, scalars, late, early, state0, mixed, pool, pull, noisy, target, lat, level):
    nodes = state0.shape[0]
    width = pool.shape[0]
    vmem = pl.BlockSpec(memory_space=pltpu.VMEM)
    anywhere = pl.BlockSpec(memory_space=pl.ANY)
    return pl.pallas_call(
        feed_kernel,
        in_specs=[pl.BlockSpec(memory_space=pltpu.SMEM)] * 2 + [anywhere, anywhere] + [vmem] * 8,
        out_shape=(
            jax.ShapeDtypeStruct((3, 2, 8, LINES, 384), BF),
            jax.ShapeDtypeStruct((3, 2, 8, LINES, 384), BF),
            jax.ShapeDtypeStruct((nodes, D), F32),
            jax.ShapeDtypeStruct((nodes, D), F32),
            jax.ShapeDtypeStruct((128, D), F32),
            jax.ShapeDtypeStruct((8, 128), F32),
        ),
        scratch_shapes=[
            pltpu.VMEM((8, LINES, GROUPS * HID), BF),
            pltpu.VMEM((8, LINES, D), BF),
            pltpu.VMEM((8, LINES, GROUPS * HID), BF),
            pltpu.VMEM((GROUPS, 8, 16, 128), BF),
            pltpu.VMEM((GROUPS, nodes, HID), F32),
            pltpu.VMEM((GROUPS, nodes, HID), BF),
            pltpu.VMEM((width, 128), F32),
            pltpu.SemaphoreType.DMA((16,)),
        ],
        compiler_params=pltpu.CompilerParams(vmem_limit_bytes=BIG),
        cost_estimate=pl.CostEstimate(flops=9_000_000_000, bytes_accessed=20_000_000, transcendentals=3_000_000),
        name="feed",
    )(place, scalars, late, early, state0, mixed, pool, pull, noisy, target, lat, level)


def return_kernel(
    place_ref, early_ref, probs_ref, query_ref, pair_ref, grad_mixed_ref, grad_state_ref, rows_ref, normed_ref, sums_ref, grad_dec_ref,
    keep_ref, send_ref,
    wq, wkv, dec, grad_query, grad_pair, turned, turn_query, turn_mixed, grad_weight, sems,
):
    copies = copies_of(early_weights(early_ref, None, wq, wkv, dec), sems)
    for copy in copies:
        copy.start()
    scale = HEAD_DIM ** (-0.5)
    turned[...] = jnp.zeros_like(turned)
    turn_query[...] = query_ref[...].astype(F32).T.astype(BF)
    turn_mixed[...] = grad_mixed_ref[...].T.astype(BF)

    def head(h, _):
        lane = pl.multiple_of(h * HEAD_DIM, HEAD_DIM)
        for band in range(2):
            at = band * BAND
            grad_low = grad_mixed_ref[at : at + BAND, pl.ds(lane, HEAD_DIM)].astype(BF)
            keys = pair_ref[at : at + WINDOW, pl.ds(lane, HEAD_DIM)]
            values = pair_ref[at : at + WINDOW, pl.ds(lane + D, HEAD_DIM)]
            probs_low = probs_ref[h, at : at + BAND, :]
            probs = probs_low.astype(F32)
            grad_probs = mm_nt(grad_low, values)
            part = probs * grad_probs
            inner = jnp.sum(part, axis=-1, keepdims=True)
            grad_scores = ((part - probs * inner) * scale).astype(BF)
            grad_query[at : at + BAND, pl.ds(lane, HEAD_DIM)] = mm(grad_scores, keys).astype(BF)
            turned[pl.ds(lane, HEAD_DIM), at : at + WINDOW] += mm(
                turn_query[pl.ds(lane, HEAD_DIM), at : at + BAND], grad_scores
            )
            turned[pl.ds(lane + D, HEAD_DIM), at : at + WINDOW] += mm(
                turn_mixed[pl.ds(lane, HEAD_DIM), at : at + BAND], probs_low
            )
        return 0

    lax.fori_loop(0, HEADS, head, 0)

    def turn(h, _):
        lane = pl.multiple_of(h * HEAD_DIM, HEAD_DIM)
        grad_pair[:, pl.ds(lane, HEAD_DIM)] = turned[pl.ds(lane, HEAD_DIM), :].T.astype(BF)
        return 0

    lax.fori_loop(0, 2 * HEADS, turn, 0)
    for copy in copies:
        copy.wait()
    gain = dec[...].reshape(D, 128).astype(F32).T[OUT : OUT + 1, :]
    grad_query_w = mm_tn(normed_ref[512:1024, :], grad_query[...]).astype(BF)
    grad_pair_w = mm_tn(normed_ref[...], grad_pair[...]).astype(BF)
    own_wide, own_narrow = place_ref[0], place_ref[1]
    grad_weight[:, :D] = grad_query_w
    grad_weight[:, D:] = grad_pair_w
    for side, out_ref in ((1, send_ref), (0, keep_ref)):
        for part in range(2):
            n = (part * 2 + side) ^ own_narrow
            for kind in range(3):
                lane = pl.multiple_of(n * 128 + kind * D, 128)
                value = grad_weight[:, pl.ds(lane, 128)]
                for w in range(8):
                    out_ref[part, w ^ own_wide, :, kind * 128 : kind * 128 + 128] = value[w * LINES : (w + 1) * LINES, :]
    grad_enc = jnp.zeros((IN, D), F32)
    gain_grad = jnp.zeros((1, D), F32)
    for block in range(3):
        at = block * 512
        grad_n = mm_nt(grad_pair[at : at + 512, :], wkv[...].reshape(D, 2 * D))
        if block == 1:
            grad_n = grad_n + mm_nt(grad_query[...], wq[...].reshape(D, D))
        normal, inverse = norm_parts(rows_ref[at : at + 512, :])
        back, gain_part = norm_pull(grad_n, normal, inverse, gain)
        gain_grad = gain_grad + gain_part
        if block == 1:
            back = back + grad_state_ref[...]
        back_low = (back * (1.0 / KG)).astype(BF)
        high, low = split_two(sums_ref[at : at + 512, :])
        grad_enc = grad_enc + mm_tn(high, back_low) + mm_tn(low, back_low)
    grad_enc = grad_enc.astype(BF)
    rows = lax.broadcasted_iota(jnp.int32, (128, 1), 0)
    grad_dec = jnp.where(rows == OUT, gain_grad, grad_dec_ref[...]).T.astype(BF)
    grad_weight[0:IN, :D] = grad_enc
    grad_weight[:, D : D + 128] = grad_dec
    for side, out_ref in ((1, send_ref), (0, keep_ref)):
        for part in range(2):
            n = (part * 2 + side) ^ own_narrow
            enc_part = grad_weight[0:IN, pl.ds(pl.multiple_of(n * 128, 128), 128)]
            dec_part = grad_weight[pl.ds(pl.multiple_of(n * 128, 128), 128), D : D + 128]
            for w in range(8):
                out_ref[part, w ^ own_wide, :, 384:512] = jnp.concatenate(
                    [enc_part[w * 32 : w * 32 + 32, :], dec_part[w * 16 : w * 16 + 16, :], jnp.zeros((16, 128), BF)], axis=0
                )


def give_back(place, early, probs, query, pair, grad_mixed, grad_state, rows, normed, sums, grad_dec):
    nodes = query.shape[0]
    vmem = pl.BlockSpec(memory_space=pltpu.VMEM)
    return pl.pallas_call(
        return_kernel,
        in_specs=[pl.BlockSpec(memory_space=pltpu.SMEM), pl.BlockSpec(memory_space=pl.ANY)] + [vmem] * 9,
        out_shape=(
            jax.ShapeDtypeStruct((2, 8, LINES, EARLY), BF),
            jax.ShapeDtypeStruct((2, 8, LINES, EARLY), BF),
        ),
        scratch_shapes=[
            pltpu.VMEM((8, 64, D), BF),
            pltpu.VMEM((8, 64, 2 * D), BF),
            pltpu.VMEM((GROUPS, 8, 16, 128), BF),
            pltpu.VMEM((nodes, D), BF),
            pltpu.VMEM((NEAR, 2 * D), BF),
            pltpu.VMEM((2 * D, NEAR), F32),
            pltpu.VMEM((D, nodes), BF),
            pltpu.VMEM((D, nodes), BF),
            pltpu.VMEM((D, 3 * D), BF),
            pltpu.SemaphoreType.DMA((16,)),
        ],
        compiler_params=pltpu.CompilerParams(vmem_limit_bytes=BIG),
        cost_estimate=pl.CostEstimate(flops=9_000_000_000, bytes_accessed=20_000_000, transcendentals=0),
        name="give_back",
    )(place, early, probs, query, pair, grad_mixed, grad_state, rows, normed, sums, grad_dec)


def adam_update(grad_raw, factor, fix_one, fix_two, weight, moment, second, average):
    grad = grad_raw * factor
    moment_new = beta_one * moment + (1.0 - beta_one) * grad
    second_new = beta_two * second + (1.0 - beta_two) * grad * grad
    weight_new = weight - learn_rate * (
        moment_new / fix_one / (jnp.sqrt(second_new / fix_two) + epsilon) + weight_decay * weight
    )
    average_new = average_decay * average + (1.0 - average_decay) * weight_new
    return [moment_new, second_new, weight_new, average_new, weight_new.astype(BF)]


def pack(encoder, up_proj, down_proj, readout):
    lines = up_proj.shape[0]
    spare = lines - encoder.shape[0] - readout.shape[0]
    side = jnp.concatenate(
        [
            encoder.astype(BF),
            jnp.pad(readout.astype(BF), ((0, 0), (0, 128 - readout.shape[1]))),
            jnp.zeros((spare, 128), BF),
        ],
        axis=0,
    )
    up = up_proj.astype(BF)
    early = jnp.concatenate([up[:, :384], side], axis=1)
    late = jnp.concatenate([up[:, 384:], down_proj.T.astype(BF)], axis=1)
    return early, late


def to_lines(array, wide):
    if wide == 8:
        return array
    lines, width = array.shape[2:]
    return jnp.moveaxis(jnp.moveaxis(array, 1, 0).reshape(GROUPS, 8, LINES, width), 0, 1)


def side_to_lines(side, wide):
    if wide == 8:
        return side
    enc_rows, read_rows = IN // wide, D // (GROUPS * wide)
    enc = to_rows(side[:, :, :enc_rows], 32)
    read = to_rows(side[:, :, enc_rows : enc_rows + read_rows], 16)
    return jnp.concatenate([enc, read, jnp.zeros((8, GROUPS, 16, 128), side.dtype)], axis=2)


def to_rows(array, rows):
    return jnp.moveaxis(jnp.moveaxis(array, 1, 0).reshape(GROUPS, 8, rows, array.shape[3]), 0, 1)


def from_rows(array, wide):
    rows, width = array.shape[2:]
    return jnp.moveaxis(jnp.moveaxis(array, 1, 0).reshape(GROUPS, wide, 8 * rows // wide, width), 0, 1)


def early_from_lines(array, wide):
    if wide == 8:
        return array
    main = from_rows(array[..., :384], wide)
    enc = from_rows(array[:, :, :32, 384:], wide)
    read = from_rows(array[:, :, 32:48, 384:], wide)
    spare = main.shape[2] - enc.shape[2] - read.shape[2]
    side = jnp.concatenate([enc, read, jnp.zeros((wide, GROUPS, spare, 128), array.dtype)], axis=2)
    return jnp.concatenate([main, side], axis=3)


def gather_weights(early, late, wide):
    both = jnp.concatenate([early, late], axis=1)
    full = lax.all_gather(both, ("wide", "narrow"), axis=0, tiled=False)
    full = full.reshape(wide, GROUPS, *both.shape)
    early_full, late_full = full[..., :EARLY], full[..., EARLY:]
    if wide != 8:
        early_full = jnp.concatenate(
            [to_lines(early_full[..., :384], wide), side_to_lines(early_full[..., 384:], wide)], axis=3
        )
        late_full = to_lines(late_full, wide)
    return early_full, late_full


def swap(array, bit):
    count = lax.axis_size("wide") * lax.axis_size("narrow")
    return lax.ppermute(array, ("wide", "narrow"), [(i, i ^ (1 << bit)) for i in range(count)])


def halve(parts, axis, bit):
    sent = sum(lax.index_in_dim(part, 1, axis, keepdims=False).astype(F32) for part in parts).astype(BF)
    return [lax.index_in_dim(part, 0, axis, keepdims=False) for part in parts] + [swap(sent, bit)]


def reduce_parts(parts, order):
    axes = [1, 4, 3, 2]
    for bit in order:
        axis = axes.index(bit)
        parts = halve(parts, axis, bit)
        axes.pop(axis)
    return sum(part.astype(F32) for part in parts)


def cube(array):
    return array.reshape(2, 2, 2, 2, *array.shape[2:])


ORDERS = ((1, 2, 3, 4), (2, 3, 1, 4), (3, 1, 2, 4))


def reduce_late(keep, send):
    got = swap(send, 0)
    return jnp.concatenate(
        [reduce_parts([cube(keep[i]), cube(got[i])], order) for i, order in enumerate(ORDERS)], axis=1
    )


def reduce_early(keep, send):
    got = swap(send, 0)
    cuts = ((0, 128), (128, 256), (256, 512))
    return jnp.concatenate(
        [
            reduce_parts([cube(keep[..., low:high]), cube(got[..., low:high])], order)
            for (low, high), order in zip(cuts, ORDERS)
        ],
        axis=1,
    )


def in_order(keep, send):
    both = jnp.stack([keep, send], axis=2)
    return jnp.moveaxis(both.reshape(both.shape[0], 4, *both.shape[3:]), 1, 2)


def scatter_sum(blocks):
    return lax.psum_scatter(
        blocks.astype(F32).reshape(-1, blocks.shape[3]), ("wide", "narrow"), scatter_dimension=0, tiled=True
    )


def sum_all(values):
    count = lax.axis_size("wide") * lax.axis_size("narrow")
    row = jnp.pad(jnp.stack(values)[None, :], ((0, 7), (0, 128 - len(values))))
    bit = 0
    while 1 << bit < count:
        row = row + swap(row, bit)
        bit += 1
    return [row[0, i] for i in range(len(values))]


def body(
    cond_fields,
    target,
    noise_draw,
    noise_sigma,
    grid_to_mesh,
    mesh_edges,
    mesh_to_grid,
    latitude_row,
    level_index,
    encoder,
    up_proj,
    down_proj,
    readout,
    encoder_moment,
    up_moment,
    down_moment,
    readout_moment,
    encoder_second,
    up_second,
    down_second,
    readout_second,
    encoder_average,
    up_average,
    down_average,
    readout_average,
):
    wide_index = lax.axis_index("wide")
    wide = lax.axis_size("wide")
    globe = lax.axis_index("narrow")
    nodes = mesh_edges.shape[0]
    pixels = cond_fields.shape[1]
    all_nodes = nodes * wide
    width = -(-pixels // 128) * 128

    early, late = pack(encoder, up_proj, down_proj, readout)
    early_full, late_full = gather_weights(early, late, wide)

    sigma = lax.dynamic_index_in_dim(noise_sigma, globe, 0, keepdims=False)
    square = sigma * sigma
    c_in = lax.rsqrt(square + 1.0)
    c_skip = 1.0 / (square + 1.0)
    c_out = sigma * c_in
    lam = (square + 1.0) / square
    cond = lax.dynamic_index_in_dim(cond_fields, globe, 0, keepdims=False)
    goal = lax.dynamic_index_in_dim(target, globe, 0, keepdims=False)
    noisy = goal + sigma * lax.dynamic_index_in_dim(noise_draw, globe, 0, keepdims=False)
    grid = jnp.concatenate([cond, (c_in * noisy).astype(BF)], axis=1)
    grid = jnp.pad(grid, ((0, width - pixels), (0, 0)))
    pixel_rows = grid_to_mesh - wide_index * pixels
    slot_rows = jnp.where(
        mesh_edges >= 0, (mesh_edges - wide_index * nodes + nodes + all_nodes) % all_nodes, -1
    )
    up_rows = jnp.pad(mesh_to_grid - wide_index * nodes, ((0, width - pixels), (0, 0)), constant_values=-1)
    sums, bias, pool, pull = prepare(grid, pixel_rows, slot_rows, up_rows, up_rows.T)
    before = lax.ppermute(sums, "wide", [(i, (i + 1) % wide) for i in range(wide)])
    after = lax.ppermute(sums, "wide", [((i + 1) % wide, i) for i in range(wide)])
    near = jnp.concatenate([before, sums, after], axis=0)

    lat_weight = jnp.cos((latitude_row.astype(F32) - 90.0) * (math.pi / 180.0))
    level_weight = (level_index.astype(F32) + 1.0) / LEVELS
    pix_total = jnp.sum(lat_weight) * jnp.sum(level_weight)

    state0, rows, normed, query, pair, mixed, probs = attend(early_full, near, bias)
    place = jnp.stack([wide_index, globe]) if wide == 8 else jnp.zeros((2,), jnp.int32)
    keep_late, send_late, grad_state, grad_mixed, grad_dec, loss_part = feed(
        place, jnp.stack([c_skip, c_out, lam]),
        late_full, early_full, state0, mixed, pool, pull, noisy, goal, lat_weight[:, None], level_weight[None, :],
    )
    keep_early, send_early = give_back(
        place, early_full, probs, query, pair, grad_mixed, grad_state, rows, normed, near, grad_dec
    )
    if wide == 8:
        share_late = reduce_late(keep_late, send_late)
        share_early = reduce_early(keep_early, send_early)
    else:
        late_lines = jnp.concatenate(list(in_order(keep_late, send_late)), axis=3)
        early_lines = in_order(keep_early[None], send_early[None])[0]
        share_late = scatter_sum(from_rows(late_lines, wide))
        share_early = scatter_sum(early_from_lines(early_lines, wide))
    share = jnp.concatenate([share_early, share_late], axis=1)
    share_up = jnp.concatenate([share[:, :384], share[:, 512:1024]], axis=1)
    share_down = share[:, 1024:].T
    enc_rows, read_rows = encoder.shape[0], readout.shape[0]
    share_enc = share[:enc_rows, 384:512]
    share_read = share[enc_rows : enc_rows + read_rows, 384 : 384 + OUT + 2]
    first = (globe == 0).astype(F32)
    square_all, loss_all, pixel_all = sum_all([jnp.sum(share * share), loss_part[0, 0], pix_total * first])
    total = pixel_all * MB
    norm_value = jnp.sqrt(square_all) / total
    factor = jnp.minimum(1.0, clip_norm / norm_value) / total
    step = jnp.asarray(STEPS_DONE, F32)
    fix_one = 1.0 - jnp.power(beta_one, step)
    fix_two = 1.0 - jnp.power(beta_two, step)
    states = [
        (share_enc, encoder, encoder_moment, encoder_second, encoder_average),
        (share_up, up_proj, up_moment, up_second, up_average),
        (share_down, down_proj, down_moment, down_second, down_average),
        (share_read, readout, readout_moment, readout_second, readout_average),
    ]
    outputs = [loss_all / total, norm_value]
    for part, weight, moment, second, average in states:
        outputs.extend(adam_update(part, factor, fix_one, fix_two, weight, moment, second, average))
    return tuple(outputs)


def solution(mesh):
    if mesh.shape["narrow"] != GROUPS or MB != GROUPS:
        raise ValueError("narrow size")
    by_pixel = P(None, "wide", None)
    pair = P("wide", "narrow")
    weights = (pair, pair, P("narrow", "wide"), P(("narrow", "wide"), None))
    placed = (by_pixel, by_pixel, by_pixel, P()) + (P("wide", None),) * 3 + (P("wide"), P()) + weights * 4
    given = (P(), P())
    for spec in weights:
        given = given + (spec,) * 5
    return jax.shard_map(body, mesh=mesh, in_specs=placed, out_specs=given, check_vma=False)
```

```python
import functools
import math

import jax
import jax.numpy as jnp
from jax import lax
from jax.experimental import pallas as pl
from jax.experimental.pallas import tpu as pltpu
from jax.sharding import PartitionSpec as P

D = 512
HEADS = 4
HEAD_DIM = 128
OUT = 84
IN = 256
LEVELS = 13
KM = 16
KG = 8
KD = 3
STEPS_DONE = 7
MB = 4
GROUPS = 4
HID = 512
ROWS = 8
LINES = 64
EARLY = 512
LATE = 1152
BAND = 256
WINDOW = 1280
NEAR = 1536

clip_norm = 0.001
beta_one = 0.9
beta_two = 0.999
epsilon = 1e-08
learn_rate = 0.04
weight_decay = 0.1
average_decay = 0.9

BF = jnp.bfloat16
F32 = jnp.float32
MIB = 1024 * 1024
BIG = 60 * MIB


def mm(left, right):
    return jnp.dot(left, right, preferred_element_type=F32)


def mm_nt(left, right):
    return lax.dot_general(left, right, (((1,), (1,)), ((), ())), preferred_element_type=F32)


def mm_tn(left, right):
    return lax.dot_general(left, right, (((0,), (0,)), ((), ())), preferred_element_type=F32)


def split_two(value):
    high = value.astype(BF)
    return high, (value - high.astype(F32)).astype(BF)


def norm_parts(rows_low):
    values = rows_low.astype(F32)
    center = values - jnp.mean(values, axis=-1, keepdims=True)
    inverse = lax.rsqrt(jnp.mean(center * center, axis=-1, keepdims=True) + 1e-05)
    return center * inverse, inverse


def norm_pull(grad_out, normal, inverse, gain):
    scaled = grad_out * gain
    inner = (
        scaled
        - jnp.mean(scaled, axis=-1, keepdims=True)
        - normal * jnp.mean(scaled * normal, axis=-1, keepdims=True)
    )
    return inner * inverse, jnp.sum(grad_out * normal, axis=0, keepdims=True)


def sums_kernel(grid_ref, pixels_ref, sums_ref, count_ref):
    width, nodes = count_ref.shape
    step = 32
    picks = [jnp.broadcast_to(pixels_ref[k : k + 1, :], (step, nodes)) for k in range(KG)]
    rows = lax.broadcasted_iota(jnp.int32, (step, nodes), 0)

    def count(i, _):
        at = pl.multiple_of(i * step, step)
        total = jnp.zeros((step, nodes), F32)
        for pick in picks:
            total = total + jnp.where(pick - at == rows, 1.0, 0.0)
        count_ref[pl.ds(at, step), :] = total.astype(BF)
        return 0

    lax.fori_loop(0, width // step, count, 0)
    sums_ref[...] = mm(grid_ref[...], count_ref[...])


def grid_sums(grid, pixel_rows):
    nodes, width = pixel_rows.shape[1], grid.shape[1]
    return pl.pallas_call(
        sums_kernel,
        out_shape=jax.ShapeDtypeStruct((IN, nodes), F32),
        scratch_shapes=[pltpu.VMEM((width, nodes), BF)],
        compiler_params=pltpu.CompilerParams(vmem_limit_bytes=16 * 1024 * 1024),
        cost_estimate=pl.CostEstimate(flops=240_000_000, bytes_accessed=1_000_000, transcendentals=0),
        name="grid_sums",
    )(grid, pixel_rows)


def counts_kernel(slots_ref, across_ref, bias_ref, pool_ref, pull_ref):
    nodes, width = pull_ref.shape
    step = 64
    for band in range(nodes // BAND):
        low = band * BAND
        picks = slots_ref[:, low : low + BAND] - low
        rows = lax.broadcasted_iota(jnp.int32, (step, BAND), 0)

        def count_slots(i, _):
            at = pl.multiple_of(i * step, step)
            total = jnp.zeros((step, BAND), F32)
            for k in range(KM):
                total = total + jnp.where(picks[k : k + 1, :] - at == rows, 1.0, 0.0)
            bias_ref[band, pl.ds(at, step), :] = jnp.where(total > 0.0, jnp.log2(jnp.maximum(total, 1.0)), -1e30)
            return 0

        lax.fori_loop(0, WINDOW // step, count_slots, 0)

    def count_across(i, _):
        at = pl.multiple_of(i * 128, 128)
        rows = lax.broadcasted_iota(jnp.int32, (128, width), 0) + at
        total = jnp.zeros((128, width), F32)
        for k in range(KD):
            total = total + jnp.where(across_ref[k : k + 1, :] == rows, 1.0, 0.0)
        pull_ref[pl.ds(at, 128), :] = total.astype(BF)
        pool_ref[:, pl.ds(at, 128)] = total.T.astype(BF)
        return 0

    lax.fori_loop(0, nodes // 128, count_across, 0)


def counts(slot_rows, across_rows):
    nodes, width = slot_rows.shape[1], across_rows.shape[1]
    return pl.pallas_call(
        counts_kernel,
        out_shape=(
            jax.ShapeDtypeStruct((nodes // BAND, WINDOW, BAND), F32),
            jax.ShapeDtypeStruct((width, nodes), BF),
            jax.ShapeDtypeStruct((nodes, width), BF),
        ),
        compiler_params=pltpu.CompilerParams(vmem_limit_bytes=16 * 1024 * 1024),
        cost_estimate=pl.CostEstimate(flops=60_000_000, bytes_accessed=5_000_000, transcendentals=700_000),
        name="counts",
    )(slot_rows, across_rows)


def blocks_of(place_ref, dims, refs):
    own_wide, own_narrow = place_ref[0], place_ref[1]
    found = []
    for side in range(2):
        for j in range(16):
            bits = dict(zip(dims, ((j >> 3) & 1, (j >> 2) & 1, (j >> 1) & 1, j & 1)))
            wide = own_wide ^ (bits[4] * 4 + bits[3] * 2 + bits[2])
            narrow = own_narrow ^ (bits[1] * 2 + side)
            found.append((wide, narrow, refs[2 * side + (j >> 3)].at[j & 7]))
    return found


def fetch_early(place_ref, refs, early, sems):
    copies = []
    for colour in range(2):
        for wide, narrow, source in blocks_of(place_ref, DIMS[colour], refs[4 * colour : 4 * colour + 4]):
            copies.append(
                pltpu.make_async_copy(
                    source, early.at[wide, narrow, :, colour * 256 : colour * 256 + 256], sems.at[len(copies)]
                )
            )
    return copies


def enc_of(early):
    return jnp.concatenate([early[:, n, 0:32, 384:512].reshape(IN, 128) for n in range(GROUPS)], axis=1)


def dec_of(early):
    return jnp.concatenate([early[:, n, 32:48, 384:512].reshape(128, 128) for n in range(GROUPS)], axis=0)


def query_of(early):
    return jnp.concatenate([early[:, n, :, 0:128].reshape(D, 128) for n in range(GROUPS)], axis=1)


def pair_of(early):
    return jnp.concatenate([early[:, n, :, 128:384].reshape(D, 256) for n in range(GROUPS)], axis=1)


class Leaving:
    def __init__(self, sems):
        self.sems, self.copies = sems, []

    def __call__(self, source, there):
        self.copies.append(pltpu.make_async_copy(source, there, self.sems.at[len(self.copies)]))
        self.copies[-1].start()

    def wait(self):
        for copy in self.copies:
            copy.wait()


def encode_kernel(
    place_ref, a_0, a_1, a_2, a_3, b_0, b_1, b_2, b_3, before_ref, sums_ref, after_ref,
    state_ref, rows_ref, normed_ref, query_ref, pair_ref, early_ref,
    early, state, rows_all, normed_all, query_all, pair_all, sems, out_sems,
):
    copies = fetch_early(place_ref, (a_0, a_1, a_2, a_3, b_0, b_1, b_2, b_3), early, sems)
    for copy in copies:
        copy.start()
    for copy in copies:
        copy.wait()
    leave = Leaving(out_sems)
    leave(early, early_ref)
    gain = dec_of(early).astype(F32).T[OUT : OUT + 1, :]
    enc = enc_of(early)
    weights = pair_of(early)
    for block, ref in enumerate((before_ref, sums_ref, after_ref)):
        here = slice(block * 512, block * 512 + 512)
        if block == 1:
            high, low = split_two(ref[...])
            embedded = (mm_tn(high, enc) + mm_tn(low, enc)) * (1.0 / KG)
            state[...] = embedded
            leave(state, state_ref)
        else:
            embedded = mm_tn(ref[...], enc) * (1.0 / KG)
        rows = embedded.astype(BF)
        rows_all[here, :] = rows
        leave(rows_all.at[here], rows_ref.at[here])
        normal, _inverse = norm_parts(rows)
        normed = (normal * gain).astype(BF)
        normed_all[here, :] = normed
        leave(normed_all.at[here], normed_ref.at[here])
        if block == 1:
            query_all[...] = mm(normed, query_of(early)).astype(BF)
            leave(query_all, query_ref)
        pair_all[here, :] = mm(normed, weights).astype(BF)
        leave(pair_all.at[here], pair_ref.at[here])
    leave.wait()


def encode(place, gathered, before, sums, after):
    nodes = sums.shape[1]
    vmem = pl.BlockSpec(memory_space=pltpu.VMEM)
    outside = pl.BlockSpec(memory_space=pltpu.HBM)
    shapes = (
        jax.ShapeDtypeStruct((nodes, D), F32),
        jax.ShapeDtypeStruct((NEAR, D), BF),
        jax.ShapeDtypeStruct((NEAR, D), BF),
        jax.ShapeDtypeStruct((nodes, D), BF),
        jax.ShapeDtypeStruct((NEAR, 2 * D), BF),
        jax.ShapeDtypeStruct((8, GROUPS, LINES, EARLY), BF),
    )
    return pl.pallas_call(
        encode_kernel,
        in_specs=[pl.BlockSpec(memory_space=pltpu.SMEM)] + [outside] * 8 + [vmem] * 3,
        out_specs=[outside] * 6,
        out_shape=shapes,
        scratch_shapes=[pltpu.VMEM((8, GROUPS, LINES, EARLY), BF)]
        + [pltpu.VMEM(shape.shape, shape.dtype) for shape in shapes[:5]]
        + [pltpu.SemaphoreType.DMA((64,)), pltpu.SemaphoreType.DMA((12,))],
        compiler_params=pltpu.CompilerParams(vmem_limit_bytes=BIG),
        cost_estimate=pl.CostEstimate(flops=5_000_000_000, bytes_accessed=12_000_000, transcendentals=0),
        name="encode",
    )(place, *gathered, before, sums, after)


def attend_kernel(
    query_in, pair_in, bias_in, mixed_ref, probs_ref,
    query_all, pair_all, bias, mixed_all, probs, scores, value_turned, sems, out_sems,
):
    def pair_copy(h):
        return pltpu.make_async_copy(pair_in.at[:, pl.ds(pl.multiple_of(h * 256, 256), 256)], pair_all.at[h], sems.at[h])

    query_copy = pltpu.make_async_copy(query_in, query_all, sems.at[4])
    bias_copies = [pltpu.make_async_copy(bias_in.at[i], bias.at[i], sems.at[5 + i]) for i in range(2)]
    pair_copy(0).start()
    query_copy.start()
    bias_copies[0].start()
    bias_copies[1].start()
    for h in range(1, HEADS):
        pair_copy(h).start()
    query_copy.wait()
    bias_copies[0].wait()
    bias_copies[1].wait()
    factor = HEAD_DIM ** (-0.5) * math.log2(math.e)
    chunk = 128

    def head(h, _):
        lane = pl.multiple_of(h * HEAD_DIM, HEAD_DIM)
        pair_copy(h).wait()
        value_turned[...] = pair_all[h, :, HEAD_DIM:].astype(F32).T.astype(BF)
        for band in range(2):
            at = band * BAND
            query = query_all[at : at + BAND, pl.ds(lane, HEAD_DIM)]
            top = jnp.full((1, BAND), -3e38, F32)
            for i in range(WINDOW // chunk):
                row = i * chunk
                part = mm_nt(pair_all[h, at + row : at + row + chunk, :HEAD_DIM], query)
                part = part * factor + bias[band, row : row + chunk, :]
                scores[row : row + chunk, :] = part
                top = jnp.maximum(top, jnp.max(part, axis=0, keepdims=True))
            total = jnp.zeros((1, BAND), F32)
            mixed = jnp.zeros((HEAD_DIM, BAND), F32)
            for i in range(WINDOW // chunk):
                row = i * chunk
                expo = jnp.exp2(scores[row : row + chunk, :] - top)
                scores[row : row + chunk, :] = expo
                total = total + jnp.sum(expo, axis=0, keepdims=True)
                mixed = mixed + mm(value_turned[:, at + row : at + row + chunk], expo.astype(BF))
            inverse = 1.0 / total
            mixed_all[at : at + BAND, pl.ds(lane, HEAD_DIM)] = (mixed * inverse).T.astype(BF)
            for i in range(WINDOW // chunk):
                row = i * chunk
                probs[h, band, row : row + chunk, :] = (scores[row : row + chunk, :] * inverse).astype(BF)
            pltpu.make_async_copy(probs.at[h, band], probs_ref.at[h, band], out_sems.at[1 + 2 * h + band]).start()
        return 0

    lax.fori_loop(0, HEADS, head, 0)
    leave = pltpu.make_async_copy(mixed_all, mixed_ref, out_sems.at[0])
    leave.start()
    leave.wait()
    for h in range(HEADS):
        for band in range(2):
            pltpu.make_async_copy(probs.at[h, band], probs_ref.at[h, band], out_sems.at[1 + 2 * h + band]).wait()


def attend(query, pair, bias):
    nodes = query.shape[0]
    outside = pl.BlockSpec(memory_space=pltpu.HBM)
    return pl.pallas_call(
        attend_kernel,
        in_specs=[outside] * 3,
        out_specs=[outside] * 2,
        out_shape=(
            jax.ShapeDtypeStruct((nodes, D), BF),
            jax.ShapeDtypeStruct((HEADS, 2, WINDOW, BAND), BF),
        ),
        scratch_shapes=[
            pltpu.VMEM((nodes, D), BF),
            pltpu.VMEM((HEADS, NEAR, 2 * HEAD_DIM), BF),
            pltpu.VMEM((2, WINDOW, BAND), F32),
            pltpu.VMEM((nodes, D), BF),
            pltpu.VMEM((HEADS, 2, WINDOW, BAND), BF),
            pltpu.VMEM((WINDOW, BAND), F32),
            pltpu.VMEM((HEAD_DIM, NEAR), BF),
            pltpu.SemaphoreType.DMA((7,)),
            pltpu.SemaphoreType.DMA((9,)),
        ],
        compiler_params=pltpu.CompilerParams(vmem_limit_bytes=BIG),
        cost_estimate=pl.CostEstimate(flops=3_000_000_000, bytes_accessed=12_000_000, transcendentals=3_000_000),
        name="attend",
    )(query, pair, bias)


def feed_kernel(
    place_ref, scalars_ref, a_0, a_1, a_2, a_3, b_0, b_1, b_2, b_3, early_ref, state_in, mixed_in, pool_in, pull_in, noisy_ref, target_ref, lat_ref, level_ref,
    keep_out, send_out, grad_state_out, grad_mixed_out, grad_dec_ref, loss_ref,
    late, dec, pre_ref, act_ref, grad_pred_ref,
    state_ref, mixed_ref, pool_ref, pull_ref, keep_ref, send_ref, grad_state_ref, grad_mixed_ref, sems, group_sems, out_sems,
):
    own_wide, own_narrow = place_ref[0], place_ref[1]

    refs = (a_0, a_1, a_2, a_3), (b_0, b_1, b_2, b_3)

    def fetch(colour, columns, first, sem):
        there = slice(first, first + columns.stop - columns.start)
        return [
            pltpu.make_async_copy(source.at[:, columns], late.at[wide, narrow, :, there], sem(narrow, i))
            for i, (wide, narrow, source) in enumerate(blocks_of(place_ref, DIMS[colour], refs[colour]))
        ]

    def group(n, columns, row):
        return pltpu.make_async_copy(late.at[:, n, :, columns], late.at[:, n, :, columns], group_sems.at[row, n])

    hidden, outer, lower = slice(0, 512), slice(512, 640), slice(640, 1152)
    pairs = [(state_in, state_ref), (mixed_in, mixed_ref), (early_ref.at[:, :, 32:48, 384:512], dec)]
    small = [pltpu.make_async_copy(source, there, sems.at[32 + i]) for i, (source, there) in enumerate(pairs)]
    small += fetch(0, outer, 512, lambda n, i: sems.at[i])
    pool_copy = pltpu.make_async_copy(pool_in, pool_ref, sems.at[35])
    pull_copy = pltpu.make_async_copy(pull_in, pull_ref, sems.at[36])
    first = fetch(0, hidden, 0, lambda n, i: group_sems.at[0, n])
    second = fetch(1, slice(0, 512), 640, lambda n, i: group_sems.at[1, n])
    for copy in (*small, *first, *second, pool_copy, pull_copy):
        copy.start()
    for copy in small:
        copy.wait()
    dec_turned = jnp.concatenate([dec[:, n].reshape(128, 128) for n in range(GROUPS)], axis=0).astype(F32).T
    gain = dec_turned[OUT + 1 : OUT + 2, :]
    rows = lax.broadcasted_iota(jnp.int32, (128, 1), 0)
    dec_only = jnp.where(rows < OUT, dec_turned, 0.0).astype(BF)
    out_full = jnp.concatenate([late[:, n, :, 512:640].reshape(D, 128) for n in range(GROUPS)], axis=1)
    mixed = mixed_ref[...]
    state1 = state_ref[...] + mm_nt(mixed, out_full)
    normal, inverse = norm_parts(state1.astype(BF))
    normed = (normal * gain).astype(BF)

    def forward(i, state):
        n = i ^ own_narrow
        group(n, hidden, 0).wait()
        pre = mm(normed, late[:, n, :, 0:512].reshape(D, HID))
        pre_ref[n] = pre
        act = (pre / (1.0 + jnp.exp(-pre))).astype(BF)
        act_ref[n] = act
        group(n, lower, 1).wait()
        return state + mm_nt(act, late[:, n, :, 640:1152].reshape(D, HID))

    state2 = lax.fori_loop(0, GROUPS, forward, state1)
    high, low = split_two(state2)
    pool_copy.wait()
    pull_copy.wait()
    pool = pool_ref[...]
    pooled = ((mm(pool, high) + mm(pool, low)) / KD).astype(BF)
    pixels = noisy_ref.shape[1]
    pred = mm_nt(dec_only, pooled)[:OUT, :pixels]
    c_skip, c_out, lam = scalars_ref[0], scalars_ref[1], scalars_ref[2]
    error = c_skip * noisy_ref[...] + c_out * pred - target_ref[...]
    weighted = lam * (lat_ref[...] * level_ref[...])
    loss_ref[...] = jnp.broadcast_to(jnp.sum(weighted * error * error), loss_ref.shape)
    grad_pred_ref[...] = jnp.zeros_like(grad_pred_ref)
    grad_pred_ref[:OUT, :pixels] = 2.0 * c_out * weighted * error
    grad_pred = grad_pred_ref[...].astype(BF)
    grad_dec_ref[...] = mm(grad_pred, pooled)
    up_high, up_low = split_two(mm_nt(pull_ref[...], grad_pred))
    grad_state2 = (mm(up_high, dec_only) + mm(up_low, dec_only)) / KD
    grad_low = grad_state2.astype(BF)
    grad_turned = grad_state2.T.astype(BF)
    normed_turned = normed.astype(F32).T.astype(BF)

    def put(out_ref, side, part, first, value):
        done = 0
        while done < value.shape[1]:
            colour, column = divmod(first + done, 384)
            count = min(384 - column, value.shape[1] - done)
            for w in range(8):
                out_ref[colour, part, w ^ own_wide, :, column : column + count] = value[
                    w * LINES : (w + 1) * LINES, done : done + count
                ]
            done += count

    def backward(part, grad_n, out_ref, side):
        n = (part * 2 + side) ^ own_narrow
        act = act_ref[n]
        pre = pre_ref[n]
        put(out_ref, side, part, 640, mm(grad_turned, act).astype(BF))
        grad_act = mm(grad_low, late[:, n, :, 640:1152].reshape(D, HID))
        logistic = 1.0 / (1.0 + jnp.exp(-pre))
        grad_pre = (grad_act * logistic * (1.0 + pre * (1.0 - logistic))).astype(BF)
        put(out_ref, side, part, 0, mm(normed_turned, grad_pre).astype(BF))
        return grad_n + mm_nt(grad_pre, late[:, n, :, 0:512].reshape(D, HID))

    grad_n = jnp.zeros((D, D), F32)
    leaving = []

    def leave(source, there):
        leaving.append(pltpu.make_async_copy(source, there, out_sems.at[len(leaving)]))
        leaving[-1].start()

    for side, out_ref, there in ((1, send_ref, send_out), (0, keep_ref, keep_out)):
        grad_n = lax.fori_loop(0, 2, functools.partial(backward, out_ref=out_ref, side=side), grad_n)
        leave(out_ref.at[0], there.at[0])
        leave(out_ref.at[2], there.at[2])
    back, gain_grad = norm_pull(grad_n, normal, inverse, gain)
    grad_dec_ref[OUT + 1 : OUT + 2, :] = gain_grad
    grad_state1 = grad_state2 + back
    grad_state_ref[...] = grad_state1
    leave(grad_state_ref, grad_state_out)
    grad_low1 = grad_state1.astype(BF)
    grad_turned1 = grad_state1.T.astype(BF)
    for side, out_ref, there in ((1, send_ref, send_out), (0, keep_ref, keep_out)):
        for part in range(2):
            lane = pl.multiple_of(((part * 2 + side) ^ own_narrow) * 128, 128)
            put(out_ref, side, part, 512, mm(grad_turned1, mixed_ref[:, pl.ds(lane, 128)]).astype(BF))
        leave(out_ref.at[1], there.at[1])
    grad_mixed_ref[...] = mm(grad_low1, out_full).astype(BF)
    leave(grad_mixed_ref, grad_mixed_out)
    for copy in leaving:
        copy.wait()


def feed(place, scalars, late, early, state0, mixed, pool, pull, noisy, target, lat, level):
    nodes = state0.shape[0]
    width = pool.shape[0]
    vmem = pl.BlockSpec(memory_space=pltpu.VMEM)
    outside = pl.BlockSpec(memory_space=pltpu.HBM)
    return pl.pallas_call(
        feed_kernel,
        in_specs=[pl.BlockSpec(memory_space=pltpu.SMEM)] * 2 + [outside] * 13 + [vmem] * 4,
        out_specs=[outside] * 4 + [vmem] * 2,
        out_shape=(
            jax.ShapeDtypeStruct((3, 2, 8, LINES, 384), BF),
            jax.ShapeDtypeStruct((3, 2, 8, LINES, 384), BF),
            jax.ShapeDtypeStruct((nodes, D), F32),
            jax.ShapeDtypeStruct((nodes, D), BF),
            jax.ShapeDtypeStruct((128, D), F32),
            jax.ShapeDtypeStruct((8, 128), F32),
        ),
        scratch_shapes=[
            pltpu.VMEM((8, GROUPS, LINES, LATE), BF),
            pltpu.VMEM((8, GROUPS, 16, 128), BF),
            pltpu.VMEM((GROUPS, nodes, HID), F32),
            pltpu.VMEM((GROUPS, nodes, HID), BF),
            pltpu.VMEM((128, width), F32),
            pltpu.VMEM((nodes, D), F32),
            pltpu.VMEM((nodes, D), BF),
            pltpu.VMEM((width, nodes), BF),
            pltpu.VMEM((nodes, width), BF),
            pltpu.VMEM((3, 2, 8, LINES, 384), BF),
            pltpu.VMEM((3, 2, 8, LINES, 384), BF),
            pltpu.VMEM((nodes, D), F32),
            pltpu.VMEM((nodes, D), BF),
            pltpu.SemaphoreType.DMA((37,)),
            pltpu.SemaphoreType.DMA((2, GROUPS)),
            pltpu.SemaphoreType.DMA((8,)),
        ],
        compiler_params=pltpu.CompilerParams(vmem_limit_bytes=BIG),
        cost_estimate=pl.CostEstimate(flops=9_000_000_000, bytes_accessed=20_000_000, transcendentals=3_000_000),
        name="feed",
    )(place, scalars, *late, early, state0, mixed, pool, pull, noisy, target, lat, level)


def unmix_kernel(probs_ref, query_ref, keys_ref, values_ref, grad_mixed_ref, grad_query_ref, grad_pair_ref,
                 keys_sum, values_sum, grad_scores, grad_probs, key_turned):
    scale = HEAD_DIM ** (-0.5)
    chunk = 128

    def head(h, lane):
        keys_sum[...] = jnp.zeros_like(keys_sum)
        values_sum[...] = jnp.zeros_like(values_sum)
        key_turned[...] = keys_ref[:, pl.ds(lane, HEAD_DIM)].astype(F32).T.astype(BF)
        for band in range(2):
            at = band * BAND
            grad = grad_mixed_ref[at : at + BAND, pl.ds(lane, HEAD_DIM)]
            query = query_ref[at : at + BAND, pl.ds(lane, HEAD_DIM)]
            inner = jnp.zeros((1, BAND), F32)
            for i in range(WINDOW // chunk):
                row = i * chunk
                part = mm_nt(values_ref[at + row : at + row + chunk, pl.ds(lane, HEAD_DIM)], grad)
                grad_probs[row : row + chunk, :] = part
                inner = inner + jnp.sum(part * probs_ref[h, band, row : row + chunk, :].astype(F32), axis=0, keepdims=True)
            for i in range(WINDOW // chunk):
                row = i * chunk
                probs = probs_ref[h, band, row : row + chunk, :]
                low = (probs.astype(F32) * (grad_probs[row : row + chunk, :] - inner) * scale).astype(BF)
                grad_scores[row : row + chunk, :] = low
                keys_sum[at + row : at + row + chunk, :] += mm(low, query)
                values_sum[at + row : at + row + chunk, :] += mm(probs, grad)
            turned = mm(key_turned[:, at : at + WINDOW], grad_scores[...])
            grad_query_ref[at : at + BAND, pl.ds(lane, HEAD_DIM)] = turned.T.astype(BF)
        grad_pair_ref[:, 0:HEAD_DIM] = keys_sum[...].astype(BF)
        grad_pair_ref[:, HEAD_DIM : 2 * HEAD_DIM] = values_sum[...].astype(BF)

    head(0, 0)


def unmix(first, heads, probs, query, pair, grad_mixed):
    nodes = query.shape[0]
    part = pl.BlockSpec((nodes, HEAD_DIM), lambda i: (0, first + i))
    return pl.pallas_call(
        unmix_kernel,
        grid=(heads,),
        in_specs=[
            pl.BlockSpec((1, 2, WINDOW, BAND), lambda i: (first + i, 0, 0, 0)),
            part,
            pl.BlockSpec((NEAR, HEAD_DIM), lambda i: (0, 2 * (first + i))),
            pl.BlockSpec((NEAR, HEAD_DIM), lambda i: (0, 2 * (first + i) + 1)),
            part,
        ],
        out_specs=(
            pl.BlockSpec((nodes, HEAD_DIM), lambda i: (0, i)),
            pl.BlockSpec((NEAR, 2 * HEAD_DIM), lambda i: (0, i)),
        ),
        out_shape=(
            jax.ShapeDtypeStruct((nodes, heads * HEAD_DIM), BF),
            jax.ShapeDtypeStruct((NEAR, heads * 2 * HEAD_DIM), BF),
        ),
        scratch_shapes=[
            pltpu.VMEM((NEAR, HEAD_DIM), F32),
            pltpu.VMEM((NEAR, HEAD_DIM), F32),
            pltpu.VMEM((WINDOW, BAND), BF),
            pltpu.VMEM((WINDOW, BAND), F32),
            pltpu.VMEM((HEAD_DIM, NEAR), BF),
        ],
        compiler_params=pltpu.CompilerParams(vmem_limit_bytes=BIG),
        cost_estimate=pl.CostEstimate(
            flops=1_000_000_000 * heads, bytes_accessed=3_000_000 * heads, transcendentals=0
        ),
        name="unmix",
    )(probs, query, pair, pair, grad_mixed)


def return_kernel(
    place_ref, early_ref, query_in_a, query_in_b, pair_in_a, pair_in_b,
    grad_state_in, rows_in, normed_in, before_ref, sums_ref, after_ref, grad_dec_ref,
    keep_out, send_out,
    early, normed_ref, rows_ref, grad_state_ref, query_g, pair_g, keep_ref, send_ref, sems,
):
    pairs = (
        (normed_in, normed_ref),
        (query_in_a, query_g.at[:, 0:128]), (query_in_b, query_g.at[:, 128:512]),
        (pair_in_a, pair_g.at[:, 0:256]), (pair_in_b, pair_g.at[:, 256:1024]),
        (early_ref, early), (rows_in, rows_ref), (grad_state_in, grad_state_ref),
    )
    copies = [pltpu.make_async_copy(source, there, sems.at[i]) for i, (source, there) in enumerate(pairs)]
    for copy in copies:
        copy.start()
    own_wide, own_narrow = place_ref[0], place_ref[1]
    def put(n, colour, column, value, low):
        lines = value.shape[0] // 8
        for side, out_ref in ((1, send_ref), (0, keep_ref)):

            @pl.when(((n ^ own_narrow) & 1) == side)
            def _():
                part = (n ^ own_narrow) >> 1
                for w in range(8):
                    out_ref[colour, part, w ^ own_wide, low : low + lines, column : column + 128] = value[
                        w * lines : (w + 1) * lines, :
                    ]

    copies[0].wait()
    turned = normed_ref[...].astype(F32).T.astype(BF)
    for copy in copies[1:5]:
        copy.wait()
    weight_query = mm(turned[:, 512:1024], query_g[...]).astype(BF)
    weight_pair = mm(turned, pair_g[...]).astype(BF)
    for n in range(GROUPS):
        put(n, 0, 0, weight_query[:, n * 128 : n * 128 + 128], 0)
        put(n, 0, 128, weight_pair[:, n * 256 : n * 256 + 128], 0)
        put(n, 1, 0, weight_pair[:, n * 256 + 128 : n * 256 + 256], 0)
    leaving = [
        pltpu.make_async_copy(send_ref.at[0], send_out.at[0], sems.at[10]),
        pltpu.make_async_copy(keep_ref.at[0], keep_out.at[0], sems.at[11]),
        pltpu.make_async_copy(send_ref.at[1], send_out.at[1], sems.at[12]),
        pltpu.make_async_copy(keep_ref.at[1], keep_out.at[1], sems.at[13]),
    ]
    leaving[0].start()
    leaving[1].start()
    for copy in copies[5:]:
        copy.wait()
    gain = dec_of(early).astype(F32).T[OUT : OUT + 1, :]
    pair_weights = pair_of(early)
    grad_enc = jnp.zeros((IN, D), F32)
    gain_grad = jnp.zeros((1, D), F32)
    for block, sums in enumerate((before_ref, sums_ref, after_ref)):
        at = block * 512
        grad_block = mm_nt(pair_g[at : at + 512, :], pair_weights)
        if block == 1:
            grad_block = grad_block + mm_nt(query_g[...], query_of(early))
        normal, inverse = norm_parts(rows_ref[at : at + 512, :])
        back, gain_part = norm_pull(grad_block, normal, inverse, gain)
        gain_grad = gain_grad + gain_part
        if block == 1:
            back = back + grad_state_ref[...]
        back_low = (back * (1.0 / KG)).astype(BF)
        grad_enc = grad_enc + mm(sums[...].astype(BF), back_low)
    grad_enc = grad_enc.astype(BF)
    rows = lax.broadcasted_iota(jnp.int32, (128, 1), 0)
    grad_dec = jnp.where(rows == OUT, gain_grad, grad_dec_ref[...]).T.astype(BF)
    for n in range(GROUPS):
        put(n, 1, 128, grad_enc[:, n * 128 : n * 128 + 128], 0)
        put(n, 1, 128, grad_dec[n * 128 : n * 128 + 128, :], 32)
        put(n, 1, 128, jnp.zeros((128, 128), BF), 48)
    leaving[2].start()
    leaving[3].start()
    for copy in leaving:
        copy.wait()


def give_back(place, early, first, second, grad_state, rows, normed, before, sums, after, grad_dec):
    vmem = pl.BlockSpec(memory_space=pltpu.VMEM)
    outside = pl.BlockSpec(memory_space=pltpu.HBM)
    return pl.pallas_call(
        return_kernel,
        in_specs=[pl.BlockSpec(memory_space=pltpu.SMEM), outside] + [outside] * 7 + [vmem] * 4,
        out_specs=[outside] * 2,
        out_shape=(
            jax.ShapeDtypeStruct((2, 2, 8, LINES, 256), BF),
            jax.ShapeDtypeStruct((2, 2, 8, LINES, 256), BF),
        ),
        scratch_shapes=[
            pltpu.VMEM((8, GROUPS, LINES, EARLY), BF),
            pltpu.VMEM((NEAR, D), BF),
            pltpu.VMEM((NEAR, D), BF),
            pltpu.VMEM((512, D), F32),
            pltpu.VMEM((512, D), BF),
            pltpu.VMEM((NEAR, 2 * D), BF),
            pltpu.VMEM((2, 2, 8, LINES, 256), BF),
            pltpu.VMEM((2, 2, 8, LINES, 256), BF),
            pltpu.SemaphoreType.DMA((14,)),
        ],
        compiler_params=pltpu.CompilerParams(vmem_limit_bytes=BIG),
        cost_estimate=pl.CostEstimate(flops=5_000_000_000, bytes_accessed=12_000_000, transcendentals=0),
        name="give_back",
    )(
        place, early, first[0], second[0], first[1], second[1],
        grad_state, rows, normed, before, sums, after, grad_dec,
    )


def adam_kernel(row_ref, early_ref, late_ref, *refs):
    total = row_ref[0:1, 2:3] * MB
    norm_value = jnp.sqrt(row_ref[0:1, 0:1]) / total
    factor = jnp.minimum(1.0, clip_norm / norm_value) / total
    lanes = lax.broadcasted_iota(jnp.int32, (8, 128), 1)
    refs[36][...] = jnp.where(lanes == 0, row_ref[0:1, 1:2] / total, norm_value)
    fix_one = 1.0 - beta_one**STEPS_DONE
    fix_two = 1.0 - beta_two**STEPS_DONE
    enc_rows, read_rows = refs[0].shape[0], refs[12].shape[0]
    shares = (
        ((early_ref, slice(0, enc_rows), slice(384, 512), slice(None)),),
        ((early_ref, slice(None), slice(0, 384), slice(0, 384)), (late_ref, slice(None), slice(0, 512), slice(384, 896))),
        ((late_ref, slice(None), slice(512, 1152), slice(None)),),
        ((early_ref, slice(enc_rows, enc_rows + read_rows), slice(384, 384 + OUT + 2), slice(None)),),
    )
    for i, pieces in enumerate(shares):
        weight_ref, moment_ref, second_ref, average_ref = refs[4 * i : 4 * i + 4]
        outs = refs[16 + 5 * i : 21 + 5 * i]
        for share_ref, rows, columns, there in pieces:
            grad = share_ref[rows, columns] * factor
            weight = weight_ref[:, there]
            moment = beta_one * moment_ref[:, there] + (1.0 - beta_one) * grad
            second = beta_two * second_ref[:, there] + (1.0 - beta_two) * grad * grad
            weight = weight - learn_rate * (
                moment / fix_one / (jnp.sqrt(second / fix_two) + epsilon) + weight_decay * weight
            )
            outs[0][:, there] = moment
            outs[1][:, there] = second
            outs[2][:, there] = weight
            outs[3][:, there] = average_decay * average_ref[:, there] + (1.0 - average_decay) * weight
            outs[4][:, there] = weight.astype(BF)


def adam(row, early, late, states):
    arrays = [array for state in states for array in state]
    shapes = []
    for state in states:
        shapes += [jax.ShapeDtypeStruct(state[0].shape, F32)] * 4 + [jax.ShapeDtypeStruct(state[0].shape, BF)]
    shapes.append(jax.ShapeDtypeStruct((8, 128), F32))
    vmem = pl.BlockSpec(memory_space=pltpu.VMEM)
    return pl.pallas_call(
        adam_kernel,
        in_specs=[vmem] * 19,
        out_specs=[vmem] * 21,
        out_shape=shapes,
        compiler_params=pltpu.CompilerParams(vmem_limit_bytes=16 * MIB),
        cost_estimate=pl.CostEstimate(flops=3_000_000, bytes_accessed=4_000_000, transcendentals=200_000),
        name="adam",
    )(row, early, late, *arrays)


def pack_kernel(encoder_ref, up_ref, down_ref, readout_ref, early_ref, late_ref):
    enc_rows, read_rows = encoder_ref.shape[0], readout_ref.shape[0]
    early_ref[:, 0:384] = up_ref[:, 0:384].astype(BF)
    side = jnp.zeros((early_ref.shape[0] - enc_rows, 128), F32)
    early_ref[enc_rows:, 384:512] = side.astype(BF)
    early_ref[0:enc_rows, 384:512] = encoder_ref[...].astype(BF)
    early_ref[enc_rows : enc_rows + read_rows, 384 : 384 + OUT + 2] = readout_ref[...].astype(BF)
    late_ref[:, 0:512] = up_ref[:, 384:896].astype(BF)
    late_ref[:, 512:1152] = down_ref[...].astype(BF)


def pack(encoder, up_proj, down_turned, readout):
    lines = up_proj.shape[0]
    vmem = pl.BlockSpec(memory_space=pltpu.VMEM)
    return pl.pallas_call(
        pack_kernel,
        in_specs=[vmem] * 4,
        out_specs=[vmem] * 2,
        out_shape=(jax.ShapeDtypeStruct((lines, EARLY), BF), jax.ShapeDtypeStruct((lines, LATE), BF)),
        compiler_params=pltpu.CompilerParams(vmem_limit_bytes=8 * MIB),
        cost_estimate=pl.CostEstimate(flops=100_000, bytes_accessed=600_000, transcendentals=0),
        name="pack",
    )(encoder, up_proj, down_turned, readout)


def to_lines(array, wide):
    if wide == 8:
        return array
    lines, width = array.shape[2:]
    return jnp.moveaxis(jnp.moveaxis(array, 1, 0).reshape(GROUPS, 8, LINES, width), 0, 1)


def side_to_lines(side, wide):
    if wide == 8:
        return side
    enc_rows, read_rows = IN // wide, D // (GROUPS * wide)
    enc = to_rows(side[:, :, :enc_rows], 32)
    read = to_rows(side[:, :, enc_rows : enc_rows + read_rows], 16)
    return jnp.concatenate([enc, read, jnp.zeros((8, GROUPS, 16, 128), side.dtype)], axis=2)


def to_rows(array, rows):
    return jnp.moveaxis(jnp.moveaxis(array, 1, 0).reshape(GROUPS, 8, rows, array.shape[3]), 0, 1)


def from_rows(array, wide):
    rows, width = array.shape[2:]
    return jnp.moveaxis(jnp.moveaxis(array, 1, 0).reshape(GROUPS, wide, 8 * rows // wide, width), 0, 1)


def early_from_lines(array, wide):
    if wide == 8:
        return array
    main = from_rows(array[..., :384], wide)
    enc = from_rows(array[:, :, :32, 384:], wide)
    read = from_rows(array[:, :, 32:48, 384:], wide)
    spare = main.shape[2] - enc.shape[2] - read.shape[2]
    side = jnp.concatenate([enc, read, jnp.zeros((wide, GROUPS, spare, 128), array.dtype)], axis=2)
    return jnp.concatenate([main, side], axis=3)


ORDERS = ((1, 2, 3, 4), (2, 3, 1, 4), (3, 1, 2, 4))
DIMS = ((1, 2, 3, 4), (2, 1, 3, 4))
CUTS = (640, 512)


def by_relative(array, dims):
    array = array.reshape(2, 2, 2, 2, 2, *array.shape[2:])
    axes = {4: 0, 3: 1, 2: 2, 1: 3}
    turned = jnp.transpose(array, (4, *(axes[bit] for bit in dims), 5, 6))
    turned = turned.reshape(4, 8, *turned.shape[5:])
    return [turned[i] for i in range(4)]


def gather_plain(early, late, wide):
    def gathered(array):
        full = lax.all_gather(array, ("wide", "narrow"), axis=0, tiled=False)
        return full.reshape(wide, GROUPS, *array.shape)

    full = gathered(early)
    full = jnp.concatenate([to_lines(full[..., :384], wide), side_to_lines(full[..., 384:], wide)], axis=3)
    first = [by_relative(full[..., 256 * i : 256 * i + 256], DIMS[i]) for i in range(2)]
    full = to_lines(gathered(late), wide)
    second = [by_relative(part, DIMS[i]) for i, part in enumerate(jnp.split(full, [CUTS[0]], axis=3))]
    return sum(first, []), sum(second, [])


def joined(array, other):
    return jnp.concatenate([array[None], other[None]], axis=0)


def swap(array, bit):
    count = lax.axis_size("wide") * lax.axis_size("narrow")
    return lax.ppermute(array, ("wide", "narrow"), [(i, i ^ (1 << bit)) for i in range(count)])


def half_sum(parts, axis):
    return sum(lax.index_in_dim(part, 1, axis, keepdims=False).astype(F32) for part in parts).astype(BF)


def half_left(parts, axis):
    return [lax.index_in_dim(part, 0, axis, keepdims=False) for part in parts]


def halve(parts, axis, bit):
    return half_left(parts, axis) + [swap(half_sum(parts, axis), bit)]


def cube(array):
    return array.reshape(2, 2, 2, 2, *array.shape[2:])


def flat(array):
    return array.reshape(8, *array.shape[3:])


class Late:
    def __init__(self, keep, send):
        got = swap(send, 0)
        self.parts = [[cube(keep[i]), cube(got[i])] for i in range(3)]
        self.axes = [[1, 4, 3, 2] for _ in range(3)]

    def step(self, phase, values=()):
        at = [self.axes[i].index(order[phase]) for i, order in enumerate(ORDERS)]
        sent = [half_sum(self.parts[i], at[i]) for i in range(3)]
        sent, values = lax.optimization_barrier((sent, values))
        for i, order in enumerate(ORDERS):
            self.parts[i] = half_left(self.parts[i], at[i]) + [swap(sent[i], order[phase])]
            self.axes[i].pop(at[i])
        return values

    def last(self):
        sent = jnp.concatenate([half_sum(parts, 0) for parts in self.parts], axis=1)
        self.got = swap(sent, 4)
        self.parts = [half_left(parts, 0) for parts in self.parts]

    def total(self):
        kept = [sum(part.astype(F32) for part in parts) for parts in self.parts]
        return jnp.concatenate(kept, axis=1) + self.got.astype(F32)


class Early:
    def __init__(self, keep, send):
        got = swap(send, 0)
        self.first = [cube(keep[0]), cube(got[0])]
        self.second = [cube(keep[1]), cube(got[1])]

    def step(self, phase, late=None):
        if phase < 2:
            (at, bit), (at_other, bit_other) = (((0, 1), (3, 2)), ((2, 2), (0, 1)))[phase]
            sent = [half_sum(self.first, at), half_sum(self.second, at_other)]
            sent, late.parts = lax.optimization_barrier((sent, late.parts))
            self.first = half_left(self.first, at) + [swap(sent[0], bit)]
            self.second = half_left(self.second, at_other) + [swap(sent[1], bit_other)]
        else:
            if phase == 2:
                self.parts = [jnp.concatenate(pair, axis=3) for pair in zip(self.first, self.second)]
            self.parts = halve(self.parts, 3 - phase, phase + 1)

    def total(self):
        return sum(part.astype(F32) for part in self.parts)


def in_order(keep, send):
    both = jnp.stack([keep, send], axis=2)
    return jnp.moveaxis(both.reshape(both.shape[0], 4, *both.shape[3:]), 1, 2)


def scatter_sum(blocks):
    return lax.psum_scatter(
        blocks.astype(F32).reshape(-1, blocks.shape[3]), ("wide", "narrow"), scatter_dimension=0, tiled=True
    )


def sum_all(values):
    row = jnp.pad(jnp.stack(values)[None, :], ((0, 7), (0, 128 - len(values))))
    count = lax.axis_size("wide") * lax.axis_size("narrow")
    bit = 0
    while 1 << bit < count:
        masks = (1,) if bit == 0 or 2 << bit == count else (1, 2, 3)
        others = [lax.ppermute(row, ("wide", "narrow"), [(i, i ^ (mask << bit)) for i in range(count)]) for mask in masks]
        row = sum(others, row)
        bit += 1 if len(masks) == 1 else 2
    return row


def body(
    cond_fields,
    target,
    noise_draw,
    noise_sigma,
    grid_to_mesh,
    mesh_edges,
    mesh_to_grid,
    latitude_row,
    level_index,
    encoder,
    up_proj,
    down_proj,
    readout,
    encoder_moment,
    up_moment,
    down_moment,
    readout_moment,
    encoder_second,
    up_second,
    down_second,
    readout_second,
    encoder_average,
    up_average,
    down_average,
    readout_average,
):
    wide_index = lax.axis_index("wide")
    wide = lax.axis_size("wide")
    globe = lax.axis_index("narrow")
    nodes = mesh_edges.shape[0]
    pixels = cond_fields.shape[1]
    all_nodes = nodes * wide
    width = -(-pixels // 128) * 128

    place = jnp.stack([wide_index, globe]) if wide == 8 else jnp.zeros((2,), jnp.int32)
    early, late = pack(encoder, up_proj, down_proj.T, readout)
    moving = wide == 8
    tie = lax.optimization_barrier
    if moving:
        early_4 = swap(early, 4)

    if moving:
        early_1 = joined(early, early_4)
        late, early_1 = tie((late, early_1))
        late_4 = swap(late, 4)
        early_3 = swap(early_1, 3)
        early_1, target, noise_draw, noise_sigma = tie((early_1, target, noise_draw, noise_sigma))

    def own(array):
        return lax.dynamic_index_in_dim(jnp.transpose(array, (2, 0, 1)), globe, 1, keepdims=False)

    goal, noise = own(target), own(noise_draw)
    sigma = lax.dynamic_index_in_dim(noise_sigma, globe, 0, keepdims=False)
    square = sigma * sigma
    c_in = lax.rsqrt(square + 1.0)
    c_skip = 1.0 / (square + 1.0)
    c_out = sigma * c_in
    lam = (square + 1.0) / square
    if moving:
        early_3, late_4, goal, noise = tie((early_3, late_4, goal, noise))
        both, late_1 = joined(early_1, early_3), joined(late, late_4)
        first, second = both[..., :256], both[..., 256:]
        first, second, late_1, goal, noise = tie((first, second, late_1, goal, noise))
        first_2, second_2 = swap(first, 2), swap(second, 1)
        late_3 = swap(late_1, 3)
    noisy = goal + sigma * noise
    grid = jnp.concatenate([own(cond_fields), (c_in * noisy).astype(BF)], axis=0)
    grid = jnp.pad(grid, ((0, 0), (0, width - pixels)))
    edges = mesh_edges.T
    slot_rows = jnp.where(edges >= 0, (edges - wide_index * nodes + nodes + all_nodes) % all_nodes, -1)
    across = jnp.pad(mesh_to_grid.T - wide_index * nodes, ((0, 0), (0, width - pixels)), constant_values=-1)

    def halo(sums):
        low = sums.astype(BF)
        ring = [(i, (i + 1) % wide) for i in range(wide)]
        return lax.ppermute(low, "wide", ring), lax.ppermute(low, "wide", [(j, i) for i, j in ring])

    if moving:
        sums = grid_sums(grid, grid_to_mesh.T - wide_index * pixels)
        before, after = halo(sums)
        first_2, second_2, sums = tie((first_2, second_2, sums))
        first, second = joined(first, first_2), joined(second, second_2)
        first, second, late_3 = tie((first, second, late_3))
        first_1, second_1 = swap(first, 1), swap(second, 2)
        both = joined(late_1, late_3)
        parts = [both[..., : CUTS[0]], both[..., CUTS[0] :]]
        parts, slot_rows = tie((parts, slot_rows))
        got = [swap(parts[0], 2), swap(parts[1], 1)]
        bias, pool, pull = counts(slot_rows, across)
        bias, first_1, second_1, before, after, got = tie((bias, first_1, second_1, before, after, got))
        halves = [flat(first), first_1.reshape(8, LINES, 256), flat(second), second_1.reshape(8, LINES, 256)]
        others = [swap(half, 0) for half in halves]
        gathered = halves[:2] + others[:2] + halves[2:] + others[2:]
        parts = [joined(part, one) for part, one in zip(parts, got)]
        parts, sums = tie((parts, sums))
        got = [swap(parts[0], 1), swap(parts[1], 2)]
    else:
        gathered, late_full = gather_plain(early, late, wide)
        sums = grid_sums(grid, grid_to_mesh.T - wide_index * pixels)
        bias, pool, pull = counts(slot_rows, across)
        before, after = halo(sums)

    lat_weight = jnp.cos((latitude_row.astype(F32) - 90.0) * (math.pi / 180.0))
    level_weight = (level_index.astype(F32) + 1.0) / LEVELS
    pix_total = jnp.sum(lat_weight) * jnp.sum(level_weight)

    state0, rows, normed, query, pair, early_full = encode(place, gathered, before, sums, after)
    if moving:
        got, query = tie((got, query))
        late_full = []
        for part, one, cut in zip(parts, got, CUTS):
            halves = [flat(part), one.reshape(8, LINES, cut)]
            late_full += halves + [swap(half, 0) for half in halves]
    mixed, probs = attend(query, pair, bias)
    if moving:
        mixed, late_full = tie((mixed, late_full))
    keep_late, send_late, grad_state, grad_mixed, grad_dec, loss_part = feed(
        place, jnp.stack([c_skip, c_out, lam]),
        late_full, early_full, state0, mixed, pool, pull, noisy, goal, lat_weight[None, :], level_weight[:, None],
    )
    if moving:
        late_sum = Late(keep_late, send_late)
    first_heads = unmix(0, 1, probs, query, pair, grad_mixed)
    if moving:
        query, first_heads = late_sum.step(0, (query, first_heads))
    last_heads = unmix(1, 3, probs, query, pair, grad_mixed)
    if moving:
        grad_state, last_heads = late_sum.step(1, (grad_state, last_heads))
    keep_early, send_early = give_back(
        place, early_full, first_heads, last_heads, grad_state, rows, normed, before, sums, after, grad_dec
    )
    if moving:
        early_sum = Early(keep_early, send_early)
        early_sum.step(0, late_sum)
        late_sum.step(2)
        early_sum.step(1, late_sum)
        late_sum.last()
        early_sum.step(2)
        early_sum.step(3)
        share_late, share_early = late_sum.total(), early_sum.total()
    else:
        late_lines = jnp.concatenate(list(in_order(keep_late, send_late)), axis=3)
        early_lines = jnp.concatenate(list(in_order(keep_early, send_early)), axis=3)
        share_late = scatter_sum(from_rows(late_lines, wide))
        share_early = scatter_sum(early_from_lines(early_lines, wide))
    first_globe = (globe == 0).astype(F32)
    row = sum_all(
        [jnp.sum(share_early * share_early) + jnp.sum(share_late * share_late), loss_part[0, 0], pix_total * first_globe]
    )
    states = [
        (encoder, encoder_moment, encoder_second, encoder_average),
        (up_proj, up_moment, up_second, up_average),
        (down_proj.T, down_moment.T, down_second.T, down_average.T),
        (readout, readout_moment, readout_second, readout_average),
    ]
    news = list(adam(row, share_early, share_late, states))
    news[10:15] = [array.T for array in news[10:15]]
    return (news[20][0, 0], news[20][0, 1], *news[:20])


def solution(mesh):
    if mesh.shape["narrow"] != GROUPS or MB != GROUPS:
        raise ValueError("narrow size")
    by_pixel = P(None, "wide", None)
    pair = P("wide", "narrow")
    weights = (pair, pair, P("narrow", "wide"), P(("narrow", "wide"), None))
    placed = (by_pixel, by_pixel, by_pixel, P()) + (P("wide", None),) * 3 + (P("wide"), P()) + weights * 4
    given = (P(), P())
    for spec in weights:
        given = given + (spec,) * 5
    return jax.shard_map(body, mesh=mesh, in_specs=placed, out_specs=given, check_vma=False)
```

```python
import functools
import math

import jax
import jax.numpy as jnp
from jax import lax
from jax.experimental import pallas as pl
from jax.experimental.pallas import tpu as pltpu
from jax.sharding import PartitionSpec as P

D = 512
HEADS = 4
HEAD_DIM = 128
OUT = 84
IN = 256
LEVELS = 13
KM = 16
KG = 8
KD = 3
STEPS_DONE = 7
MB = 4
GROUPS = 4
HID = 512
ROWS = 8
LINES = 64
EARLY = 512
LATE = 1152
BAND = 256
WINDOW = 1280
NEAR = 1536

clip_norm = 0.001
beta_one = 0.9
beta_two = 0.999
epsilon = 1e-08
learn_rate = 0.04
weight_decay = 0.1
average_decay = 0.9

BF = jnp.bfloat16
F32 = jnp.float32
MIB = 1024 * 1024
QUICK = pl.CostEstimate(flops=1000, bytes_accessed=1000, transcendentals=0)
BIG = 60 * MIB


def mm(left, right):
    return jnp.dot(left, right, preferred_element_type=F32)


def mm_nt(left, right):
    return lax.dot_general(left, right, (((1,), (1,)), ((), ())), preferred_element_type=F32)


def mm_tn(left, right):
    return lax.dot_general(left, right, (((0,), (0,)), ((), ())), preferred_element_type=F32)


def split_two(value):
    high = value.astype(BF)
    return high, (value - high.astype(F32)).astype(BF)


def norm_parts(rows_low):
    values = rows_low.astype(F32)
    center = values - jnp.mean(values, axis=-1, keepdims=True)
    inverse = lax.rsqrt(jnp.mean(center * center, axis=-1, keepdims=True) + 1e-05)
    return center * inverse, inverse


def norm_pull(grad_out, normal, inverse, gain):
    scaled = grad_out * gain
    inner = (
        scaled
        - jnp.mean(scaled, axis=-1, keepdims=True)
        - normal * jnp.mean(scaled * normal, axis=-1, keepdims=True)
    )
    return inner * inverse, jnp.sum(grad_out * normal, axis=0, keepdims=True)


class Leaving:
    def __init__(self, sems):
        self.sems, self.copies = sems, []

    def __call__(self, source, there):
        self.copies.append(pltpu.make_async_copy(source, there, self.sems.at[len(self.copies)]))
        self.copies[-1].start()

    def wait(self):
        for copy in self.copies:
            copy.wait()


def sums_kernel(grid_ref, pixels_ref, sums_ref, count_ref):
    width, nodes = count_ref.shape
    step = 32
    picks = [jnp.broadcast_to(pixels_ref[k : k + 1, :], (step, nodes)) for k in range(KG)]
    rows = lax.broadcasted_iota(jnp.int32, (step, nodes), 0)

    def count(i, _):
        at = pl.multiple_of(i * step, step)
        total = jnp.zeros((step, nodes), F32)
        for pick in picks:
            total = total + jnp.where(pick - at == rows, 1.0, 0.0)
        count_ref[pl.ds(at, step), :] = total.astype(BF)
        return 0

    lax.fori_loop(0, width // step, count, 0)
    sums_ref[...] = mm(grid_ref[...], count_ref[...])


def grid_sums(grid, pixel_rows):
    nodes, width = pixel_rows.shape[1], grid.shape[1]
    return pl.pallas_call(
        sums_kernel,
        out_shape=jax.ShapeDtypeStruct((IN, nodes), F32),
        scratch_shapes=[pltpu.VMEM((width, nodes), BF)],
        compiler_params=pltpu.CompilerParams(vmem_limit_bytes=16 * 1024 * 1024),
        cost_estimate=QUICK,
        name="grid_sums",
    )(grid, pixel_rows)


def counts_kernel(slots_ref, across_ref, bias_out, pool_out, pull_out, bias_ref, pool_ref, pull_ref, sems):
    nodes, width = pull_ref.shape
    step = 64
    leave = Leaving(sems)

    def count_across(i, _):
        at = pl.multiple_of(i * 128, 128)
        rows = lax.broadcasted_iota(jnp.int32, (128, width), 0) + at
        total = jnp.zeros((128, width), F32)
        for k in range(KD):
            total = total + jnp.where(across_ref[k : k + 1, :] == rows, 1.0, 0.0)
        pull_ref[pl.ds(at, 128), :] = total.astype(BF)
        pool_ref[:, pl.ds(at, 128)] = total.T.astype(BF)
        return 0

    lax.fori_loop(0, nodes // 128, count_across, 0)
    leave(pool_ref, pool_out)
    leave(pull_ref, pull_out)
    for band in range(nodes // BAND):
        low = band * BAND
        picks = slots_ref[:, low : low + BAND] - low
        rows = lax.broadcasted_iota(jnp.int32, (step, BAND), 0)
        alike = jnp.zeros((KM, BAND), F32)
        for k in range(KM):
            alike = alike + jnp.where(picks == picks[k : k + 1, :], 1.0, 0.0)
        weight = jnp.log2(alike)

        def count_slots(i, _):
            at = pl.multiple_of(i * step, step)
            value = jnp.full((step, BAND), -1e30, F32)
            for k in range(KM):
                value = jnp.where(picks[k : k + 1, :] - at == rows, weight[k : k + 1, :], value)
            bias_ref[band, pl.ds(at, step), :] = value
            return 0

        for part in range(2):
            half = WINDOW // step // 2
            lax.fori_loop(part * half, (part + 1) * half, count_slots, 0)
            here = slice(part * half * step, (part + 1) * half * step)
            leave(bias_ref.at[band, here], bias_out.at[band, here])
    leave.wait()


def counts(slot_rows, across_rows):
    nodes, width = slot_rows.shape[1], across_rows.shape[1]
    shapes = (
        jax.ShapeDtypeStruct((nodes // BAND, WINDOW, BAND), F32),
        jax.ShapeDtypeStruct((width, nodes), BF),
        jax.ShapeDtypeStruct((nodes, width), BF),
    )
    return pl.pallas_call(
        counts_kernel,
        out_specs=[pl.BlockSpec(memory_space=pltpu.HBM)] * 3,
        out_shape=shapes,
        scratch_shapes=[pltpu.VMEM(shape.shape, shape.dtype) for shape in shapes] + [pltpu.SemaphoreType.DMA((6,))],
        compiler_params=pltpu.CompilerParams(vmem_limit_bytes=BIG),
        cost_estimate=QUICK,
        name="counts",
    )(slot_rows, across_rows)


def blocks_of(place_ref, dims, refs):
    own_wide, own_narrow = place_ref[0], place_ref[1]
    found = []
    for side in range(2):
        for j in range(16):
            bits = dict(zip(dims, ((j >> 3) & 1, (j >> 2) & 1, (j >> 1) & 1, j & 1)))
            wide = own_wide ^ (bits[4] * 4 + bits[3] * 2 + bits[2])
            narrow = own_narrow ^ (bits[1] * 2 + side)
            found.append((wide, narrow, refs[2 * side + (j >> 3)].at[j & 7]))
    return found


def block_at(dims, part, wide):
    bits = {1: part, 2: wide & 1, 3: (wide >> 1) & 1, 4: wide >> 2}
    return ((bits[dims[0]] * 2 + bits[dims[1]]) * 2 + bits[dims[2]]) * 2 + bits[dims[3]]


def fetch_early(place_ref, refs, early, sems):
    return [
        pltpu.make_async_copy(source, early.at[wide, narrow], sems.at[i])
        for i, (wide, narrow, source) in enumerate(blocks_of(place_ref, DIMS[0], refs))
    ]


def enc_of(early):
    return jnp.concatenate([early[:, n, 0:32, 384:512].reshape(IN, 128) for n in range(GROUPS)], axis=1)


def dec_of(early):
    return jnp.concatenate([early[:, n, 32:48, 384:512].reshape(128, 128) for n in range(GROUPS)], axis=0)


def query_of(early):
    return jnp.concatenate([early[:, n, :, 0:128].reshape(D, 128) for n in range(GROUPS)], axis=1)


def pair_of(early):
    return jnp.concatenate([early[:, n, :, 128:384].reshape(D, 256) for n in range(GROUPS)], axis=1)


def encode_kernel(
    place_ref, a_0, a_1, a_2, a_3, before_ref, sums_ref, after_ref,
    state_ref, rows_ref, normed_ref, early_ref,
    early, state, rows_all, normed_all, sems, out_sems,
):
    copies = fetch_early(place_ref, (a_0, a_1, a_2, a_3), early, sems)
    for copy in copies:
        copy.start()
    for copy in copies:
        copy.wait()
    leave = Leaving(out_sems)
    leave(early, early_ref)
    gain = dec_of(early).astype(F32).T[OUT : OUT + 1, :]
    enc = enc_of(early)
    for block, ref in enumerate((before_ref, sums_ref, after_ref)):
        here = slice(block * 512, block * 512 + 512)
        if block == 1:
            high, low = split_two(ref[...])
            embedded = (mm_tn(high, enc) + mm_tn(low, enc)) * (1.0 / KG)
            state[...] = embedded
            leave(state, state_ref)
        else:
            embedded = mm_tn(ref[...], enc) * (1.0 / KG)
        rows = embedded.astype(BF)
        rows_all[here, :] = rows
        leave(rows_all.at[here], rows_ref.at[here])
        normal, _inverse = norm_parts(rows)
        normed_all[here, :] = (normal * gain).astype(BF)
        leave(normed_all.at[here], normed_ref.at[here])
    leave.wait()


def encode(place, gathered, before, sums, after):
    nodes = sums.shape[1]
    vmem = pl.BlockSpec(memory_space=pltpu.VMEM)
    outside = pl.BlockSpec(memory_space=pltpu.HBM)
    shapes = (
        jax.ShapeDtypeStruct((nodes, D), F32),
        jax.ShapeDtypeStruct((NEAR, D), BF),
        jax.ShapeDtypeStruct((NEAR, D), BF),
        jax.ShapeDtypeStruct((8, GROUPS, LINES, EARLY), BF),
    )
    return pl.pallas_call(
        encode_kernel,
        in_specs=[pl.BlockSpec(memory_space=pltpu.SMEM)] + [outside] * 4 + [vmem] * 3,
        out_specs=[outside] * 4,
        out_shape=shapes,
        scratch_shapes=[pltpu.VMEM((8, GROUPS, LINES, EARLY), BF)]
        + [pltpu.VMEM(shape.shape, shape.dtype) for shape in shapes[:3]]
        + [pltpu.SemaphoreType.DMA((32,)), pltpu.SemaphoreType.DMA((8,))],
        compiler_params=pltpu.CompilerParams(vmem_limit_bytes=BIG),
        cost_estimate=QUICK,
        name="encode",
    )(place, *gathered, before, sums, after)


def attend_kernel(
    normed_in, early_in, bias_in, mixed_ref, probs_ref, query_ref, pair_ref, inverse_ref,
    normed, early, bias, query_all, pair_all, mixed_all, probs, inverse_all, sems, out_sems,
):
    def weight_copy(h):
        return pltpu.make_async_copy(early_in.at[:, h, :, 0:384], early.at[h], sems.at[h])

    normed_copy = pltpu.make_async_copy(normed_in, normed, sems.at[4])
    bias_copies = [pltpu.make_async_copy(bias_in.at[i], bias.at[i], sems.at[5 + i]) for i in range(2)]
    weight_copy(0).start()
    normed_copy.start()
    bias_copies[0].start()
    bias_copies[1].start()
    for h in range(1, HEADS):
        weight_copy(h).start()
    normed_copy.wait()
    factor = HEAD_DIM ** (-0.5) * math.log2(math.e)

    def pair_leave(h):
        return pltpu.make_async_copy(pair_all.at[h], pair_ref.at[h], out_sems.at[8 + h])

    def probs_leave(h):
        return pltpu.make_async_copy(probs.at[h], probs_ref.at[h], out_sems.at[4 + h])

    for h in range(HEADS):
        lanes = slice(h * HEAD_DIM, h * HEAD_DIM + HEAD_DIM)
        weight_copy(h).wait()
        weights = early[h].reshape(D, 384)
        pair_all[h] = mm(normed[...], weights[:, 128:384]).astype(BF)
        query_all[:, lanes] = mm(normed[512:1024, :], weights[:, 0:128]).astype(BF)
        if h == 0:
            bias_copies[0].wait()
            bias_copies[1].wait()
        for band in range(2):
            at = band * BAND
            near, here = slice(at, at + WINDOW), slice(at, at + BAND)
            part = mm_nt(pair_all[h, near, :HEAD_DIM], query_all[here, lanes]) * factor + bias[band]
            expo = jnp.exp2(part - jnp.max(part, axis=0, keepdims=True))
            inverse = 1.0 / jnp.sum(expo, axis=0, keepdims=True)
            low = expo.astype(BF)
            probs[h, near, here] = low
            inverse_all[h : h + 1, here] = inverse
            column = jnp.broadcast_to(inverse, (8, BAND)).T[:, 0:1]
            mixed_all[here, lanes] = mm_tn(low, pair_all[h, near, HEAD_DIM:]) * column
        probs_leave(h).start()
        pair_leave(h).start()
    inverse_all[HEADS:8, :] = jnp.zeros((8 - HEADS, inverse_all.shape[1]), F32)
    leave = Leaving(out_sems)
    leave(mixed_all, mixed_ref)
    leave(query_all, query_ref)
    leave(inverse_all, inverse_ref)
    leave.wait()
    for h in range(HEADS):
        pair_leave(h).wait()
        probs_leave(h).wait()


def attend(normed, early, bias):
    nodes = normed.shape[0] // 3
    outside = pl.BlockSpec(memory_space=pltpu.HBM)
    return pl.pallas_call(
        attend_kernel,
        in_specs=[outside] * 3,
        out_specs=[outside] * 5,
        out_shape=(
            jax.ShapeDtypeStruct((nodes, D), F32),
            jax.ShapeDtypeStruct((HEADS, NEAR, nodes), BF),
            jax.ShapeDtypeStruct((nodes, D), BF),
            jax.ShapeDtypeStruct((HEADS, NEAR, 2 * HEAD_DIM), BF),
            jax.ShapeDtypeStruct((8, nodes), F32),
        ),
        scratch_shapes=[
            pltpu.VMEM((NEAR, D), BF),
            pltpu.VMEM((GROUPS, 8, LINES, 384), BF),
            pltpu.VMEM((2, WINDOW, BAND), F32),
            pltpu.VMEM((nodes, D), BF),
            pltpu.VMEM((HEADS, NEAR, 2 * HEAD_DIM), BF),
            pltpu.VMEM((nodes, D), F32),
            pltpu.VMEM((HEADS, NEAR, nodes), BF),
            pltpu.VMEM((8, nodes), F32),
            pltpu.SemaphoreType.DMA((7,)),
            pltpu.SemaphoreType.DMA((12,)),
        ],
        compiler_params=pltpu.CompilerParams(vmem_limit_bytes=BIG),
        cost_estimate=QUICK,
        name="attend",
    )(normed, early, bias)


def feed_kernel(
    place_ref, sigma_ref, a_0, a_1, a_2, a_3, b_0, b_1, b_2, b_3, early_ref, state_in, mixed_in, pool_in, pull_in, inverse_ref, noisy_ref, target_ref, lat_ref, level_ref,
    keep_0, keep_1, keep_2, send_0, send_1, send_2, grad_state_out, grad_mixed_out, grad_scaled_out, inner_ref, grad_dec_ref, loss_ref,
    late, dec, pre_ref, act_ref, grad_pred_ref,
    state_ref, mixed_ref, pool_ref, pull_ref, keep_ref, send_ref, grad_state_ref, grad_mixed_ref, grad_scaled_ref, sems, group_sems, out_sems,
):
    own_wide, own_narrow = place_ref[0], place_ref[1]

    refs = (a_0, a_1, a_2, a_3), (b_0, b_1, b_2, b_3)

    def fetch(colour, columns, first, sem):
        there = slice(first, first + columns.stop - columns.start)
        return [
            pltpu.make_async_copy(source.at[:, columns], late.at[wide, narrow, :, there], sem(narrow, i))
            for i, (wide, narrow, source) in enumerate(blocks_of(place_ref, DIMS[colour], refs[colour]))
        ]

    def group(n, columns, row):
        return pltpu.make_async_copy(late.at[:, n, :, columns], late.at[:, n, :, columns], group_sems.at[row, n])

    hidden, outer, lower = slice(0, 512), slice(512, 640), slice(640, 1152)
    pairs = [(state_in, state_ref), (mixed_in, mixed_ref), (early_ref.at[:, :, 32:48, 384:512], dec)]
    small = [pltpu.make_async_copy(source, there, sems.at[32 + i]) for i, (source, there) in enumerate(pairs)]
    small += fetch(0, outer, 512, lambda n, i: sems.at[i])
    pool_copy = pltpu.make_async_copy(pool_in, pool_ref, sems.at[35])
    pull_copy = pltpu.make_async_copy(pull_in, pull_ref, sems.at[36])
    first = fetch(0, hidden, 0, lambda n, i: group_sems.at[0, n])
    second = fetch(1, slice(0, 512), 640, lambda n, i: group_sems.at[1, n])
    for copy in (*small, *first, *second, pool_copy, pull_copy):
        copy.start()
    for copy in small:
        copy.wait()
    dec_turned = jnp.concatenate([dec[:, n].reshape(128, 128) for n in range(GROUPS)], axis=0).astype(F32).T
    gain = dec_turned[OUT + 1 : OUT + 2, :]
    rows = lax.broadcasted_iota(jnp.int32, (128, 1), 0)
    dec_only = jnp.where(rows < OUT, dec_turned, 0.0).astype(BF)
    out_full = jnp.concatenate([late[:, n, :, 512:640].reshape(D, 128) for n in range(GROUPS)], axis=1)
    mixed = mixed_ref[...].astype(BF)
    state1 = state_ref[...] + mm_nt(mixed, out_full)
    normal, inverse = norm_parts(state1.astype(BF))
    normed = (normal * gain).astype(BF)

    def forward(i, state):
        n = i ^ own_narrow
        group(n, hidden, 0).wait()
        pre = mm(normed, late[:, n, :, 0:512].reshape(D, HID))
        pre_ref[n] = pre
        act = (pre / (1.0 + jnp.exp(-pre))).astype(BF)
        act_ref[n] = act
        group(n, lower, 1).wait()
        return state + mm_nt(act, late[:, n, :, 640:1152].reshape(D, HID))

    state2 = state1
    for i in range(GROUPS):
        state2 = forward(i, state2)
    high, low = split_two(state2)
    pool_copy.wait()
    pull_copy.wait()
    pool = pool_ref[...]
    pooled = ((mm(pool, high) + mm(pool, low)) / KD).astype(BF)
    pixels = noisy_ref.shape[1]
    pred = mm_nt(dec_only, pooled)[:OUT, :pixels]
    sigma = jnp.full((1, 1), sigma_ref[place_ref[2]], F32)
    square = sigma * sigma
    c_skip = 1.0 / (square + 1.0)
    c_out = sigma * lax.rsqrt(square + 1.0)
    lam = (square + 1.0) / square
    error = c_skip * noisy_ref[...] + c_out * pred - target_ref[...]
    weight = jnp.cos((lat_ref[...].astype(F32) - 90.0) * (math.pi / 180.0)) * ((level_ref[...].astype(F32) + 1.0) / LEVELS)
    weighted = lam * weight
    first_globe = (jnp.full((1, 1), place_ref[2], jnp.int32) == 0).astype(F32)
    lanes = lax.broadcasted_iota(jnp.int32, (1, 128), 1)
    loss_ref[...] = jnp.where(lanes == 1, jnp.sum(weighted * error * error), 0.0) + jnp.where(
        lanes == 2, jnp.sum(weight) * first_globe, 0.0
    )
    grad_pred_ref[...] = jnp.zeros_like(grad_pred_ref)
    grad_pred_ref[:OUT, :pixels] = 2.0 * c_out * weighted * error
    grad_pred = grad_pred_ref[...].astype(BF)
    grad_dec_ref[...] = mm(grad_pred, pooled)
    up_high, up_low = split_two(mm_nt(pull_ref[...], grad_pred))
    grad_state2 = (mm(up_high, dec_only) + mm(up_low, dec_only)) / KD
    grad_low = grad_state2.astype(BF)
    grad_turned = grad_state2.T.astype(BF)
    normed_turned = normed.astype(F32).T.astype(BF)

    def put(out_ref, side, part, first, value):
        done = 0
        while done < value.shape[1]:
            colour, column = divmod(first + done, 384)
            count = min(384 - column, value.shape[1] - done)
            for w in range(8):
                out_ref[colour, block_at(ORDERS[colour], part, w ^ own_wide), :, column : column + count] = value[
                    w * LINES : (w + 1) * LINES, done : done + count
                ]
            done += count

    def backward(part, grad_n, out_ref, side):
        n = (part * 2 + side) ^ own_narrow
        act = act_ref[n]
        pre = pre_ref[n]
        put(out_ref, side, part, 640, mm(grad_turned, act).astype(BF))
        grad_act = mm(grad_low, late[:, n, :, 640:1152].reshape(D, HID))
        logistic = 1.0 / (1.0 + jnp.exp(-pre))
        grad_pre = (grad_act * logistic * (1.0 + pre * (1.0 - logistic))).astype(BF)
        put(out_ref, side, part, 0, mm(normed_turned, grad_pre).astype(BF))
        return grad_n + mm_nt(grad_pre, late[:, n, :, 0:512].reshape(D, HID))

    grad_n = jnp.zeros((D, D), F32)
    leaving = []

    def leave(source, there):
        leaving.append(pltpu.make_async_copy(source, there, out_sems.at[len(leaving)]))
        leaving[-1].start()

    sides = ((1, send_ref, (send_0, send_1, send_2)), (0, keep_ref, (keep_0, keep_1, keep_2)))
    for side, out_ref, there in sides:
        for part in range(2):
            grad_n = backward(part, grad_n, out_ref, side)
        leave(out_ref.at[0], there[0])
        leave(out_ref.at[2], there[2])
    back, gain_grad = norm_pull(grad_n, normal, inverse, gain)
    grad_dec_ref[OUT + 1 : OUT + 2, :] = gain_grad
    grad_state1 = grad_state2 + back
    grad_state_ref[...] = grad_state1
    leave(grad_state_ref, grad_state_out)
    grad_low1 = grad_state1.astype(BF)
    act_ref[0] = mixed
    grad_turned1 = grad_state1.T.astype(BF)
    for side, out_ref, there in sides:
        for part in range(2):
            lane = pl.multiple_of(((part * 2 + side) ^ own_narrow) * 128, 128)
            put(out_ref, side, part, 512, mm(grad_turned1, act_ref[0, :, pl.ds(lane, 128)]).astype(BF))
        leave(out_ref.at[1], there[1])
    grad_mixed = mm(grad_low1, out_full)
    grad_mixed_ref[...] = grad_mixed.astype(BF)
    leave(grad_mixed_ref, grad_mixed_out)
    columns = inverse_ref[...].T
    lanes = lax.broadcasted_iota(jnp.int32, (1, 128), 1)
    inner = jnp.zeros((grad_mixed.shape[0], 128), F32)
    for h in range(HEADS):
        here = slice(h * HEAD_DIM, h * HEAD_DIM + HEAD_DIM)
        grad = grad_mixed[:, here]
        grad_scaled_ref[:, here] = (grad * columns[:, h : h + 1]).astype(BF)
        inner = jnp.where(lanes == h, jnp.sum(grad * mixed_ref[:, here], axis=1, keepdims=True), inner)
    leave(grad_scaled_ref, grad_scaled_out)
    inner_ref[...] = inner.T[0:8, :]
    for copy in leaving:
        copy.wait()


def feed(place, sigma, late, early, state0, mixed, pool, pull, inverse, noisy, target, lat, level):
    nodes = state0.shape[0]
    width = pool.shape[0]
    vmem = pl.BlockSpec(memory_space=pltpu.VMEM)
    outside = pl.BlockSpec(memory_space=pltpu.HBM)
    return pl.pallas_call(
        feed_kernel,
        in_specs=[pl.BlockSpec(memory_space=pltpu.SMEM)] * 2 + [outside] * 13 + [vmem] * 5,
        out_specs=[outside] * 9 + [vmem] * 3,
        out_shape=(
            *([jax.ShapeDtypeStruct((16, LINES, 384), BF)] * 6),
            jax.ShapeDtypeStruct((nodes, D), F32),
            jax.ShapeDtypeStruct((nodes, D), BF),
            jax.ShapeDtypeStruct((nodes, D), BF),
            jax.ShapeDtypeStruct((8, nodes), F32),
            jax.ShapeDtypeStruct((128, D), F32),
            jax.ShapeDtypeStruct((1, 128), F32),
        ),
        scratch_shapes=[
            pltpu.VMEM((8, GROUPS, LINES, LATE), BF),
            pltpu.VMEM((8, GROUPS, 16, 128), BF),
            pltpu.VMEM((GROUPS, nodes, HID), F32),
            pltpu.VMEM((GROUPS, nodes, HID), BF),
            pltpu.VMEM((128, width), F32),
            pltpu.VMEM((nodes, D), F32),
            pltpu.VMEM((nodes, D), F32),
            pltpu.VMEM((width, nodes), BF),
            pltpu.VMEM((nodes, width), BF),
            pltpu.VMEM((3, 16, LINES, 384), BF),
            pltpu.VMEM((3, 16, LINES, 384), BF),
            pltpu.VMEM((nodes, D), F32),
            pltpu.VMEM((nodes, D), BF),
            pltpu.VMEM((nodes, D), BF),
            pltpu.SemaphoreType.DMA((37,)),
            pltpu.SemaphoreType.DMA((2, GROUPS)),
            pltpu.SemaphoreType.DMA((9,)),
        ],
        compiler_params=pltpu.CompilerParams(vmem_limit_bytes=BIG),
        cost_estimate=QUICK,
        name="feed",
    )(place, sigma, *late, early, state0, mixed, pool, pull, inverse, noisy, target, lat, level)


def unmix_kernel(first, probs_ref, query_ref, keys_ref, values_ref, grad_mixed_ref, grad_scaled_ref, inner_ref, inverse_ref,
                 grad_query_ref, grad_pair_ref, grad_scores):
    scale = HEAD_DIM ** (-0.5)
    row = pl.ds(first + pl.program_id(0), 1)
    inner = inner_ref[row, :]
    factor = inverse_ref[row, :] * scale
    pieces = ((0, 256, 0, 256), (256, 768, 0, 512), (768, 1280, 0, 512), (1280, 1536, 256, 512))
    for low_row, high_row, low_column, high_column in pieces:
        rows, columns = slice(low_row, high_row), slice(low_column, high_column)
        probs = probs_ref[0, rows, columns]
        grad_probs = mm_nt(values_ref[0, rows, :], grad_mixed_ref[columns, :])
        low = (probs.astype(F32) * ((grad_probs - inner[:, columns]) * factor[:, columns])).astype(BF)
        grad_scores[rows, columns] = low
        grad_pair_ref[rows, 0:HEAD_DIM] = mm(low, query_ref[columns, :]).astype(BF)
        grad_pair_ref[rows, HEAD_DIM : 2 * HEAD_DIM] = mm(probs, grad_scaled_ref[columns, :]).astype(BF)
    for at in (0, BAND):
        grad_query_ref[at : at + BAND, :] = mm_tn(
            grad_scores[at : at + WINDOW, at : at + BAND], keys_ref[0, at : at + WINDOW, :]
        ).astype(BF)


def unmix(first, heads, probs, query, pair, grad_mixed, grad_scaled, inner, inverse):
    nodes = query.shape[0]
    part = pl.BlockSpec((nodes, HEAD_DIM), lambda i: (0, first + i))
    whole = pl.BlockSpec((8, nodes), lambda i: (0, 0))
    return pl.pallas_call(
        functools.partial(unmix_kernel, first),
        grid=(heads,),
        in_specs=[
            pl.BlockSpec((1, NEAR, nodes), lambda i: (first + i, 0, 0)),
            part,
            pl.BlockSpec((1, NEAR, HEAD_DIM), lambda i: (first + i, 0, 0)),
            pl.BlockSpec((1, NEAR, HEAD_DIM), lambda i: (first + i, 0, 1)),
            part,
            part,
            whole,
            whole,
        ],
        out_specs=(
            pl.BlockSpec((nodes, HEAD_DIM), lambda i: (0, i)),
            pl.BlockSpec((NEAR, 2 * HEAD_DIM), lambda i: (0, i)),
        ),
        out_shape=(
            jax.ShapeDtypeStruct((nodes, heads * HEAD_DIM), BF),
            jax.ShapeDtypeStruct((NEAR, heads * 2 * HEAD_DIM), BF),
        ),
        scratch_shapes=[pltpu.VMEM((NEAR, nodes), BF)],
        compiler_params=pltpu.CompilerParams(vmem_limit_bytes=BIG),
        cost_estimate=QUICK,
        name="unmix",
    )(probs, query, pair, pair, grad_mixed, grad_scaled, inner, inverse)


def return_kernel(
    place_ref, early_ref, query_in_a, query_in_b, pair_in_a, pair_in_b,
    grad_state_in, rows_in, normed_in, before_ref, sums_ref, after_ref, grad_dec_ref,
    keep_0, keep_1, send_0, send_1,
    early, normed_ref, rows_ref, grad_state_ref, query_g, pair_g, keep_ref, send_ref, sems,
):
    pairs = (
        (normed_in, normed_ref),
        (query_in_a, query_g.at[:, 0:128]), (query_in_b, query_g.at[:, 128:512]),
        (pair_in_a, pair_g.at[:, 0:256]), (pair_in_b, pair_g.at[:, 256:1024]),
        (early_ref, early), (rows_in, rows_ref), (grad_state_in, grad_state_ref),
    )
    copies = [pltpu.make_async_copy(source, there, sems.at[i]) for i, (source, there) in enumerate(pairs)]
    for copy in copies:
        copy.start()
    own_wide, own_narrow = place_ref[0], place_ref[1]
    def put(n, colour, column, value, low):
        lines = value.shape[0] // 8
        for side, out_ref in ((1, send_ref), (0, keep_ref)):

            @pl.when(((n ^ own_narrow) & 1) == side)
            def _():
                part = (n ^ own_narrow) >> 1
                for w in range(8):
                    out_ref[colour, block_at(DIMS[colour], part, w ^ own_wide), low : low + lines, column : column + 128] = value[
                        w * lines : (w + 1) * lines, :
                    ]

    copies[0].wait()
    turned = normed_ref[...].astype(F32).T.astype(BF)
    for copy in copies[1:5]:
        copy.wait()
    weight_query = mm(turned[:, 512:1024], query_g[...]).astype(BF)
    weight_pair = mm(turned, pair_g[...]).astype(BF)
    for n in range(GROUPS):
        put(n, 0, 0, weight_query[:, n * 128 : n * 128 + 128], 0)
        put(n, 0, 128, weight_pair[:, n * 256 : n * 256 + 128], 0)
        put(n, 1, 0, weight_pair[:, n * 256 + 128 : n * 256 + 256], 0)
    leaving = [
        pltpu.make_async_copy(send_ref.at[0], send_0, sems.at[10]),
        pltpu.make_async_copy(keep_ref.at[0], keep_0, sems.at[11]),
        pltpu.make_async_copy(send_ref.at[1], send_1, sems.at[12]),
        pltpu.make_async_copy(keep_ref.at[1], keep_1, sems.at[13]),
    ]
    leaving[0].start()
    leaving[1].start()
    for copy in copies[5:]:
        copy.wait()
    gain = dec_of(early).astype(F32).T[OUT : OUT + 1, :]
    pair_weights = pair_of(early)
    grad_enc = jnp.zeros((IN, D), F32)
    gain_grad = jnp.zeros((1, D), F32)
    for block, sums in enumerate((before_ref, sums_ref, after_ref)):
        at = block * 512
        grad_block = mm_nt(pair_g[at : at + 512, :], pair_weights)
        if block == 1:
            grad_block = grad_block + mm_nt(query_g[...], query_of(early))
        normal, inverse = norm_parts(rows_ref[at : at + 512, :])
        back, gain_part = norm_pull(grad_block, normal, inverse, gain)
        gain_grad = gain_grad + gain_part
        if block == 1:
            back = back + grad_state_ref[...]
        back_low = (back * (1.0 / KG)).astype(BF)
        grad_enc = grad_enc + mm(sums[...].astype(BF), back_low)
    grad_enc = grad_enc.astype(BF)
    rows = lax.broadcasted_iota(jnp.int32, (128, 1), 0)
    grad_dec = jnp.where(rows == OUT, gain_grad, grad_dec_ref[...]).T.astype(BF)
    for n in range(GROUPS):
        put(n, 1, 128, grad_enc[:, n * 128 : n * 128 + 128], 0)
        put(n, 1, 128, grad_dec[n * 128 : n * 128 + 128, :], 32)
        put(n, 1, 128, jnp.zeros((128, 128), BF), 48)
    leaving[2].start()
    leaving[3].start()
    for copy in leaving:
        copy.wait()


def give_back(place, early, first, second, grad_state, rows, normed, before, sums, after, grad_dec):
    vmem = pl.BlockSpec(memory_space=pltpu.VMEM)
    outside = pl.BlockSpec(memory_space=pltpu.HBM)
    return pl.pallas_call(
        return_kernel,
        in_specs=[pl.BlockSpec(memory_space=pltpu.SMEM), outside] + [outside] * 7 + [vmem] * 4,
        out_specs=[outside] * 4,
        out_shape=[jax.ShapeDtypeStruct((16, LINES, 256), BF)] * 4,
        scratch_shapes=[
            pltpu.VMEM((8, GROUPS, LINES, EARLY), BF),
            pltpu.VMEM((NEAR, D), BF),
            pltpu.VMEM((NEAR, D), BF),
            pltpu.VMEM((512, D), F32),
            pltpu.VMEM((512, D), BF),
            pltpu.VMEM((NEAR, 2 * D), BF),
            pltpu.VMEM((2, 16, LINES, 256), BF),
            pltpu.VMEM((2, 16, LINES, 256), BF),
            pltpu.SemaphoreType.DMA((14,)),
        ],
        compiler_params=pltpu.CompilerParams(vmem_limit_bytes=BIG),
        cost_estimate=QUICK,
        name="give_back",
    )(
        place, early, first[0], second[0], first[1], second[1],
        grad_state, rows, normed, before, sums, after, grad_dec,
    )


def adam_kernel(row_ref, early_ref, late_ref, *refs):
    total = row_ref[0:1, 2:3] * MB
    norm_value = jnp.sqrt(row_ref[0:1, 0:1]) / total
    factor = jnp.minimum(1.0, clip_norm / norm_value) / total
    lanes = lax.broadcasted_iota(jnp.int32, (8, 128), 1)
    refs[36][...] = jnp.where(lanes == 0, row_ref[0:1, 1:2] / total, norm_value)
    fix_one = 1.0 - beta_one**STEPS_DONE
    fix_two = 1.0 - beta_two**STEPS_DONE
    enc_rows, read_rows = refs[0].shape[0], refs[12].shape[0]
    shares = (
        ((early_ref, slice(0, enc_rows), slice(384, 512), slice(None)),),
        ((early_ref, slice(None), slice(0, 384), slice(0, 384)), (late_ref, slice(None), slice(0, 512), slice(384, 896))),
        ((late_ref, slice(None), slice(512, 1152), slice(None)),),
        ((early_ref, slice(enc_rows, enc_rows + read_rows), slice(384, 384 + OUT + 2), slice(None)),),
    )
    for i, pieces in enumerate(shares):
        weight_ref, moment_ref, second_ref, average_ref = refs[4 * i : 4 * i + 4]
        outs = refs[16 + 5 * i : 21 + 5 * i]
        for share_ref, rows, columns, there in pieces:
            grad = share_ref[rows, columns] * factor
            weight = weight_ref[:, there]
            moment = beta_one * moment_ref[:, there] + (1.0 - beta_one) * grad
            second = beta_two * second_ref[:, there] + (1.0 - beta_two) * grad * grad
            weight = weight - learn_rate * (
                moment / fix_one / (jnp.sqrt(second / fix_two) + epsilon) + weight_decay * weight
            )
            outs[0][:, there] = moment
            outs[1][:, there] = second
            outs[2][:, there] = weight
            outs[3][:, there] = average_decay * average_ref[:, there] + (1.0 - average_decay) * weight
            outs[4][:, there] = weight.astype(BF)


def adam(row, early, late, states):
    arrays = [array for state in states for array in state]
    shapes = []
    for state in states:
        shapes += [jax.ShapeDtypeStruct(state[0].shape, F32)] * 4 + [jax.ShapeDtypeStruct(state[0].shape, BF)]
    shapes.append(jax.ShapeDtypeStruct((8, 128), F32))
    vmem = pl.BlockSpec(memory_space=pltpu.VMEM)
    return pl.pallas_call(
        adam_kernel,
        in_specs=[vmem] * 19,
        out_specs=[vmem] * 21,
        out_shape=shapes,
        compiler_params=pltpu.CompilerParams(vmem_limit_bytes=16 * MIB),
        cost_estimate=QUICK,
        name="adam",
    )(row, early, late, *arrays)


def pack_kernel(encoder_in, up_in, down_in, readout_in, early_ref, late_ref, encoder_ref, up_ref, down_ref, readout_ref, sems):
    pairs = ((up_in, up_ref), (encoder_in, encoder_ref), (readout_in, readout_ref), (down_in, down_ref))
    copies = [pltpu.make_async_copy(source, there, sems.at[i]) for i, (source, there) in enumerate(pairs)]
    for copy in copies:
        copy.start()
    for copy in copies:
        copy.wait()
    enc_rows, read_rows = encoder_ref.shape[0], readout_ref.shape[0]
    early_ref[:, 0:384] = up_ref[:, 0:384].astype(BF)
    side = jnp.zeros((early_ref.shape[0] - enc_rows, 128), F32)
    early_ref[enc_rows:, 384:512] = side.astype(BF)
    early_ref[0:enc_rows, 384:512] = encoder_ref[...].astype(BF)
    early_ref[enc_rows : enc_rows + read_rows, 384 : 384 + OUT + 2] = readout_ref[...].astype(BF)
    late_ref[:, 0:512] = up_ref[:, 384:896].astype(BF)
    late_ref[:, 512:1152] = down_ref[...].astype(BF)


def pack(encoder, up_proj, down_turned, readout):
    lines = up_proj.shape[0]
    vmem = pl.BlockSpec(memory_space=pltpu.VMEM)
    outside = pl.BlockSpec(memory_space=pltpu.HBM)
    return pl.pallas_call(
        pack_kernel,
        in_specs=[outside] * 4,
        out_specs=[vmem] * 2,
        out_shape=(jax.ShapeDtypeStruct((lines, EARLY), BF), jax.ShapeDtypeStruct((lines, LATE), BF)),
        scratch_shapes=[pltpu.VMEM(array.shape, F32) for array in (encoder, up_proj, down_turned, readout)]
        + [pltpu.SemaphoreType.DMA((4,))],
        compiler_params=pltpu.CompilerParams(vmem_limit_bytes=BIG),
        cost_estimate=QUICK,
        name="pack",
    )(encoder, up_proj, down_turned, readout)


def to_lines(array, wide):
    if wide == 8:
        return array
    lines, width = array.shape[2:]
    return jnp.moveaxis(jnp.moveaxis(array, 1, 0).reshape(GROUPS, 8, LINES, width), 0, 1)


def side_to_lines(side, wide):
    if wide == 8:
        return side
    enc_rows, read_rows = IN // wide, D // (GROUPS * wide)
    enc = to_rows(side[:, :, :enc_rows], 32)
    read = to_rows(side[:, :, enc_rows : enc_rows + read_rows], 16)
    return jnp.concatenate([enc, read, jnp.zeros((8, GROUPS, 16, 128), side.dtype)], axis=2)


def to_rows(array, rows):
    return jnp.moveaxis(jnp.moveaxis(array, 1, 0).reshape(GROUPS, 8, rows, array.shape[3]), 0, 1)


def from_rows(array, wide):
    rows, width = array.shape[2:]
    return jnp.moveaxis(jnp.moveaxis(array, 1, 0).reshape(GROUPS, wide, 8 * rows // wide, width), 0, 1)


def early_from_lines(array, wide):
    if wide == 8:
        return array
    main = from_rows(array[..., :384], wide)
    enc = from_rows(array[:, :, :32, 384:], wide)
    read = from_rows(array[:, :, 32:48, 384:], wide)
    spare = main.shape[2] - enc.shape[2] - read.shape[2]
    side = jnp.concatenate([enc, read, jnp.zeros((wide, GROUPS, spare, 128), array.dtype)], axis=2)
    return jnp.concatenate([main, side], axis=3)


ORDERS = ((1, 2, 3, 4), (2, 3, 1, 4), (3, 1, 2, 4))
DIMS = ((1, 2, 3, 4), (2, 1, 3, 4))
CUTS = (640, 512)


def by_relative(array, dims):
    array = array.reshape(2, 2, 2, 2, 2, *array.shape[2:])
    axes = {4: 0, 3: 1, 2: 2, 1: 3}
    turned = jnp.transpose(array, (4, *(axes[bit] for bit in dims), 5, 6))
    turned = turned.reshape(4, 8, *turned.shape[5:])
    return [turned[i] for i in range(4)]


def gather_plain(early, late, wide):
    def gathered(array):
        full = lax.all_gather(array, ("wide", "narrow"), axis=0, tiled=False)
        return full.reshape(wide, GROUPS, *array.shape)

    full = gathered(early)
    full = jnp.concatenate([to_lines(full[..., :384], wide), side_to_lines(full[..., 384:], wide)], axis=3)
    first = by_relative(full, DIMS[0])
    full = to_lines(gathered(late), wide)
    second = [by_relative(part, DIMS[i]) for i, part in enumerate(jnp.split(full, [CUTS[0]], axis=3))]
    return first, sum(second, [])


def joined(array, other):
    return jnp.concatenate([array[None], other[None]], axis=0)


def swap(array, bit):
    count = lax.axis_size("wide") * lax.axis_size("narrow")
    return lax.ppermute(array, ("wide", "narrow"), [(i, i ^ (1 << bit)) for i in range(count)])


def cube(array):
    return array.reshape(2, 2, 2, 2, *array.shape[1:])


def flat(array):
    return array.reshape(8, *array.shape[3:])


def halve_kernel(groups, keep, *refs):
    count = len(groups)
    total = sum(groups)
    flat_refs, refs = refs[:total], refs[total:]
    outs, refs = refs[: count * (1 + keep)], refs[count * (1 + keep) :]
    flat_there, refs = refs[:total], refs[total:]
    held, (in_sems, out_sems) = refs[:-2], refs[-2:]
    starts = [sum(groups[:i]) for i in range(count)]
    order = [(i, side) for side in ((1, 0) if keep else (1,)) for i in range(count)]

    def fetch(i, side):
        half = held[i].shape[0]
        here = pl.ds(side * half, half)
        return [
            pltpu.make_async_copy(
                flat_refs[starts[i] + k].at[here],
                flat_there[starts[i] + k].at[here if keep else pl.ds(0, half)],
                in_sems.at[starts[i] + k, side],
            )
            for k in range(groups[i])
        ]

    def leave(i, side):
        at = i if side else count + i
        return pltpu.make_async_copy(held[at], outs[at], out_sems.at[at])

    fetches = {at: fetch(*at) for at in order}
    for at in order:
        for copy in fetches[at]:
            copy.start()
    for i, side in order:
        for copy in fetches[i, side]:
            copy.wait()
        half = held[i].shape[0]
        here = pl.ds(side * half if keep else 0, half)
        added = sum(ref[here].astype(F32) for ref in flat_there[starts[i] : starts[i] + groups[i]])
        at = i if side else count + i
        held[at][...] = added.astype(held[at].dtype)
        leave(i, side).start()
    for i, side in order:
        leave(i, side).wait()


def halve_far(lists, keep):
    groups = [len(arrays) for arrays in lists]
    sizes = [min(array.shape[0] for array in arrays) for arrays in lists]
    halves = [(size // 2, *arrays[0].shape[1:]) for size, arrays in zip(sizes, lists)]
    kinds = (BF, F32)[: 1 + keep]
    outside = pl.BlockSpec(memory_space=pltpu.HBM)
    there = [
        pltpu.VMEM((size if keep else size // 2, *array.shape[1:]), array.dtype)
        for size, arrays in zip(sizes, lists)
        for array in arrays
    ]
    outs = pl.pallas_call(
        functools.partial(halve_kernel, groups, keep),
        in_specs=[outside] * sum(groups),
        out_specs=[outside] * (len(kinds) * len(lists)),
        out_shape=[jax.ShapeDtypeStruct(shape, kind) for kind in kinds for shape in halves],
        scratch_shapes=there
        + [pltpu.VMEM(shape, kind) for kind in kinds for shape in halves]
        + [pltpu.SemaphoreType.DMA((sum(groups), 2)), pltpu.SemaphoreType.DMA((len(kinds) * len(lists),))],
        compiler_params=pltpu.CompilerParams(vmem_limit_bytes=BIG),
        cost_estimate=QUICK,
        name="halve_far",
    )(*(array for arrays in lists for array in arrays))
    return outs[: len(lists)], outs[len(lists) :]


def halve_near_kernel(joint, count, *refs):
    column = 0
    for i in range(count):
        first, second = refs[2 * i], refs[2 * i + 1]
        half, width = first.shape[0] // 2, first.shape[2]
        sent, kept = (refs[2 * count], refs[2 * count + 1]) if joint else refs[2 * count + 2 * i : 2 * count + 2 * i + 2]
        there = slice(column, column + width) if joint else slice(None)
        sent[:, :, there] = (first[half:].astype(F32) + second[half:].astype(F32)).astype(BF)
        kept[:, :, there] = first[:half].astype(F32) + second[:half].astype(F32)
        column += width


def halve_near(pairs, joint=False):
    count = len(pairs)
    vmem = pl.BlockSpec(memory_space=pltpu.VMEM)
    halves = [(pair[0].shape[0] // 2, *pair[0].shape[1:]) for pair in pairs]
    if joint:
        halves = [(*halves[0][:2], sum(shape[2] for shape in halves))]
    outs = pl.pallas_call(
        functools.partial(halve_near_kernel, joint, count),
        in_specs=[vmem] * (2 * count),
        out_specs=[vmem] * (2 * len(halves)),
        out_shape=[jax.ShapeDtypeStruct(shape, kind) for shape in halves for kind in (BF, F32)],
        compiler_params=pltpu.CompilerParams(vmem_limit_bytes=12 * MIB),
        cost_estimate=QUICK,
        name="halve_near",
    )(*(array for pair in pairs for array in pair))
    return outs[0::2], outs[1::2]


class Sums:
    def __init__(self, keep, send, orders):
        self.pairs = [(mine, swap(other, 0)) for mine, other in zip(keep, send)]
        self.orders = orders

    def far_step(self, phase, values):
        sent, kept = halve_far(self.pairs, keep=phase > 0)
        sent, values = lax.optimization_barrier((sent, values))
        came = [swap(out, order[phase]) for out, order in zip(sent, self.orders)]
        self.pairs = [(*(pair if phase == 0 else (kept[i],)), came[i]) for i, pair in enumerate(self.pairs)]
        return values

    def step(self, phase, values=(), **how):
        sent, kept = halve_near(self.pairs, **how)
        sent, values = lax.optimization_barrier((sent, values))
        self.pairs = [(mine, swap(out, order[phase])) for mine, out, order in zip(kept, sent, self.orders)]
        return values

    def came(self, values):
        others, values = lax.optimization_barrier(([other for _, other in self.pairs], values))
        self.pairs = [(mine, other) for (mine, _), other in zip(self.pairs, others)]
        return values


def shares_kernel(loss_ref, early_a, early_b, late_a, late_b, early_ref, late_ref, row_ref):
    early = early_a[0] + early_b[0].astype(F32)
    early_ref[...] = early
    late = late_a[0] + late_b[0].astype(F32)
    late_ref[...] = late
    total = jnp.sum(early * early) + jnp.sum(late * late)
    lanes = lax.broadcasted_iota(jnp.int32, (1, 128), 1)
    row_ref[...] = loss_ref[...] + jnp.where(lanes == 0, total, 0.0)


def shares(loss_part, early, late):
    lines = early[0].shape[1]
    vmem = pl.BlockSpec(memory_space=pltpu.VMEM)
    return pl.pallas_call(
        shares_kernel,
        in_specs=[vmem] * 5,
        out_specs=[vmem] * 3,
        out_shape=(
            jax.ShapeDtypeStruct((lines, EARLY), F32),
            jax.ShapeDtypeStruct((lines, LATE), F32),
            jax.ShapeDtypeStruct((1, 128), F32),
        ),
        compiler_params=pltpu.CompilerParams(vmem_limit_bytes=8 * MIB),
        cost_estimate=QUICK,
        name="shares",
    )(loss_part, *early, *late)


def in_order(keep, send, dims):
    both = jnp.stack([keep, send]).reshape(2, 2, 2, 2, 2, *keep.shape[1:])
    turned = jnp.transpose(both, (*(1 + dims.index(bit) for bit in (4, 3, 2, 1)), 0, 5, 6))
    return turned.reshape(8, 4, *keep.shape[1:])


def scatter_sum(blocks):
    return lax.psum_scatter(
        blocks.astype(F32).reshape(-1, blocks.shape[3]), ("wide", "narrow"), scatter_dimension=0, tiled=True
    )


def sum_all(row):
    count = lax.axis_size("wide") * lax.axis_size("narrow")
    bit = 0
    while 1 << bit < count:
        masks = (1, 2, 3) if bit == 1 else (1,)
        others = [lax.ppermute(row, ("wide", "narrow"), [(i, i ^ (mask << bit)) for i in range(count)]) for mask in masks]
        row = sum(others, row)
        bit += len(masks) // 2 + 1
    return row


def body(
    cond_fields,
    target,
    noise_draw,
    noise_sigma,
    grid_to_mesh,
    mesh_edges,
    mesh_to_grid,
    latitude_row,
    level_index,
    encoder,
    up_proj,
    down_proj,
    readout,
    encoder_moment,
    up_moment,
    down_moment,
    readout_moment,
    encoder_second,
    up_second,
    down_second,
    readout_second,
    encoder_average,
    up_average,
    down_average,
    readout_average,
):
    wide_index = lax.axis_index("wide")
    wide = lax.axis_size("wide")
    globe = lax.axis_index("narrow")
    nodes = mesh_edges.shape[0]
    pixels = cond_fields.shape[1]
    all_nodes = nodes * wide
    width = -(-pixels // 128) * 128

    own_place = [wide_index, globe] if wide == 8 else [0, 0]
    place = jnp.stack([*own_place, globe]).astype(jnp.int32)
    early, late = pack(encoder, up_proj, down_proj.T, readout)
    moving = wide == 8
    tie = lax.optimization_barrier
    if moving:
        early_4 = swap(early, 4)

    if moving:
        early_1 = joined(early, early_4)
        early_3 = swap(early_1, 3)
        early_1, target, noise_draw, noise_sigma = tie((early_1, target, noise_draw, noise_sigma))

    def own(array):
        return lax.dynamic_index_in_dim(jnp.transpose(array, (2, 0, 1)), globe, 1, keepdims=False)

    goal, noise = own(target), own(noise_draw)
    sigma = lax.dynamic_index_in_dim(noise_sigma, globe, 0, keepdims=False)
    square = sigma * sigma
    c_in = lax.rsqrt(square + 1.0)
    if moving:
        early_3, goal, noise = tie((early_3, goal, noise))
        both = joined(early_1, early_3)
        both, goal, noise = tie((both, goal, noise))
        early_2 = swap(both, 2)
    noisy = goal + sigma * noise
    if moving:
        noisy, late = tie((noisy, late))
        late_4 = swap(late, 4)
    grid = jnp.concatenate([own(cond_fields), (c_in * noisy).astype(BF)], axis=0)
    grid = jnp.pad(grid, ((0, 0), (0, width - pixels)))
    edges = mesh_edges.T
    slot_rows = jnp.where(edges >= 0, (edges - wide_index * nodes + nodes + all_nodes) % all_nodes, -1)
    across = jnp.pad(mesh_to_grid.T - wide_index * nodes, ((0, 0), (0, width - pixels)), constant_values=-1)

    def halo(sums):
        low = sums.astype(BF)
        ring = [(i, (i + 1) % wide) for i in range(wide)]
        return lax.ppermute(low, "wide", ring), lax.ppermute(low, "wide", [(j, i) for i, j in ring])

    if moving:
        sums = grid_sums(grid, grid_to_mesh.T - wide_index * pixels)
        before, after = halo(sums)
        early_2, sums = tie((early_2, sums))
        quad, late_1 = joined(both, early_2), joined(late, late_4)
        quad, late_1, slot_rows = tie((quad, late_1, slot_rows))
        early_0 = swap(quad, 1)
        late_3 = swap(late_1, 3)
        bias, pool, pull = counts(slot_rows, across)
        bias, late_3 = tie((bias, late_3))
        both = joined(late_1, late_3)
        parts = [both[..., : CUTS[0]], both[..., CUTS[0] :]]
        parts, early_0, before, after = tie((parts, early_0, before, after))
        got = [swap(parts[0], 2), swap(parts[1], 1)]
        halves = [flat(quad), flat(early_0)]
        gathered = halves + [swap(half, 0) for half in halves]
    else:
        gathered, late_full = gather_plain(early, late, wide)
        sums = grid_sums(grid, grid_to_mesh.T - wide_index * pixels)
        bias, pool, pull = counts(slot_rows, across)
        before, after = halo(sums)

    state0, rows, normed, early_full = encode(place, gathered, before, sums, after)
    if moving:
        got, normed = tie((got, normed))
        parts = [joined(part, one) for part, one in zip(parts, got)]
        parts, normed = tie((parts, normed))
        got = [swap(parts[0], 1), swap(parts[1], 2)]
        halves = [flat(part) for part in parts]
        others = [swap(half, 0) for half in halves]
    mixed, probs, query, pair, inverse = attend(normed, early_full, bias)
    if moving:
        mixed, got, others = tie((mixed, got, others))
        late_full = []
        for half, one, other in zip(halves, got, others):
            late_full += [half, flat(one), other, swap(flat(one), 0)]
    *blocks, grad_state, grad_mixed, grad_scaled, inner, grad_dec, loss_part = feed(
        place, noise_sigma,
        late_full, early_full, state0, mixed, pool, pull, inverse, noisy, goal, latitude_row[None, :], level_index[:, None],
    )
    keep_late, send_late = blocks[:3], blocks[3:]
    if moving:
        late_sum = Sums(keep_late, send_late, ORDERS)
    first_heads = unmix(0, 1, probs, query, pair, grad_mixed, grad_scaled, inner, inverse)
    if moving:
        query, first_heads = late_sum.far_step(0, (query, first_heads))
    last_heads = unmix(1, 3, probs, query, pair, grad_mixed, grad_scaled, inner, inverse)
    if moving:
        grad_state, last_heads = late_sum.far_step(1, (grad_state, last_heads))
    *blocks, = give_back(
        place, early_full, first_heads, last_heads, grad_state, rows, normed, before, sums, after, grad_dec
    )
    keep_early, send_early = blocks[:2], blocks[2:]
    if moving:
        keep_early, send_early = late_sum.came((keep_early, send_early))
        early_sum = Sums(keep_early, send_early, DIMS)
        late_sum.pairs = early_sum.step(0, late_sum.pairs)
        late_sum.step(2)
        late_sum.pairs = early_sum.step(1, late_sum.pairs)
        late_sum.step(3, joint=True)
        early_sum.step(2, joint=True)
        early_sum.step(3)
        share_early, share_late, row = shares(loss_part, early_sum.pairs[0], late_sum.pairs[0])
    else:
        late_lines = jnp.concatenate([in_order(keep_late[i], send_late[i], ORDERS[i]) for i in range(3)], axis=3)
        early_lines = jnp.concatenate([in_order(keep_early[i], send_early[i], DIMS[i]) for i in range(2)], axis=3)
        share_late = scatter_sum(from_rows(late_lines, wide))
        share_early = scatter_sum(early_from_lines(early_lines, wide))
        squares = jnp.sum(share_early * share_early) + jnp.sum(share_late * share_late)
        row = loss_part + jnp.where(lax.broadcasted_iota(jnp.int32, (1, 128), 1) == 0, squares, 0.0)
    row = sum_all(row)
    states = [
        (encoder, encoder_moment, encoder_second, encoder_average),
        (up_proj, up_moment, up_second, up_average),
        (down_proj.T, down_moment.T, down_second.T, down_average.T),
        (readout, readout_moment, readout_second, readout_average),
    ]
    news = list(adam(row, share_early, share_late, states))
    news[10:15] = [array.T for array in news[10:15]]
    return (news[20][0, 0], news[20][0, 1], *news[:20])


def solution(mesh):
    if mesh.shape["narrow"] != GROUPS or MB != GROUPS:
        raise ValueError("narrow size")
    by_pixel = P(None, "wide", None)
    pair = P("wide", "narrow")
    weights = (pair, pair, P("narrow", "wide"), P(("narrow", "wide"), None))
    placed = (by_pixel, by_pixel, by_pixel, P()) + (P("wide", None),) * 3 + (P("wide"), P()) + weights * 4
    given = (P(), P())
    for spec in weights:
        given = given + (spec,) * 5
    return jax.shard_map(body, mesh=mesh, in_specs=placed, out_specs=given, check_vma=False)
```

```python
import functools
import math

import jax
import jax.numpy as jnp
from jax import lax
from jax.experimental import pallas as pl
from jax.experimental.pallas import tpu as pltpu
from jax.sharding import PartitionSpec as P

D = 512
HEADS = 4
HEAD_DIM = 128
OUT = 84
IN = 256
LEVELS = 13
KM = 16
KG = 8
KD = 3
STEPS_DONE = 7
MB = 4
GROUPS = 4
HID = 512
ROWS = 8
LINES = 64
EARLY = 512
LATE = 1152
BAND = 256
WINDOW = 1280
NEAR = 1536

clip_norm = 0.001
beta_one = 0.9
beta_two = 0.999
epsilon = 1e-08
learn_rate = 0.04
weight_decay = 0.1
average_decay = 0.9

BF = jnp.bfloat16
F32 = jnp.float32
MIB = 1024 * 1024
QUICK = pl.CostEstimate(flops=1000, bytes_accessed=1000, transcendentals=0)
BIG = 60 * MIB


def mm(left, right):
    return jnp.dot(left, right, preferred_element_type=F32)


def mm_nt(left, right):
    return lax.dot_general(left, right, (((1,), (1,)), ((), ())), preferred_element_type=F32)


def mm_tn(left, right):
    return lax.dot_general(left, right, (((0,), (0,)), ((), ())), preferred_element_type=F32)


def split_two(value):
    high = value.astype(BF)
    return high, (value - high.astype(F32)).astype(BF)


def norm_parts(rows_low):
    values = rows_low.astype(F32)
    center = values - jnp.mean(values, axis=-1, keepdims=True)
    inverse = lax.rsqrt(jnp.mean(center * center, axis=-1, keepdims=True) + 1e-05)
    return center * inverse, inverse


def norm_pull(grad_out, normal, inverse, gain):
    scaled = grad_out * gain
    inner = (
        scaled
        - jnp.mean(scaled, axis=-1, keepdims=True)
        - normal * jnp.mean(scaled * normal, axis=-1, keepdims=True)
    )
    return inner * inverse, jnp.sum(grad_out * normal, axis=0, keepdims=True)


class Leaving:
    def __init__(self, sems):
        self.sems, self.copies = sems, []

    def __call__(self, source, there):
        self.copies.append(pltpu.make_async_copy(source, there, self.sems.at[len(self.copies)]))
        self.copies[-1].start()

    def wait(self):
        for copy in self.copies:
            copy.wait()


def sums_kernel(grid_ref, pixels_ref, sums_ref, count_ref):
    width, nodes = count_ref.shape
    step = 32
    picks = [jnp.broadcast_to(pixels_ref[k : k + 1, :], (step, nodes)) for k in range(KG)]
    rows = lax.broadcasted_iota(jnp.int32, (step, nodes), 0)

    def count(i, _):
        at = pl.multiple_of(i * step, step)
        total = jnp.zeros((step, nodes), F32)
        for pick in picks:
            total = total + jnp.where(pick - at == rows, 1.0, 0.0)
        count_ref[pl.ds(at, step), :] = total.astype(BF)
        return 0

    lax.fori_loop(0, width // step, count, 0)
    sums_ref[...] = mm(grid_ref[...], count_ref[...])


def grid_sums(grid, pixel_rows):
    nodes, width = pixel_rows.shape[1], grid.shape[1]
    return pl.pallas_call(
        sums_kernel,
        out_shape=jax.ShapeDtypeStruct((IN, nodes), F32),
        scratch_shapes=[pltpu.VMEM((width, nodes), BF)],
        compiler_params=pltpu.CompilerParams(vmem_limit_bytes=16 * 1024 * 1024),
        cost_estimate=QUICK,
        name="grid_sums",
    )(grid, pixel_rows)


def counts_kernel(slots_ref, across_ref, bias_out, pool_out, pull_out, bias_ref, pool_ref, pull_ref, sems):
    nodes, width = pull_ref.shape
    step = 64
    leave = Leaving(sems)
    across = across_ref[...]

    def count_across(i, _):
        at = pl.multiple_of(i * 128, 128)
        rows = lax.broadcasted_iota(jnp.int32, (128, width), 0) + at
        total = jnp.zeros((128, width), F32)
        for k in range(KD):
            total = total + jnp.where(across[k : k + 1, :] == rows, 1.0, 0.0)
        pull_ref[pl.ds(at, 128), :] = total.astype(BF)
        pool_ref[:, pl.ds(at, 128)] = total.T.astype(BF)
        return 0

    lax.fori_loop(0, nodes // 128, count_across, 0)
    leave(pool_ref, pool_out)
    leave(pull_ref, pull_out)
    for band in range(nodes // BAND):
        low = band * BAND
        picks = slots_ref[:, low : low + BAND] - low
        rows = lax.broadcasted_iota(jnp.int32, (step, BAND), 0)
        alike = jnp.zeros((KM, BAND), F32)
        for k in range(KM):
            alike = alike + jnp.where(picks == picks[k : k + 1, :], 1.0, 0.0)
        weight = jnp.log2(alike)

        def count_slots(i, _):
            at = pl.multiple_of(i * step, step)
            value = jnp.full((step, BAND), -1e30, F32)
            for k in range(KM):
                value = jnp.where(picks[k : k + 1, :] - at == rows, weight[k : k + 1, :], value)
            bias_ref[band, pl.ds(at, step), :] = value
            return 0

        for part in range(2):
            half = WINDOW // step // 2
            lax.fori_loop(part * half, (part + 1) * half, count_slots, 0)
            here = slice(part * half * step, (part + 1) * half * step)
            leave(bias_ref.at[band, here], bias_out.at[band, here])
    leave.wait()


def counts(slot_rows, across_rows):
    nodes, width = slot_rows.shape[1], across_rows.shape[1]
    shapes = (
        jax.ShapeDtypeStruct((nodes // BAND, WINDOW, BAND), F32),
        jax.ShapeDtypeStruct((width, nodes), BF),
        jax.ShapeDtypeStruct((nodes, width), BF),
    )
    return pl.pallas_call(
        counts_kernel,
        out_specs=[pl.BlockSpec(memory_space=pltpu.HBM)] * 3,
        out_shape=shapes,
        scratch_shapes=[pltpu.VMEM(shape.shape, shape.dtype) for shape in shapes] + [pltpu.SemaphoreType.DMA((6,))],
        compiler_params=pltpu.CompilerParams(vmem_limit_bytes=BIG),
        cost_estimate=QUICK,
        name="counts",
    )(slot_rows, across_rows)


def blocks_of(place_ref, dims, refs):
    own_wide, own_narrow = place_ref[0], place_ref[1]
    found = []
    for side in range(2):
        for j in range(16):
            bits = dict(zip(dims, ((j >> 3) & 1, (j >> 2) & 1, (j >> 1) & 1, j & 1)))
            wide = own_wide ^ (bits[4] * 4 + bits[3] * 2 + bits[2])
            narrow = own_narrow ^ (bits[1] * 2 + side)
            found.append((wide, narrow, refs[2 * side + (j >> 3)].at[j & 7]))
    return found


def block_at(dims, part, wide):
    bits = {1: part, 2: wide & 1, 3: (wide >> 1) & 1, 4: wide >> 2}
    return ((bits[dims[0]] * 2 + bits[dims[1]]) * 2 + bits[dims[2]]) * 2 + bits[dims[3]]


def fetch_early(place_ref, refs, early, sems):
    return [
        pltpu.make_async_copy(source, early.at[wide, narrow], sems.at[i])
        for i, (wide, narrow, source) in enumerate(blocks_of(place_ref, DIMS[0], refs))
    ]


def enc_of(early):
    return jnp.concatenate([early[:, n, 0:32, 384:512].reshape(IN, 128) for n in range(GROUPS)], axis=1)


def dec_of(early):
    return jnp.concatenate([early[:, n, 32:48, 384:512].reshape(128, 128) for n in range(GROUPS)], axis=0)


def query_of(early):
    return jnp.concatenate([early[:, n, :, 0:128].reshape(D, 128) for n in range(GROUPS)], axis=1)


def pair_of(early):
    return jnp.concatenate([early[:, n, :, 128:384].reshape(D, 256) for n in range(GROUPS)], axis=1)


def encode_kernel(
    place_ref, a_0, a_1, a_2, a_3, before_ref, sums_ref, after_ref,
    state_ref, rows_ref, normed_ref, early_ref,
    early, state, rows_all, normed_all, sems, out_sems,
):
    copies = fetch_early(place_ref, (a_0, a_1, a_2, a_3), early, sems)
    for copy in copies:
        copy.start()
    for copy in copies:
        copy.wait()
    leave = Leaving(out_sems)
    leave(early, early_ref)
    gain = dec_of(early).astype(F32).T[OUT : OUT + 1, :]
    enc = enc_of(early)
    for block, ref in enumerate((before_ref, sums_ref, after_ref)):
        here = slice(block * 512, block * 512 + 512)
        if block == 1:
            high, low = split_two(ref[...])
            embedded = (mm_tn(high, enc) + mm_tn(low, enc)) * (1.0 / KG)
            state[...] = embedded
            leave(state, state_ref)
        else:
            embedded = mm_tn(ref[...], enc) * (1.0 / KG)
        rows = embedded.astype(BF)
        rows_all[here, :] = rows
        leave(rows_all.at[here], rows_ref.at[here])
        normal, _inverse = norm_parts(rows)
        normed_all[here, :] = (normal * gain).astype(BF)
        leave(normed_all.at[here], normed_ref.at[here])
    leave.wait()


def encode(place, gathered, before, sums, after):
    nodes = sums.shape[1]
    vmem = pl.BlockSpec(memory_space=pltpu.VMEM)
    outside = pl.BlockSpec(memory_space=pltpu.HBM)
    shapes = (
        jax.ShapeDtypeStruct((nodes, D), F32),
        jax.ShapeDtypeStruct((NEAR, D), BF),
        jax.ShapeDtypeStruct((NEAR, D), BF),
        jax.ShapeDtypeStruct((8, GROUPS, LINES, EARLY), BF),
    )
    return pl.pallas_call(
        encode_kernel,
        in_specs=[pl.BlockSpec(memory_space=pltpu.SMEM)] + [outside] * 4 + [vmem] * 3,
        out_specs=[outside] * 4,
        out_shape=shapes,
        scratch_shapes=[pltpu.VMEM((8, GROUPS, LINES, EARLY), BF)]
        + [pltpu.VMEM(shape.shape, shape.dtype) for shape in shapes[:3]]
        + [pltpu.SemaphoreType.DMA((32,)), pltpu.SemaphoreType.DMA((8,))],
        compiler_params=pltpu.CompilerParams(vmem_limit_bytes=BIG),
        cost_estimate=QUICK,
        name="encode",
    )(place, *gathered, before, sums, after)


def attend_kernel(
    normed_in, early_in, bias_in, mixed_ref, probs_ref, query_ref, pair_ref, inverse_ref,
    normed, early, bias, query_all, pair_all, mixed_all, probs, inverse_all, sems, out_sems,
):
    def weight_copy(h):
        return pltpu.make_async_copy(early_in.at[:, h, :, 0:384], early.at[h], sems.at[h])

    normed_copy = pltpu.make_async_copy(normed_in, normed, sems.at[4])
    bias_copies = [pltpu.make_async_copy(bias_in.at[i], bias.at[i], sems.at[5 + i]) for i in range(2)]
    weight_copy(0).start()
    normed_copy.start()
    bias_copies[0].start()
    bias_copies[1].start()
    for h in range(1, HEADS):
        weight_copy(h).start()
    normed_copy.wait()
    factor = HEAD_DIM ** (-0.5) * math.log2(math.e)

    def pair_leave(h):
        return pltpu.make_async_copy(pair_all.at[h], pair_ref.at[h], out_sems.at[8 + h])

    def probs_leave(h):
        return pltpu.make_async_copy(probs.at[h], probs_ref.at[h], out_sems.at[4 + h])

    for h in range(HEADS):
        lanes = slice(h * HEAD_DIM, h * HEAD_DIM + HEAD_DIM)
        weight_copy(h).wait()
        weights = early[h].reshape(D, 384)
        pair_all[h] = mm(normed[...], weights[:, 128:384]).astype(BF)
        query_all[:, lanes] = mm(normed[512:1024, :], weights[:, 0:128]).astype(BF)
        if h == 0:
            bias_copies[0].wait()
            bias_copies[1].wait()
        for band in range(2):
            at = band * BAND
            near, here = slice(at, at + WINDOW), slice(at, at + BAND)
            part = mm_nt(pair_all[h, near, :HEAD_DIM], query_all[here, lanes]) * factor + bias[band]
            expo = jnp.exp2(part - jnp.max(part, axis=0, keepdims=True))
            inverse = 1.0 / jnp.sum(expo, axis=0, keepdims=True)
            low = expo.astype(BF)
            probs[h, near, here] = low
            inverse_all[h : h + 1, here] = inverse
            column = jnp.broadcast_to(inverse, (8, BAND)).T[:, 0:1]
            mixed_all[here, lanes] = mm_tn(low, pair_all[h, near, HEAD_DIM:]) * column
        probs_leave(h).start()
        pair_leave(h).start()
    inverse_all[HEADS:8, :] = jnp.zeros((8 - HEADS, inverse_all.shape[1]), F32)
    leave = Leaving(out_sems)
    leave(mixed_all, mixed_ref)
    leave(query_all, query_ref)
    leave(inverse_all, inverse_ref)
    leave.wait()
    for h in range(HEADS):
        pair_leave(h).wait()
        probs_leave(h).wait()


def attend(normed, early, bias):
    nodes = normed.shape[0] // 3
    outside = pl.BlockSpec(memory_space=pltpu.HBM)
    return pl.pallas_call(
        attend_kernel,
        in_specs=[outside] * 3,
        out_specs=[outside] * 5,
        out_shape=(
            jax.ShapeDtypeStruct((nodes, D), F32),
            jax.ShapeDtypeStruct((HEADS, NEAR, nodes), BF),
            jax.ShapeDtypeStruct((nodes, D), BF),
            jax.ShapeDtypeStruct((HEADS, NEAR, 2 * HEAD_DIM), BF),
            jax.ShapeDtypeStruct((8, nodes), F32),
        ),
        scratch_shapes=[
            pltpu.VMEM((NEAR, D), BF),
            pltpu.VMEM((GROUPS, 8, LINES, 384), BF),
            pltpu.VMEM((2, WINDOW, BAND), F32),
            pltpu.VMEM((nodes, D), BF),
            pltpu.VMEM((HEADS, NEAR, 2 * HEAD_DIM), BF),
            pltpu.VMEM((nodes, D), F32),
            pltpu.VMEM((HEADS, NEAR, nodes), BF),
            pltpu.VMEM((8, nodes), F32),
            pltpu.SemaphoreType.DMA((7,)),
            pltpu.SemaphoreType.DMA((12,)),
        ],
        compiler_params=pltpu.CompilerParams(vmem_limit_bytes=BIG),
        cost_estimate=QUICK,
        name="attend",
    )(normed, early, bias)


def feed_kernel(
    place_ref, sigma_ref, a_0, a_1, a_2, a_3, b_0, b_1, b_2, b_3, early_ref, state_in, mixed_in, pool_in, pull_in, inverse_ref, noisy_ref, target_ref, lat_ref, level_ref,
    keep_0, keep_1, keep_2, send_0, send_1, send_2, grad_state_out, grad_mixed_out, grad_scaled_out, inner_ref, grad_dec_ref, loss_ref,
    late, dec, pre_ref, act_ref, grad_pred_ref,
    state_ref, mixed_ref, pool_ref, pull_ref, keep_ref, send_ref, grad_state_ref, grad_mixed_ref, grad_scaled_ref, sems, group_sems, out_sems,
):
    own_wide, own_narrow = place_ref[0], place_ref[1]

    refs = (a_0, a_1, a_2, a_3), (b_0, b_1, b_2, b_3)

    def fetch(colour, columns, first, sem):
        there = slice(first, first + columns.stop - columns.start)
        return [
            pltpu.make_async_copy(source.at[:, columns], late.at[wide, narrow, :, there], sem(narrow, i))
            for i, (wide, narrow, source) in enumerate(blocks_of(place_ref, DIMS[colour], refs[colour]))
        ]

    def group(n, columns, row):
        return pltpu.make_async_copy(late.at[:, n, :, columns], late.at[:, n, :, columns], group_sems.at[row, n])

    hidden, outer, lower = slice(0, 512), slice(512, 640), slice(640, 1152)
    pairs = [(state_in, state_ref), (mixed_in, mixed_ref), (early_ref.at[:, :, 32:48, 384:512], dec)]
    small = [pltpu.make_async_copy(source, there, sems.at[32 + i]) for i, (source, there) in enumerate(pairs)]
    small += fetch(0, outer, 512, lambda n, i: sems.at[i])
    pool_copy = pltpu.make_async_copy(pool_in, pool_ref, sems.at[35])
    pull_copy = pltpu.make_async_copy(pull_in, pull_ref, sems.at[36])
    first = fetch(0, hidden, 0, lambda n, i: group_sems.at[0, n])
    second = fetch(1, slice(0, 512), 640, lambda n, i: group_sems.at[1, n])
    for copy in (*small, *first, *second, pool_copy, pull_copy):
        copy.start()
    for copy in small:
        copy.wait()
    dec_turned = jnp.concatenate([dec[:, n].reshape(128, 128) for n in range(GROUPS)], axis=0).astype(F32).T
    gain = dec_turned[OUT + 1 : OUT + 2, :]
    rows = lax.broadcasted_iota(jnp.int32, (128, 1), 0)
    dec_only = jnp.where(rows < OUT, dec_turned, 0.0).astype(BF)
    out_full = jnp.concatenate([late[:, n, :, 512:640].reshape(D, 128) for n in range(GROUPS)], axis=1)
    mixed = mixed_ref[...].astype(BF)
    state1 = state_ref[...] + mm_nt(mixed, out_full)
    normal, inverse = norm_parts(state1.astype(BF))
    normed = (normal * gain).astype(BF)

    def forward(i, state):
        n = i ^ own_narrow
        group(n, hidden, 0).wait()
        pre = mm(normed, late[:, n, :, 0:512].reshape(D, HID))
        pre_ref[n] = pre
        act = (pre / (1.0 + jnp.exp(-pre))).astype(BF)
        act_ref[n] = act
        group(n, lower, 1).wait()
        return state + mm_nt(act, late[:, n, :, 640:1152].reshape(D, HID))

    state2 = state1
    for i in range(GROUPS):
        state2 = forward(i, state2)
    high, low = split_two(state2)
    pool_copy.wait()
    pull_copy.wait()
    pool = pool_ref[...]
    pooled = ((mm(pool, high) + mm(pool, low)) / KD).astype(BF)
    pixels = noisy_ref.shape[1]
    pred = mm_nt(dec_only, pooled)[:OUT, :pixels]
    sigma = jnp.full((1, 1), sigma_ref[place_ref[2]], F32)
    square = sigma * sigma
    c_skip = 1.0 / (square + 1.0)
    c_out = sigma * lax.rsqrt(square + 1.0)
    lam = (square + 1.0) / square
    error = c_skip * noisy_ref[...] + c_out * pred - target_ref[...]
    weight = jnp.cos((lat_ref[...].astype(F32) - 90.0) * (math.pi / 180.0)) * ((level_ref[...].astype(F32) + 1.0) / LEVELS)
    weighted = lam * weight
    first_globe = (jnp.full((1, 1), place_ref[2], jnp.int32) == 0).astype(F32)
    lanes = lax.broadcasted_iota(jnp.int32, (1, 128), 1)
    loss_ref[...] = jnp.where(lanes == 1, jnp.sum(weighted * error * error), 0.0) + jnp.where(
        lanes == 2, jnp.sum(weight) * first_globe, 0.0
    )
    grad_pred_ref[...] = jnp.zeros_like(grad_pred_ref)
    grad_pred_ref[:OUT, :pixels] = 2.0 * c_out * weighted * error
    grad_pred = grad_pred_ref[...].astype(BF)
    grad_dec_ref[...] = mm(grad_pred, pooled)
    up_high, up_low = split_two(mm_nt(pull_ref[...], grad_pred))
    grad_state2 = (mm(up_high, dec_only) + mm(up_low, dec_only)) / KD
    grad_low = grad_state2.astype(BF)
    grad_turned = grad_state2.T.astype(BF)
    normed_turned = normed.astype(F32).T.astype(BF)

    def put(out_ref, side, part, first, value):
        done = 0
        while done < value.shape[1]:
            colour, column = divmod(first + done, 384)
            count = min(384 - column, value.shape[1] - done)
            for w in range(8):
                out_ref[colour, block_at(ORDERS[colour], part, w ^ own_wide), :, column : column + count] = value[
                    w * LINES : (w + 1) * LINES, done : done + count
                ]
            done += count

    def backward(part, grad_n, out_ref, side):
        n = (part * 2 + side) ^ own_narrow
        act = act_ref[n]
        pre = pre_ref[n]
        put(out_ref, side, part, 640, mm(grad_turned, act).astype(BF))
        grad_act = mm(grad_low, late[:, n, :, 640:1152].reshape(D, HID))
        logistic = 1.0 / (1.0 + jnp.exp(-pre))
        grad_pre = (grad_act * logistic * (1.0 + pre * (1.0 - logistic))).astype(BF)
        put(out_ref, side, part, 0, mm(normed_turned, grad_pre).astype(BF))
        return grad_n + mm_nt(grad_pre, late[:, n, :, 0:512].reshape(D, HID))

    grad_n = jnp.zeros((D, D), F32)
    leaving = []

    def leave(source, there):
        leaving.append(pltpu.make_async_copy(source, there, out_sems.at[len(leaving)]))
        leaving[-1].start()

    sides = ((1, send_ref, (send_0, send_1, send_2)), (0, keep_ref, (keep_0, keep_1, keep_2)))
    for side, out_ref, there in sides:
        for part in range(2):
            grad_n = backward(part, grad_n, out_ref, side)
        leave(out_ref.at[0], there[0])
        leave(out_ref.at[2], there[2])
    back, gain_grad = norm_pull(grad_n, normal, inverse, gain)
    grad_dec_ref[OUT + 1 : OUT + 2, :] = gain_grad
    grad_state1 = grad_state2 + back
    grad_state_ref[...] = grad_state1
    leave(grad_state_ref, grad_state_out)
    grad_low1 = grad_state1.astype(BF)
    act_ref[0] = mixed
    grad_turned1 = grad_state1.T.astype(BF)
    for side, out_ref, there in sides:
        for part in range(2):
            lane = pl.multiple_of(((part * 2 + side) ^ own_narrow) * 128, 128)
            put(out_ref, side, part, 512, mm(grad_turned1, act_ref[0, :, pl.ds(lane, 128)]).astype(BF))
        leave(out_ref.at[1], there[1])
    grad_mixed = mm(grad_low1, out_full)
    grad_mixed_ref[...] = grad_mixed.astype(BF)
    leave(grad_mixed_ref, grad_mixed_out)
    columns = inverse_ref[...].T
    lanes = lax.broadcasted_iota(jnp.int32, (1, 128), 1)
    inner = jnp.zeros((grad_mixed.shape[0], 128), F32)
    for h in range(HEADS):
        here = slice(h * HEAD_DIM, h * HEAD_DIM + HEAD_DIM)
        grad = grad_mixed[:, here]
        grad_scaled_ref[:, here] = (grad * columns[:, h : h + 1]).astype(BF)
        inner = jnp.where(lanes == h, jnp.sum(grad * mixed_ref[:, here], axis=1, keepdims=True), inner)
    leave(grad_scaled_ref, grad_scaled_out)
    inner_ref[...] = inner.T[0:8, :]
    for copy in leaving:
        copy.wait()


def feed(place, sigma, late, early, state0, mixed, pool, pull, inverse, noisy, target, lat, level):
    nodes = state0.shape[0]
    width = pool.shape[0]
    vmem = pl.BlockSpec(memory_space=pltpu.VMEM)
    outside = pl.BlockSpec(memory_space=pltpu.HBM)
    return pl.pallas_call(
        feed_kernel,
        in_specs=[pl.BlockSpec(memory_space=pltpu.SMEM)] * 2 + [outside] * 13 + [vmem] * 5,
        out_specs=[outside] * 9 + [vmem] * 3,
        out_shape=(
            *([jax.ShapeDtypeStruct((16, LINES, 384), BF)] * 6),
            jax.ShapeDtypeStruct((nodes, D), F32),
            jax.ShapeDtypeStruct((nodes, D), BF),
            jax.ShapeDtypeStruct((nodes, D), BF),
            jax.ShapeDtypeStruct((8, nodes), F32),
            jax.ShapeDtypeStruct((128, D), F32),
            jax.ShapeDtypeStruct((1, 128), F32),
        ),
        scratch_shapes=[
            pltpu.VMEM((8, GROUPS, LINES, LATE), BF),
            pltpu.VMEM((8, GROUPS, 16, 128), BF),
            pltpu.VMEM((GROUPS, nodes, HID), F32),
            pltpu.VMEM((GROUPS, nodes, HID), BF),
            pltpu.VMEM((128, width), F32),
            pltpu.VMEM((nodes, D), F32),
            pltpu.VMEM((nodes, D), F32),
            pltpu.VMEM((width, nodes), BF),
            pltpu.VMEM((nodes, width), BF),
            pltpu.VMEM((3, 16, LINES, 384), BF),
            pltpu.VMEM((3, 16, LINES, 384), BF),
            pltpu.VMEM((nodes, D), F32),
            pltpu.VMEM((nodes, D), BF),
            pltpu.VMEM((nodes, D), BF),
            pltpu.SemaphoreType.DMA((37,)),
            pltpu.SemaphoreType.DMA((2, GROUPS)),
            pltpu.SemaphoreType.DMA((9,)),
        ],
        compiler_params=pltpu.CompilerParams(vmem_limit_bytes=BIG),
        cost_estimate=QUICK,
        name="feed",
    )(place, sigma, *late, early, state0, mixed, pool, pull, inverse, noisy, target, lat, level)


def unmix_kernel(first, probs_ref, query_ref, keys_ref, values_ref, grad_mixed_ref, grad_scaled_ref, inner_ref, inverse_ref,
                 grad_query_ref, grad_pair_ref, grad_scores):
    scale = HEAD_DIM ** (-0.5)
    row = pl.ds(first + pl.program_id(0), 1)
    inner = inner_ref[row, :]
    factor = inverse_ref[row, :] * scale
    pieces = ((0, 256, 0, 256), (256, 768, 0, 512), (768, 1280, 0, 512), (1280, 1536, 256, 512))
    for low_row, high_row, low_column, high_column in pieces:
        rows, columns = slice(low_row, high_row), slice(low_column, high_column)
        probs = probs_ref[0, rows, columns]
        grad_probs = mm_nt(values_ref[0, rows, :], grad_mixed_ref[columns, :])
        low = (probs.astype(F32) * ((grad_probs - inner[:, columns]) * factor[:, columns])).astype(BF)
        grad_scores[rows, columns] = low
        grad_pair_ref[rows, 0:HEAD_DIM] = mm(low, query_ref[columns, :]).astype(BF)
        grad_pair_ref[rows, HEAD_DIM : 2 * HEAD_DIM] = mm(probs, grad_scaled_ref[columns, :]).astype(BF)
    for at in (0, BAND):
        grad_query_ref[at : at + BAND, :] = mm_tn(
            grad_scores[at : at + WINDOW, at : at + BAND], keys_ref[0, at : at + WINDOW, :]
        ).astype(BF)


def unmix(first, heads, probs, query, pair, grad_mixed, grad_scaled, inner, inverse):
    nodes = query.shape[0]
    part = pl.BlockSpec((nodes, HEAD_DIM), lambda i: (0, first + i))
    whole = pl.BlockSpec((8, nodes), lambda i: (0, 0))
    return pl.pallas_call(
        functools.partial(unmix_kernel, first),
        grid=(heads,),
        in_specs=[
            pl.BlockSpec((1, NEAR, nodes), lambda i: (first + i, 0, 0)),
            part,
            pl.BlockSpec((1, NEAR, HEAD_DIM), lambda i: (first + i, 0, 0)),
            pl.BlockSpec((1, NEAR, HEAD_DIM), lambda i: (first + i, 0, 1)),
            part,
            part,
            whole,
            whole,
        ],
        out_specs=(
            pl.BlockSpec((nodes, HEAD_DIM), lambda i: (0, i)),
            pl.BlockSpec((NEAR, 2 * HEAD_DIM), lambda i: (0, i)),
        ),
        out_shape=(
            jax.ShapeDtypeStruct((nodes, heads * HEAD_DIM), BF),
            jax.ShapeDtypeStruct((NEAR, heads * 2 * HEAD_DIM), BF),
        ),
        scratch_shapes=[pltpu.VMEM((NEAR, nodes), BF)],
        compiler_params=pltpu.CompilerParams(vmem_limit_bytes=BIG),
        cost_estimate=QUICK,
        name="unmix",
    )(probs, query, pair, pair, grad_mixed, grad_scaled, inner, inverse)


def return_kernel(
    place_ref, early_ref, query_in_a, query_in_b, pair_in_a, pair_in_b,
    grad_state_in, rows_in, normed_in, before_ref, sums_ref, after_ref, grad_dec_ref,
    keep_0, keep_1, send_0, send_1,
    early, normed_ref, rows_ref, grad_state_ref, query_g, pair_g, keep_ref, send_ref, sems,
):
    pairs = (
        (normed_in, normed_ref),
        (query_in_a, query_g.at[:, 0:128]), (query_in_b, query_g.at[:, 128:512]),
        (pair_in_a, pair_g.at[:, 0:256]), (pair_in_b, pair_g.at[:, 256:1024]),
        (early_ref, early), (rows_in, rows_ref), (grad_state_in, grad_state_ref),
    )
    copies = [pltpu.make_async_copy(source, there, sems.at[i]) for i, (source, there) in enumerate(pairs)]
    for copy in copies:
        copy.start()
    own_wide, own_narrow = place_ref[0], place_ref[1]
    def put(n, colour, column, value, low):
        lines = value.shape[0] // 8
        for side, out_ref in ((1, send_ref), (0, keep_ref)):

            @pl.when(((n ^ own_narrow) & 1) == side)
            def _():
                part = (n ^ own_narrow) >> 1
                for w in range(8):
                    out_ref[colour, block_at(DIMS[colour], part, w ^ own_wide), low : low + lines, column : column + 128] = value[
                        w * lines : (w + 1) * lines, :
                    ]

    copies[0].wait()
    turned = normed_ref[...].astype(F32).T.astype(BF)
    for copy in copies[1:5]:
        copy.wait()
    weight_query = mm(turned[:, 512:1024], query_g[...]).astype(BF)
    weight_pair = mm(turned, pair_g[...]).astype(BF)
    for n in range(GROUPS):
        put(n, 0, 0, weight_query[:, n * 128 : n * 128 + 128], 0)
        put(n, 0, 128, weight_pair[:, n * 256 : n * 256 + 128], 0)
        put(n, 1, 0, weight_pair[:, n * 256 + 128 : n * 256 + 256], 0)
    leaving = [
        pltpu.make_async_copy(send_ref.at[0], send_0, sems.at[10]),
        pltpu.make_async_copy(keep_ref.at[0], keep_0, sems.at[11]),
        pltpu.make_async_copy(send_ref.at[1], send_1, sems.at[12]),
        pltpu.make_async_copy(keep_ref.at[1], keep_1, sems.at[13]),
    ]
    leaving[0].start()
    leaving[1].start()
    for copy in copies[5:]:
        copy.wait()
    gain = dec_of(early).astype(F32).T[OUT : OUT + 1, :]
    pair_weights = pair_of(early)
    grad_enc = jnp.zeros((IN, D), F32)
    gain_grad = jnp.zeros((1, D), F32)
    for block, sums in enumerate((before_ref, sums_ref, after_ref)):
        at = block * 512
        grad_block = mm_nt(pair_g[at : at + 512, :], pair_weights)
        if block == 1:
            grad_block = grad_block + mm_nt(query_g[...], query_of(early))
        normal, inverse = norm_parts(rows_ref[at : at + 512, :])
        back, gain_part = norm_pull(grad_block, normal, inverse, gain)
        gain_grad = gain_grad + gain_part
        if block == 1:
            back = back + grad_state_ref[...]
        back_low = (back * (1.0 / KG)).astype(BF)
        grad_enc = grad_enc + mm(sums[...].astype(BF), back_low)
    grad_enc = grad_enc.astype(BF)
    rows = lax.broadcasted_iota(jnp.int32, (128, 1), 0)
    grad_dec = jnp.where(rows == OUT, gain_grad, grad_dec_ref[...]).T.astype(BF)
    for n in range(GROUPS):
        put(n, 1, 128, grad_enc[:, n * 128 : n * 128 + 128], 0)
        put(n, 1, 128, grad_dec[n * 128 : n * 128 + 128, :], 32)
        put(n, 1, 128, jnp.zeros((128, 128), BF), 48)
    leaving[2].start()
    leaving[3].start()
    for copy in leaving:
        copy.wait()


def give_back(place, early, first, second, grad_state, rows, normed, before, sums, after, grad_dec):
    vmem = pl.BlockSpec(memory_space=pltpu.VMEM)
    outside = pl.BlockSpec(memory_space=pltpu.HBM)
    return pl.pallas_call(
        return_kernel,
        in_specs=[pl.BlockSpec(memory_space=pltpu.SMEM), outside] + [outside] * 7 + [vmem] * 4,
        out_specs=[outside] * 4,
        out_shape=[jax.ShapeDtypeStruct((16, LINES, 256), BF)] * 4,
        scratch_shapes=[
            pltpu.VMEM((8, GROUPS, LINES, EARLY), BF),
            pltpu.VMEM((NEAR, D), BF),
            pltpu.VMEM((NEAR, D), BF),
            pltpu.VMEM((512, D), F32),
            pltpu.VMEM((512, D), BF),
            pltpu.VMEM((NEAR, 2 * D), BF),
            pltpu.VMEM((2, 16, LINES, 256), BF),
            pltpu.VMEM((2, 16, LINES, 256), BF),
            pltpu.SemaphoreType.DMA((14,)),
        ],
        compiler_params=pltpu.CompilerParams(vmem_limit_bytes=BIG),
        cost_estimate=QUICK,
        name="give_back",
    )(
        place, early, first[0], second[0], first[1], second[1],
        grad_state, rows, normed, before, sums, after, grad_dec,
    )


def adam_kernel(row_ref, early_ref, late_ref, *refs):
    total = row_ref[0:1, 2:3] * MB
    norm_value = jnp.sqrt(row_ref[0:1, 0:1]) / total
    factor = jnp.minimum(1.0, clip_norm / norm_value) / total
    lanes = lax.broadcasted_iota(jnp.int32, (8, 128), 1)
    refs[36][...] = jnp.where(lanes == 0, row_ref[0:1, 1:2] / total, norm_value)
    fix_one = 1.0 - beta_one**STEPS_DONE
    fix_two = 1.0 - beta_two**STEPS_DONE
    enc_rows, read_rows = refs[0].shape[0], refs[12].shape[0]
    shares = (
        ((early_ref, slice(0, enc_rows), slice(384, 512), slice(None)),),
        ((early_ref, slice(None), slice(0, 384), slice(0, 384)), (late_ref, slice(None), slice(0, 512), slice(384, 896))),
        ((late_ref, slice(None), slice(512, 1152), slice(None)),),
        ((early_ref, slice(enc_rows, enc_rows + read_rows), slice(384, 384 + OUT + 2), slice(None)),),
    )
    for i, pieces in enumerate(shares):
        weight_ref, moment_ref, second_ref, average_ref = refs[4 * i : 4 * i + 4]
        outs = refs[16 + 5 * i : 21 + 5 * i]
        for share_ref, rows, columns, there in pieces:
            grad = share_ref[rows, columns] * factor
            weight = weight_ref[:, there]
            moment = beta_one * moment_ref[:, there] + (1.0 - beta_one) * grad
            second = beta_two * second_ref[:, there] + (1.0 - beta_two) * grad * grad
            weight = weight - learn_rate * (
                moment / fix_one / (jnp.sqrt(second / fix_two) + epsilon) + weight_decay * weight
            )
            outs[0][:, there] = moment
            outs[1][:, there] = second
            outs[2][:, there] = weight
            outs[3][:, there] = average_decay * average_ref[:, there] + (1.0 - average_decay) * weight
            outs[4][:, there] = weight.astype(BF)


def adam(row, early, late, states):
    arrays = [array for state in states for array in state]
    shapes = []
    for state in states:
        shapes += [jax.ShapeDtypeStruct(state[0].shape, F32)] * 4 + [jax.ShapeDtypeStruct(state[0].shape, BF)]
    shapes.append(jax.ShapeDtypeStruct((8, 128), F32))
    vmem = pl.BlockSpec(memory_space=pltpu.VMEM)
    return pl.pallas_call(
        adam_kernel,
        in_specs=[vmem] * 19,
        out_specs=[vmem] * 21,
        out_shape=shapes,
        compiler_params=pltpu.CompilerParams(vmem_limit_bytes=16 * MIB),
        cost_estimate=QUICK,
        name="adam",
    )(row, early, late, *arrays)


def pack_kernel(encoder_in, up_in, down_in, readout_in, early_ref, late_ref, encoder_ref, up_ref, down_ref, readout_ref, sems):
    pairs = ((up_in, up_ref), (encoder_in, encoder_ref), (readout_in, readout_ref), (down_in, down_ref))
    copies = [pltpu.make_async_copy(source, there, sems.at[i]) for i, (source, there) in enumerate(pairs)]
    for copy in copies:
        copy.start()
    for copy in copies:
        copy.wait()
    enc_rows, read_rows = encoder_ref.shape[0], readout_ref.shape[0]
    early_ref[:, 0:384] = up_ref[:, 0:384].astype(BF)
    side = jnp.zeros((early_ref.shape[0] - enc_rows, 128), F32)
    early_ref[enc_rows:, 384:512] = side.astype(BF)
    early_ref[0:enc_rows, 384:512] = encoder_ref[...].astype(BF)
    early_ref[enc_rows : enc_rows + read_rows, 384 : 384 + OUT + 2] = readout_ref[...].astype(BF)
    late_ref[:, 0:512] = up_ref[:, 384:896].astype(BF)
    late_ref[:, 512:1152] = down_ref[...].astype(BF)


def pack(encoder, up_proj, down_turned, readout):
    lines = up_proj.shape[0]
    vmem = pl.BlockSpec(memory_space=pltpu.VMEM)
    outside = pl.BlockSpec(memory_space=pltpu.HBM)
    return pl.pallas_call(
        pack_kernel,
        in_specs=[outside] * 4,
        out_specs=[vmem] * 2,
        out_shape=(jax.ShapeDtypeStruct((lines, EARLY), BF), jax.ShapeDtypeStruct((lines, LATE), BF)),
        scratch_shapes=[pltpu.VMEM(array.shape, F32) for array in (encoder, up_proj, down_turned, readout)]
        + [pltpu.SemaphoreType.DMA((4,))],
        compiler_params=pltpu.CompilerParams(vmem_limit_bytes=BIG),
        cost_estimate=QUICK,
        name="pack",
    )(encoder, up_proj, down_turned, readout)


def to_lines(array, wide):
    if wide == 8:
        return array
    lines, width = array.shape[2:]
    return jnp.moveaxis(jnp.moveaxis(array, 1, 0).reshape(GROUPS, 8, LINES, width), 0, 1)


def side_to_lines(side, wide):
    if wide == 8:
        return side
    enc_rows, read_rows = IN // wide, D // (GROUPS * wide)
    enc = to_rows(side[:, :, :enc_rows], 32)
    read = to_rows(side[:, :, enc_rows : enc_rows + read_rows], 16)
    return jnp.concatenate([enc, read, jnp.zeros((8, GROUPS, 16, 128), side.dtype)], axis=2)


def to_rows(array, rows):
    return jnp.moveaxis(jnp.moveaxis(array, 1, 0).reshape(GROUPS, 8, rows, array.shape[3]), 0, 1)


def from_rows(array, wide):
    rows, width = array.shape[2:]
    return jnp.moveaxis(jnp.moveaxis(array, 1, 0).reshape(GROUPS, wide, 8 * rows // wide, width), 0, 1)


def early_from_lines(array, wide):
    if wide == 8:
        return array
    main = from_rows(array[..., :384], wide)
    enc = from_rows(array[:, :, :32, 384:], wide)
    read = from_rows(array[:, :, 32:48, 384:], wide)
    spare = main.shape[2] - enc.shape[2] - read.shape[2]
    side = jnp.concatenate([enc, read, jnp.zeros((wide, GROUPS, spare, 128), array.dtype)], axis=2)
    return jnp.concatenate([main, side], axis=3)


ORDERS = ((1, 2, 3, 4), (2, 3, 1, 4), (3, 1, 2, 4))
DIMS = ((1, 2, 3, 4), (2, 1, 3, 4))
CUTS = (640, 512)


def by_relative(array, dims):
    array = array.reshape(2, 2, 2, 2, 2, *array.shape[2:])
    axes = {4: 0, 3: 1, 2: 2, 1: 3}
    turned = jnp.transpose(array, (4, *(axes[bit] for bit in dims), 5, 6))
    turned = turned.reshape(4, 8, *turned.shape[5:])
    return [turned[i] for i in range(4)]


def gather_plain(early, late, wide):
    def gathered(array):
        full = lax.all_gather(array, ("wide", "narrow"), axis=0, tiled=False)
        return full.reshape(wide, GROUPS, *array.shape)

    full = gathered(early)
    full = jnp.concatenate([to_lines(full[..., :384], wide), side_to_lines(full[..., 384:], wide)], axis=3)
    first = by_relative(full, DIMS[0])
    full = to_lines(gathered(late), wide)
    second = [by_relative(part, DIMS[i]) for i, part in enumerate(jnp.split(full, [CUTS[0]], axis=3))]
    return first, sum(second, [])


def joined(array, other):
    return jnp.concatenate([array[None], other[None]], axis=0)


def swap(array, bit):
    count = lax.axis_size("wide") * lax.axis_size("narrow")
    return lax.ppermute(array, ("wide", "narrow"), [(i, i ^ (1 << bit)) for i in range(count)])


def cube(array):
    return array.reshape(2, 2, 2, 2, *array.shape[1:])


def flat(array):
    return array.reshape(8, *array.shape[3:])


def halve_kernel(groups, keep, *refs):
    count = len(groups)
    total = sum(groups)
    flat_refs, refs = refs[:total], refs[total:]
    outs, refs = refs[: count * (1 + keep)], refs[count * (1 + keep) :]
    flat_there, refs = refs[:total], refs[total:]
    held, (in_sems, out_sems) = refs[:-2], refs[-2:]
    starts = [sum(groups[:i]) for i in range(count)]
    order = [(i, side) for side in ((1, 0) if keep else (1,)) for i in range(count)]

    def fetch(i, side):
        half = held[i].shape[0]
        here = pl.ds(side * half, half)
        return [
            pltpu.make_async_copy(
                flat_refs[starts[i] + k].at[here],
                flat_there[starts[i] + k].at[here if keep else pl.ds(0, half)],
                in_sems.at[starts[i] + k, side],
            )
            for k in range(groups[i])
        ]

    def leave(i, side):
        at = i if side else count + i
        return pltpu.make_async_copy(held[at], outs[at], out_sems.at[at])

    fetches = {at: fetch(*at) for at in order}
    for at in order:
        for copy in fetches[at]:
            copy.start()
    for i, side in order:
        for copy in fetches[i, side]:
            copy.wait()
        half = held[i].shape[0]
        here = pl.ds(side * half if keep else 0, half)
        added = sum(ref[here].astype(F32) for ref in flat_there[starts[i] : starts[i] + groups[i]])
        at = i if side else count + i
        held[at][...] = added.astype(held[at].dtype)
        leave(i, side).start()
    for i, side in order:
        leave(i, side).wait()


def halve_far(lists, keep):
    groups = [len(arrays) for arrays in lists]
    sizes = [min(array.shape[0] for array in arrays) for arrays in lists]
    halves = [(size // 2, *arrays[0].shape[1:]) for size, arrays in zip(sizes, lists)]
    kinds = (BF, F32)[: 1 + keep]
    outside = pl.BlockSpec(memory_space=pltpu.HBM)
    there = [
        pltpu.VMEM((size if keep else size // 2, *array.shape[1:]), array.dtype)
        for size, arrays in zip(sizes, lists)
        for array in arrays
    ]
    outs = pl.pallas_call(
        functools.partial(halve_kernel, groups, keep),
        in_specs=[outside] * sum(groups),
        out_specs=[outside] * (len(kinds) * len(lists)),
        out_shape=[jax.ShapeDtypeStruct(shape, kind) for kind in kinds for shape in halves],
        scratch_shapes=there
        + [pltpu.VMEM(shape, kind) for kind in kinds for shape in halves]
        + [pltpu.SemaphoreType.DMA((sum(groups), 2)), pltpu.SemaphoreType.DMA((len(kinds) * len(lists),))],
        compiler_params=pltpu.CompilerParams(vmem_limit_bytes=BIG),
        cost_estimate=QUICK,
        name="halve_far",
    )(*(array for arrays in lists for array in arrays))
    return outs[: len(lists)], outs[len(lists) :]


def halve_near_kernel(joint, count, *refs):
    column = 0
    for i in range(count):
        first, second = refs[2 * i], refs[2 * i + 1]
        half, width = first.shape[0] // 2, first.shape[2]
        sent, kept = (refs[2 * count], refs[2 * count + 1]) if joint else refs[2 * count + 2 * i : 2 * count + 2 * i + 2]
        there = slice(column, column + width) if joint else slice(None)
        sent[:, :, there] = (first[half:].astype(F32) + second[half:].astype(F32)).astype(BF)
        kept[:, :, there] = first[:half].astype(F32) + second[:half].astype(F32)
        column += width


def halve_near(pairs, joint=False):
    count = len(pairs)
    vmem = pl.BlockSpec(memory_space=pltpu.VMEM)
    halves = [(pair[0].shape[0] // 2, *pair[0].shape[1:]) for pair in pairs]
    if joint:
        halves = [(*halves[0][:2], sum(shape[2] for shape in halves))]
    outs = pl.pallas_call(
        functools.partial(halve_near_kernel, joint, count),
        in_specs=[vmem] * (2 * count),
        out_specs=[vmem] * (2 * len(halves)),
        out_shape=[jax.ShapeDtypeStruct(shape, kind) for shape in halves for kind in (BF, F32)],
        compiler_params=pltpu.CompilerParams(vmem_limit_bytes=12 * MIB),
        cost_estimate=QUICK,
        name="halve_near",
    )(*(array for pair in pairs for array in pair))
    return outs[0::2], outs[1::2]


class Sums:
    def __init__(self, keep, send, orders):
        self.pairs = [(mine, swap(other, 0)) for mine, other in zip(keep, send)]
        self.orders = orders

    def far_step(self, phase, values):
        sent, kept = halve_far(self.pairs, keep=phase > 0)
        sent, values = lax.optimization_barrier((sent, values))
        came = [swap(out, order[phase]) for out, order in zip(sent, self.orders)]
        self.pairs = [(*(pair if phase == 0 else (kept[i],)), came[i]) for i, pair in enumerate(self.pairs)]
        return values

    def step(self, phase, values=(), **how):
        sent, kept = halve_near(self.pairs, **how)
        sent, values = lax.optimization_barrier((sent, values))
        self.pairs = [(mine, swap(out, order[phase])) for mine, out, order in zip(kept, sent, self.orders)]
        return values

    def came(self, values):
        others, values = lax.optimization_barrier(([other for _, other in self.pairs], values))
        self.pairs = [(mine, other) for (mine, _), other in zip(self.pairs, others)]
        return values


def shares_kernel(loss_ref, early_a, early_b, late_a, late_b, early_ref, late_ref, row_ref):
    early = early_a[0] + early_b[0].astype(F32)
    early_ref[...] = early
    late = late_a[0] + late_b[0].astype(F32)
    late_ref[...] = late
    total = jnp.sum(early * early) + jnp.sum(late * late)
    lanes = lax.broadcasted_iota(jnp.int32, (1, 128), 1)
    row_ref[...] = loss_ref[...] + jnp.where(lanes == 0, total, 0.0)


def shares(loss_part, early, late):
    lines = early[0].shape[1]
    vmem = pl.BlockSpec(memory_space=pltpu.VMEM)
    return pl.pallas_call(
        shares_kernel,
        in_specs=[vmem] * 5,
        out_specs=[vmem] * 3,
        out_shape=(
            jax.ShapeDtypeStruct((lines, EARLY), F32),
            jax.ShapeDtypeStruct((lines, LATE), F32),
            jax.ShapeDtypeStruct((1, 128), F32),
        ),
        compiler_params=pltpu.CompilerParams(vmem_limit_bytes=8 * MIB),
        cost_estimate=QUICK,
        name="shares",
    )(loss_part, *early, *late)


def in_order(keep, send, dims):
    both = jnp.stack([keep, send]).reshape(2, 2, 2, 2, 2, *keep.shape[1:])
    turned = jnp.transpose(both, (*(1 + dims.index(bit) for bit in (4, 3, 2, 1)), 0, 5, 6))
    return turned.reshape(8, 4, *keep.shape[1:])


def scatter_sum(blocks):
    return lax.psum_scatter(
        blocks.astype(F32).reshape(-1, blocks.shape[3]), ("wide", "narrow"), scatter_dimension=0, tiled=True
    )


def sum_all(row):
    count = lax.axis_size("wide") * lax.axis_size("narrow")
    bit = 0
    while 1 << bit < count:
        masks = (1, 2, 3) if bit == 1 else (1,)
        others = [lax.ppermute(row, ("wide", "narrow"), [(i, i ^ (mask << bit)) for i in range(count)]) for mask in masks]
        row = sum(others, row)
        bit += len(masks) // 2 + 1
    return row


def body(
    cond_fields,
    target,
    noise_draw,
    noise_sigma,
    grid_to_mesh,
    mesh_edges,
    mesh_to_grid,
    latitude_row,
    level_index,
    encoder,
    up_proj,
    down_proj,
    readout,
    encoder_moment,
    up_moment,
    down_moment,
    readout_moment,
    encoder_second,
    up_second,
    down_second,
    readout_second,
    encoder_average,
    up_average,
    down_average,
    readout_average,
):
    wide_index = lax.axis_index("wide")
    wide = lax.axis_size("wide")
    globe = lax.axis_index("narrow")
    nodes = mesh_edges.shape[0]
    pixels = cond_fields.shape[1]
    all_nodes = nodes * wide
    width = -(-pixels // 128) * 128

    own_place = [wide_index, globe] if wide == 8 else [0, 0]
    place = jnp.stack([*own_place, globe]).astype(jnp.int32)
    early, late = pack(encoder, up_proj, down_proj.T, readout)
    moving = wide == 8
    tie = lax.optimization_barrier
    if moving:
        early_4 = swap(early, 4)

    if moving:
        early_1 = joined(early, early_4)
        early_3 = swap(early_1, 3)
        early_1, target, noise_draw, noise_sigma = tie((early_1, target, noise_draw, noise_sigma))

    def own(array):
        return lax.dynamic_index_in_dim(jnp.transpose(array, (2, 0, 1)), globe, 1, keepdims=False)

    goal, noise = own(target), own(noise_draw)
    sigma = lax.dynamic_index_in_dim(noise_sigma, globe, 0, keepdims=False)
    square = sigma * sigma
    c_in = lax.rsqrt(square + 1.0)
    if moving:
        early_3, goal, noise = tie((early_3, goal, noise))
        both = joined(early_1, early_3)
        both, goal, noise = tie((both, goal, noise))
        early_2 = swap(both, 2)
    noisy = goal + sigma * noise
    if moving:
        noisy, late = tie((noisy, late))
        late_4 = swap(late, 4)
    grid = jnp.concatenate([own(cond_fields), (c_in * noisy).astype(BF)], axis=0)
    grid = jnp.pad(grid, ((0, 0), (0, width - pixels)))
    edges = mesh_edges.T
    slot_rows = jnp.where(edges >= 0, (edges - wide_index * nodes + nodes + all_nodes) % all_nodes, -1)
    across = jnp.pad(mesh_to_grid.T - wide_index * nodes, ((0, 0), (0, width - pixels)), constant_values=-1)

    def halo(sums):
        low = sums.astype(BF)
        ring = [(i, (i + 1) % wide) for i in range(wide)]
        return lax.ppermute(low, "wide", ring), lax.ppermute(low, "wide", [(j, i) for i, j in ring])

    if moving:
        sums = grid_sums(grid, grid_to_mesh.T - wide_index * pixels)
        before, after = halo(sums)
        early_2, sums = tie((early_2, sums))
        quad, late_1 = joined(both, early_2), joined(late, late_4)
        quad, late_1, slot_rows = tie((quad, late_1, slot_rows))
        early_0 = swap(quad, 1)
        late_3 = swap(late_1, 3)
        bias, pool, pull = counts(slot_rows, across)
        bias, late_3 = tie((bias, late_3))
        both = joined(late_1, late_3)
        parts = [both[..., : CUTS[0]], both[..., CUTS[0] :]]
        parts, early_0, before, after = tie((parts, early_0, before, after))
        got = [swap(parts[0], 2), swap(parts[1], 1)]
        halves = [flat(quad), flat(early_0)]
        gathered = halves + [swap(half, 0) for half in halves]
    else:
        gathered, late_full = gather_plain(early, late, wide)
        sums = grid_sums(grid, grid_to_mesh.T - wide_index * pixels)
        bias, pool, pull = counts(slot_rows, across)
        before, after = halo(sums)

    state0, rows, normed, early_full = encode(place, gathered, before, sums, after)
    if moving:
        got, normed = tie((got, normed))
        parts = [joined(part, one) for part, one in zip(parts, got)]
        parts, normed = tie((parts, normed))
        got = [swap(parts[0], 1), swap(parts[1], 2)]
        halves = [flat(part) for part in parts]
        others = [swap(half, 0) for half in halves]
    mixed, probs, query, pair, inverse = attend(normed, early_full, bias)
    if moving:
        mixed, got, others = tie((mixed, got, others))
        late_full = []
        for half, one, other in zip(halves, got, others):
            late_full += [half, flat(one), other, swap(flat(one), 0)]
    *blocks, grad_state, grad_mixed, grad_scaled, inner, grad_dec, loss_part = feed(
        place, noise_sigma,
        late_full, early_full, state0, mixed, pool, pull, inverse, noisy, goal, latitude_row[None, :], level_index[:, None],
    )
    keep_late, send_late = blocks[:3], blocks[3:]
    if moving:
        late_sum = Sums(keep_late, send_late, ORDERS)
    first_heads = unmix(0, 1, probs, query, pair, grad_mixed, grad_scaled, inner, inverse)
    if moving:
        query, first_heads = late_sum.far_step(0, (query, first_heads))
    last_heads = unmix(1, 3, probs, query, pair, grad_mixed, grad_scaled, inner, inverse)
    if moving:
        grad_state, last_heads = late_sum.far_step(1, (grad_state, last_heads))
    *blocks, = give_back(
        place, early_full, first_heads, last_heads, grad_state, rows, normed, before, sums, after, grad_dec
    )
    keep_early, send_early = blocks[:2], blocks[2:]
    if moving:
        keep_early, send_early = late_sum.came((keep_early, send_early))
        early_sum = Sums(keep_early, send_early, DIMS)
        late_sum.pairs = early_sum.step(0, late_sum.pairs)
        late_sum.step(2)
        late_sum.pairs = early_sum.step(1, late_sum.pairs)
        late_sum.step(3, joint=True)
        early_sum.step(2, joint=True)
        early_sum.step(3)
        share_early, share_late, row = shares(loss_part, early_sum.pairs[0], late_sum.pairs[0])
    else:
        late_lines = jnp.concatenate([in_order(keep_late[i], send_late[i], ORDERS[i]) for i in range(3)], axis=3)
        early_lines = jnp.concatenate([in_order(keep_early[i], send_early[i], DIMS[i]) for i in range(2)], axis=3)
        share_late = scatter_sum(from_rows(late_lines, wide))
        share_early = scatter_sum(early_from_lines(early_lines, wide))
        squares = jnp.sum(share_early * share_early) + jnp.sum(share_late * share_late)
        row = loss_part + jnp.where(lax.broadcasted_iota(jnp.int32, (1, 128), 1) == 0, squares, 0.0)
    row = sum_all(row)
    states = [
        (encoder, encoder_moment, encoder_second, encoder_average),
        (up_proj, up_moment, up_second, up_average),
        (down_proj.T, down_moment.T, down_second.T, down_average.T),
        (readout, readout_moment, readout_second, readout_average),
    ]
    news = list(adam(row, share_early, share_late, states))
    news[10:15] = [array.T for array in news[10:15]]
    return (news[20][0, 0], news[20][0, 1], *news[:20])


def solution(mesh):
    if mesh.shape["narrow"] != GROUPS or MB != GROUPS:
        raise ValueError("narrow size")
    by_pixel = P(None, "wide", None)
    pair = P("wide", "narrow")
    weights = (pair, pair, P("narrow", "wide"), P(("narrow", "wide"), None))
    placed = (by_pixel, by_pixel, by_pixel, P()) + (P("wide", None),) * 3 + (P("wide"), P()) + weights * 4
    given = (P(), P())
    for spec in weights:
        given = given + (spec,) * 5
    return jax.shard_map(body, mesh=mesh, in_specs=placed, out_specs=given, check_vma=False)
```

```python
import functools
import math

import jax
import jax.numpy as jnp
from jax import lax
from jax.experimental import pallas as pl
from jax.experimental.pallas import tpu as pltpu
from jax.sharding import PartitionSpec as P

D = 512
HEADS = 4
HEAD_DIM = 128
OUT = 84
IN = 256
LEVELS = 13
KM = 16
KG = 8
KD = 3
STEPS_DONE = 7
MB = 4
GROUPS = 4
HID = 512
ROWS = 8
LINES = 64
EARLY = 512
LATE = 1152
BAND = 256
WINDOW = 1280
NEAR = 1536

clip_norm = 0.001
beta_one = 0.9
beta_two = 0.999
epsilon = 1e-08
learn_rate = 0.04
weight_decay = 0.1
average_decay = 0.9

BF = jnp.bfloat16
F32 = jnp.float32
MIB = 1024 * 1024
QUICK = pl.CostEstimate(flops=1000, bytes_accessed=1000, transcendentals=0)
BIG = 60 * MIB


def mm(left, right):
    return jnp.dot(left, right, preferred_element_type=F32)


def mm_nt(left, right):
    return lax.dot_general(left, right, (((1,), (1,)), ((), ())), preferred_element_type=F32)


def mm_tn(left, right):
    return lax.dot_general(left, right, (((0,), (0,)), ((), ())), preferred_element_type=F32)


def split_two(value):
    high = value.astype(BF)
    return high, (value - high.astype(F32)).astype(BF)


def norm_parts(rows_low):
    values = rows_low.astype(F32)
    center = values - jnp.mean(values, axis=-1, keepdims=True)
    inverse = lax.rsqrt(jnp.mean(center * center, axis=-1, keepdims=True) + 1e-05)
    return center * inverse, inverse


def norm_pull(grad_out, normal, inverse, gain):
    scaled = grad_out * gain
    inner = (
        scaled
        - jnp.mean(scaled, axis=-1, keepdims=True)
        - normal * jnp.mean(scaled * normal, axis=-1, keepdims=True)
    )
    return inner * inverse, jnp.sum(grad_out * normal, axis=0, keepdims=True)


class Leaving:
    def __init__(self, sems):
        self.sems, self.copies = sems, []

    def __call__(self, source, there):
        self.copies.append(pltpu.make_async_copy(source, there, self.sems.at[len(self.copies)]))
        self.copies[-1].start()

    def wait(self):
        for copy in self.copies:
            copy.wait()


def sums_kernel(grid_ref, pixels_ref, sums_ref, count_ref):
    width, nodes = count_ref.shape
    step = 32
    picks = [jnp.broadcast_to(pixels_ref[k : k + 1, :], (step, nodes)) for k in range(KG)]
    rows = lax.broadcasted_iota(jnp.int32, (step, nodes), 0)

    def count(i, _):
        at = pl.multiple_of(i * step, step)
        total = jnp.zeros((step, nodes), F32)
        for pick in picks:
            total = total + jnp.where(pick - at == rows, 1.0, 0.0)
        count_ref[pl.ds(at, step), :] = total.astype(BF)
        return 0

    lax.fori_loop(0, width // step, count, 0)
    sums_ref[...] = mm(grid_ref[...], count_ref[...])


def grid_sums(grid, pixel_rows):
    nodes, width = pixel_rows.shape[1], grid.shape[1]
    return pl.pallas_call(
        sums_kernel,
        out_shape=jax.ShapeDtypeStruct((IN, nodes), F32),
        scratch_shapes=[pltpu.VMEM((width, nodes), BF)],
        compiler_params=pltpu.CompilerParams(vmem_limit_bytes=16 * 1024 * 1024),
        cost_estimate=QUICK,
        name="grid_sums",
    )(grid, pixel_rows)


def pull_kernel(across_ref, pool_ref, pull_ref):
    nodes, width = pull_ref.shape
    across = across_ref[...]

    def count_across(i, _):
        at = pl.multiple_of(i * 128, 128)
        rows = lax.broadcasted_iota(jnp.int32, (128, width), 0) + at
        total = jnp.zeros((128, width), F32)
        for k in range(KD):
            total = total + jnp.where(across[k : k + 1, :] == rows, 1.0, 0.0)
        pull_ref[pl.ds(at, 128), :] = total.astype(BF)
        pool_ref[:, pl.ds(at, 128)] = total.T.astype(BF)
        return 0

    lax.fori_loop(0, nodes // 128, count_across, 0)


def pull_counts(across_rows, nodes):
    width = across_rows.shape[1]
    return pl.pallas_call(
        pull_kernel,
        out_shape=(jax.ShapeDtypeStruct((width, nodes), BF), jax.ShapeDtypeStruct((nodes, width), BF)),
        compiler_params=pltpu.CompilerParams(vmem_limit_bytes=BIG),
        cost_estimate=QUICK,
        name="pull_counts",
    )(across_rows)


def counts_kernel(slots_ref, bias_out, bias_ref, sems):
    nodes = slots_ref.shape[1]
    step = 64
    leave = Leaving(sems)
    for band in range(nodes // BAND):
        low = band * BAND
        picks = slots_ref[:, low : low + BAND] - low
        rows = lax.broadcasted_iota(jnp.int32, (step, BAND), 0)
        alike = jnp.zeros((KM, BAND), F32)
        for k in range(KM):
            alike = alike + jnp.where(picks == picks[k : k + 1, :], 1.0, 0.0)
        weight = jnp.log2(alike)

        def count_slots(i, _):
            at = pl.multiple_of(i * step, step)
            value = jnp.full((step, BAND), -1e30, F32)
            for k in range(KM):
                value = jnp.where(picks[k : k + 1, :] - at == rows, weight[k : k + 1, :], value)
            bias_ref[band, pl.ds(at, step), :] = value
            return 0

        for part in range(2):
            half = WINDOW // step // 2
            lax.fori_loop(part * half, (part + 1) * half, count_slots, 0)
            here = slice(part * half * step, (part + 1) * half * step)
            leave(bias_ref.at[band, here], bias_out.at[band, here])
    leave.wait()


def counts(slot_rows):
    nodes = slot_rows.shape[1]
    shape = jax.ShapeDtypeStruct((nodes // BAND, WINDOW, BAND), F32)
    return pl.pallas_call(
        counts_kernel,
        out_specs=pl.BlockSpec(memory_space=pltpu.HBM),
        out_shape=shape,
        scratch_shapes=[pltpu.VMEM(shape.shape, shape.dtype), pltpu.SemaphoreType.DMA((4,))],
        compiler_params=pltpu.CompilerParams(vmem_limit_bytes=BIG),
        cost_estimate=QUICK,
        name="counts",
    )(slot_rows)


def blocks_of(place_ref, dims, refs):
    own_wide, own_narrow = place_ref[0], place_ref[1]
    found = []
    for side in range(2):
        for j in range(16):
            bits = dict(zip(dims, ((j >> 3) & 1, (j >> 2) & 1, (j >> 1) & 1, j & 1)))
            wide = own_wide ^ (bits[4] * 4 + bits[3] * 2 + bits[2])
            narrow = own_narrow ^ (bits[1] * 2 + side)
            found.append((wide, narrow, refs[2 * side + (j >> 3)].at[j & 7]))
    return found


def block_at(dims, part, wide):
    bits = {1: part, 2: wide & 1, 3: (wide >> 1) & 1, 4: wide >> 2}
    return ((bits[dims[0]] * 2 + bits[dims[1]]) * 2 + bits[dims[2]]) * 2 + bits[dims[3]]


def fetch_early(place_ref, refs, early, sems):
    return [
        pltpu.make_async_copy(source, early.at[wide, narrow], sems.at[i])
        for i, (wide, narrow, source) in enumerate(blocks_of(place_ref, DIMS[0], refs))
    ]


def enc_of(early):
    return jnp.concatenate([early[:, n, 0:32, 384:512].reshape(IN, 128) for n in range(GROUPS)], axis=1)


def dec_of(early):
    return jnp.concatenate([early[:, n, 32:48, 384:512].reshape(128, 128) for n in range(GROUPS)], axis=0)


def query_of(early):
    return jnp.concatenate([early[:, n, :, 0:128].reshape(D, 128) for n in range(GROUPS)], axis=1)


def pair_of(early):
    return jnp.concatenate([early[:, n, :, 128:384].reshape(D, 256) for n in range(GROUPS)], axis=1)


def encode_kernel(
    place_ref, a_0, a_1, a_2, a_3, before_ref, sums_ref, after_ref,
    state_ref, rows_ref, normed_ref, early_ref,
    early, state, rows_all, normed_all, sems, out_sems,
):
    copies = fetch_early(place_ref, (a_0, a_1, a_2, a_3), early, sems)
    for copy in copies:
        copy.start()
    for copy in copies:
        copy.wait()
    leave = Leaving(out_sems)
    leave(early, early_ref)
    gain = dec_of(early).astype(F32).T[OUT : OUT + 1, :]
    enc = enc_of(early)
    for block, ref in enumerate((before_ref, sums_ref, after_ref)):
        here = slice(block * 512, block * 512 + 512)
        if block == 1:
            high, low = split_two(ref[...])
            embedded = (mm_tn(high, enc) + mm_tn(low, enc)) * (1.0 / KG)
            state[...] = embedded
            leave(state, state_ref)
        else:
            embedded = mm_tn(ref[...], enc) * (1.0 / KG)
        rows = embedded.astype(BF)
        rows_all[here, :] = rows
        leave(rows_all.at[here], rows_ref.at[here])
        normal, _inverse = norm_parts(rows)
        normed_all[here, :] = (normal * gain).astype(BF)
        leave(normed_all.at[here], normed_ref.at[here])
    leave.wait()


def encode(place, gathered, before, sums, after):
    nodes = sums.shape[1]
    vmem = pl.BlockSpec(memory_space=pltpu.VMEM)
    outside = pl.BlockSpec(memory_space=pltpu.HBM)
    shapes = (
        jax.ShapeDtypeStruct((nodes, D), F32),
        jax.ShapeDtypeStruct((NEAR, D), BF),
        jax.ShapeDtypeStruct((NEAR, D), BF),
        jax.ShapeDtypeStruct((8, GROUPS, LINES, EARLY), BF),
    )
    return pl.pallas_call(
        encode_kernel,
        in_specs=[pl.BlockSpec(memory_space=pltpu.SMEM)] + [outside] * 4 + [vmem] * 3,
        out_specs=[outside] * 4,
        out_shape=shapes,
        scratch_shapes=[pltpu.VMEM((8, GROUPS, LINES, EARLY), BF)]
        + [pltpu.VMEM(shape.shape, shape.dtype) for shape in shapes[:3]]
        + [pltpu.SemaphoreType.DMA((32,)), pltpu.SemaphoreType.DMA((8,))],
        compiler_params=pltpu.CompilerParams(vmem_limit_bytes=BIG),
        cost_estimate=QUICK,
        name="encode",
    )(place, *gathered, before, sums, after)


def attend_kernel(
    normed_in, early_in, bias_in, mixed_ref, probs_ref, query_ref, pair_ref, inverse_ref,
    normed, early, bias, query_all, pair_all, mixed_all, probs, inverse_all, sems, out_sems,
):
    def weight_copy(h):
        return pltpu.make_async_copy(early_in.at[:, h, :, 0:384], early.at[h], sems.at[h])

    normed_copy = pltpu.make_async_copy(normed_in, normed, sems.at[4])
    bias_copies = [pltpu.make_async_copy(bias_in.at[i], bias.at[i], sems.at[5 + i]) for i in range(2)]
    weight_copy(0).start()
    normed_copy.start()
    bias_copies[0].start()
    bias_copies[1].start()
    for h in range(1, HEADS):
        weight_copy(h).start()
    normed_copy.wait()
    factor = HEAD_DIM ** (-0.5) * math.log2(math.e)

    def pair_leave(h):
        return pltpu.make_async_copy(pair_all.at[h], pair_ref.at[h], out_sems.at[8 + h])

    def probs_leave(h):
        return pltpu.make_async_copy(probs.at[h], probs_ref.at[h], out_sems.at[4 + h])

    for h in range(HEADS):
        lanes = slice(h * HEAD_DIM, h * HEAD_DIM + HEAD_DIM)
        weight_copy(h).wait()
        weights = early[h].reshape(D, 384)
        pair_all[h] = mm(normed[...], weights[:, 128:384]).astype(BF)
        query_all[:, lanes] = mm(normed[512:1024, :], weights[:, 0:128]).astype(BF)
        if h == 0:
            bias_copies[0].wait()
            bias_copies[1].wait()
        for band in range(2):
            at = band * BAND
            near, here = slice(at, at + WINDOW), slice(at, at + BAND)
            part = mm_nt(pair_all[h, near, :HEAD_DIM], query_all[here, lanes]) * factor + bias[band]
            expo = jnp.exp2(part - jnp.max(part, axis=0, keepdims=True))
            inverse = 1.0 / jnp.sum(expo, axis=0, keepdims=True)
            low = expo.astype(BF)
            probs[h, near, here] = low
            inverse_all[h : h + 1, here] = inverse
            column = jnp.broadcast_to(inverse, (8, BAND)).T[:, 0:1]
            mixed_all[here, lanes] = mm_tn(low, pair_all[h, near, HEAD_DIM:]) * column
        probs_leave(h).start()
        pair_leave(h).start()
    inverse_all[HEADS:8, :] = jnp.zeros((8 - HEADS, inverse_all.shape[1]), F32)
    leave = Leaving(out_sems)
    leave(mixed_all, mixed_ref)
    leave(query_all, query_ref)
    leave(inverse_all, inverse_ref)
    leave.wait()
    for h in range(HEADS):
        pair_leave(h).wait()
        probs_leave(h).wait()


def attend(normed, early, bias):
    nodes = normed.shape[0] // 3
    outside = pl.BlockSpec(memory_space=pltpu.HBM)
    return pl.pallas_call(
        attend_kernel,
        in_specs=[outside] * 3,
        out_specs=[outside] * 5,
        out_shape=(
            jax.ShapeDtypeStruct((nodes, D), F32),
            jax.ShapeDtypeStruct((HEADS, NEAR, nodes), BF),
            jax.ShapeDtypeStruct((nodes, D), BF),
            jax.ShapeDtypeStruct((HEADS, NEAR, 2 * HEAD_DIM), BF),
            jax.ShapeDtypeStruct((8, nodes), F32),
        ),
        scratch_shapes=[
            pltpu.VMEM((NEAR, D), BF),
            pltpu.VMEM((GROUPS, 8, LINES, 384), BF),
            pltpu.VMEM((2, WINDOW, BAND), F32),
            pltpu.VMEM((nodes, D), BF),
            pltpu.VMEM((HEADS, NEAR, 2 * HEAD_DIM), BF),
            pltpu.VMEM((nodes, D), F32),
            pltpu.VMEM((HEADS, NEAR, nodes), BF),
            pltpu.VMEM((8, nodes), F32),
            pltpu.SemaphoreType.DMA((7,)),
            pltpu.SemaphoreType.DMA((12,)),
        ],
        compiler_params=pltpu.CompilerParams(vmem_limit_bytes=BIG),
        cost_estimate=QUICK,
        name="attend",
    )(normed, early, bias)


def feed_kernel(
    place_ref, sigma_ref, a_0, a_1, a_2, a_3, b_0, b_1, b_2, b_3, early_ref, state_in, mixed_in, pool_in, pull_in, inverse_ref, noisy_ref, target_ref, lat_ref, level_ref,
    keep_0, keep_1, keep_2, send_0, send_1, send_2, grad_state_out, grad_mixed_out, grad_scaled_out, inner_ref, grad_dec_ref, loss_ref,
    late, dec, pre_ref, act_ref, grad_pred_ref,
    state_ref, mixed_ref, pool_ref, pull_ref, keep_ref, send_ref, grad_state_ref, grad_mixed_ref, grad_scaled_ref, sems, group_sems, out_sems,
):
    own_wide, own_narrow = place_ref[0], place_ref[1]

    refs = (a_0, a_1, a_2, a_3), (b_0, b_1, b_2, b_3)

    def fetch(colour, columns, first, sem):
        there = slice(first, first + columns.stop - columns.start)
        return [
            pltpu.make_async_copy(source.at[:, columns], late.at[wide, narrow, :, there], sem(narrow, i))
            for i, (wide, narrow, source) in enumerate(blocks_of(place_ref, DIMS[colour], refs[colour]))
        ]

    def group(n, columns, row):
        return pltpu.make_async_copy(late.at[:, n, :, columns], late.at[:, n, :, columns], group_sems.at[row, n])

    hidden, outer, lower = slice(0, 512), slice(512, 640), slice(640, 1152)
    pairs = [(state_in, state_ref), (mixed_in, mixed_ref), (early_ref.at[:, :, 32:48, 384:512], dec)]
    small = [pltpu.make_async_copy(source, there, sems.at[32 + i]) for i, (source, there) in enumerate(pairs)]
    small += fetch(0, outer, 512, lambda n, i: sems.at[i])
    pool_copy = pltpu.make_async_copy(pool_in, pool_ref, sems.at[35])
    pull_copy = pltpu.make_async_copy(pull_in, pull_ref, sems.at[36])
    first = fetch(0, hidden, 0, lambda n, i: group_sems.at[0, n])
    second = fetch(1, slice(0, 512), 640, lambda n, i: group_sems.at[1, n])
    for copy in (*small, *first, *second, pool_copy, pull_copy):
        copy.start()
    for copy in small:
        copy.wait()
    dec_turned = jnp.concatenate([dec[:, n].reshape(128, 128) for n in range(GROUPS)], axis=0).astype(F32).T
    gain = dec_turned[OUT + 1 : OUT + 2, :]
    rows = lax.broadcasted_iota(jnp.int32, (128, 1), 0)
    dec_only = jnp.where(rows < OUT, dec_turned, 0.0).astype(BF)
    out_full = jnp.concatenate([late[:, n, :, 512:640].reshape(D, 128) for n in range(GROUPS)], axis=1)
    mixed = mixed_ref[...].astype(BF)
    state1 = state_ref[...] + mm_nt(mixed, out_full)
    normal, inverse = norm_parts(state1.astype(BF))
    normed = (normal * gain).astype(BF)

    def forward(i, state):
        n = i ^ own_narrow
        group(n, hidden, 0).wait()
        pre = mm(normed, late[:, n, :, 0:512].reshape(D, HID))
        pre_ref[n] = pre
        act = (pre / (1.0 + jnp.exp(-pre))).astype(BF)
        act_ref[n] = act
        group(n, lower, 1).wait()
        return state + mm_nt(act, late[:, n, :, 640:1152].reshape(D, HID))

    state2 = state1
    for i in range(GROUPS):
        state2 = forward(i, state2)
    high, low = split_two(state2)
    pool_copy.wait()
    pull_copy.wait()
    pool = pool_ref[...]
    pooled = ((mm(pool, high) + mm(pool, low)) / KD).astype(BF)
    pixels = noisy_ref.shape[1]
    pred = mm_nt(dec_only, pooled)[:OUT, :pixels]
    sigma = jnp.full((1, 1), sigma_ref[place_ref[2]], F32)
    square = sigma * sigma
    c_skip = 1.0 / (square + 1.0)
    c_out = sigma * lax.rsqrt(square + 1.0)
    lam = (square + 1.0) / square
    error = c_skip * noisy_ref[...] + c_out * pred - target_ref[...]
    weight = jnp.cos((lat_ref[...].astype(F32) - 90.0) * (math.pi / 180.0)) * ((level_ref[...].astype(F32) + 1.0) / LEVELS)
    weighted = lam * weight
    first_globe = (jnp.full((1, 1), place_ref[2], jnp.int32) == 0).astype(F32)
    lanes = lax.broadcasted_iota(jnp.int32, (1, 128), 1)
    loss_ref[...] = jnp.where(lanes == 1, jnp.sum(weighted * error * error), 0.0) + jnp.where(
        lanes == 2, jnp.sum(weight) * first_globe, 0.0
    )
    grad_pred_ref[...] = jnp.zeros_like(grad_pred_ref)
    grad_pred_ref[:OUT, :pixels] = 2.0 * c_out * weighted * error
    grad_pred = grad_pred_ref[...].astype(BF)
    grad_dec_ref[...] = mm(grad_pred, pooled)
    up_high, up_low = split_two(mm_nt(pull_ref[...], grad_pred))
    grad_state2 = (mm(up_high, dec_only) + mm(up_low, dec_only)) / KD
    grad_low = grad_state2.astype(BF)
    grad_turned = grad_state2.T.astype(BF)
    normed_turned = normed.astype(F32).T.astype(BF)

    def put(out_ref, side, part, first, value):
        done = 0
        while done < value.shape[1]:
            colour, column = divmod(first + done, 384)
            count = min(384 - column, value.shape[1] - done)
            for w in range(8):
                out_ref[colour, block_at(ORDERS[colour], part, w ^ own_wide), :, column : column + count] = value[
                    w * LINES : (w + 1) * LINES, done : done + count
                ]
            done += count

    def backward(part, grad_n, out_ref, side):
        n = (part * 2 + side) ^ own_narrow
        act = act_ref[n]
        pre = pre_ref[n]
        put(out_ref, side, part, 640, mm(grad_turned, act).astype(BF))
        grad_act = mm(grad_low, late[:, n, :, 640:1152].reshape(D, HID))
        logistic = 1.0 / (1.0 + jnp.exp(-pre))
        grad_pre = (grad_act * logistic * (1.0 + pre * (1.0 - logistic))).astype(BF)
        put(out_ref, side, part, 0, mm(normed_turned, grad_pre).astype(BF))
        return grad_n + mm_nt(grad_pre, late[:, n, :, 0:512].reshape(D, HID))

    grad_n = jnp.zeros((D, D), F32)
    leaving = []

    def leave(source, there):
        leaving.append(pltpu.make_async_copy(source, there, out_sems.at[len(leaving)]))
        leaving[-1].start()

    sides = ((1, send_ref, (send_0, send_1, send_2)), (0, keep_ref, (keep_0, keep_1, keep_2)))
    for side, out_ref, there in sides:
        for part in range(2):
            grad_n = backward(part, grad_n, out_ref, side)
        leave(out_ref.at[0], there[0])
        leave(out_ref.at[2], there[2])
    back, gain_grad = norm_pull(grad_n, normal, inverse, gain)
    grad_dec_ref[OUT + 1 : OUT + 2, :] = gain_grad
    grad_state1 = grad_state2 + back
    grad_state_ref[...] = grad_state1
    leave(grad_state_ref, grad_state_out)
    grad_low1 = grad_state1.astype(BF)
    act_ref[0] = mixed
    grad_turned1 = grad_state1.T.astype(BF)
    for side, out_ref, there in sides:
        for part in range(2):
            lane = pl.multiple_of(((part * 2 + side) ^ own_narrow) * 128, 128)
            put(out_ref, side, part, 512, mm(grad_turned1, act_ref[0, :, pl.ds(lane, 128)]).astype(BF))
        leave(out_ref.at[1], there[1])
    grad_mixed = mm(grad_low1, out_full)
    grad_mixed_ref[...] = grad_mixed.astype(BF)
    leave(grad_mixed_ref, grad_mixed_out)
    columns = inverse_ref[...].T
    lanes = lax.broadcasted_iota(jnp.int32, (1, 128), 1)
    inner = jnp.zeros((grad_mixed.shape[0], 128), F32)
    for h in range(HEADS):
        here = slice(h * HEAD_DIM, h * HEAD_DIM + HEAD_DIM)
        grad = grad_mixed[:, here]
        grad_scaled_ref[:, here] = (grad * columns[:, h : h + 1]).astype(BF)
        inner = jnp.where(lanes == h, jnp.sum(grad * mixed_ref[:, here], axis=1, keepdims=True), inner)
    leave(grad_scaled_ref, grad_scaled_out)
    inner_ref[...] = inner.T[0:8, :]
    for copy in leaving:
        copy.wait()


def feed(place, sigma, late, early, state0, mixed, pool, pull, inverse, noisy, target, lat, level):
    nodes = state0.shape[0]
    width = pool.shape[0]
    vmem = pl.BlockSpec(memory_space=pltpu.VMEM)
    outside = pl.BlockSpec(memory_space=pltpu.HBM)
    return pl.pallas_call(
        feed_kernel,
        in_specs=[pl.BlockSpec(memory_space=pltpu.SMEM)] * 2 + [outside] * 13 + [vmem] * 5,
        out_specs=[outside] * 9 + [vmem] * 3,
        out_shape=(
            *([jax.ShapeDtypeStruct((16, LINES, 384), BF)] * 6),
            jax.ShapeDtypeStruct((nodes, D), F32),
            jax.ShapeDtypeStruct((nodes, D), BF),
            jax.ShapeDtypeStruct((nodes, D), BF),
            jax.ShapeDtypeStruct((8, nodes), F32),
            jax.ShapeDtypeStruct((128, D), F32),
            jax.ShapeDtypeStruct((1, 128), F32),
        ),
        scratch_shapes=[
            pltpu.VMEM((8, GROUPS, LINES, LATE), BF),
            pltpu.VMEM((8, GROUPS, 16, 128), BF),
            pltpu.VMEM((GROUPS, nodes, HID), F32),
            pltpu.VMEM((GROUPS, nodes, HID), BF),
            pltpu.VMEM((128, width), F32),
            pltpu.VMEM((nodes, D), F32),
            pltpu.VMEM((nodes, D), F32),
            pltpu.VMEM((width, nodes), BF),
            pltpu.VMEM((nodes, width), BF),
            pltpu.VMEM((3, 16, LINES, 384), BF),
            pltpu.VMEM((3, 16, LINES, 384), BF),
            pltpu.VMEM((nodes, D), F32),
            pltpu.VMEM((nodes, D), BF),
            pltpu.VMEM((nodes, D), BF),
            pltpu.SemaphoreType.DMA((37,)),
            pltpu.SemaphoreType.DMA((2, GROUPS)),
            pltpu.SemaphoreType.DMA((9,)),
        ],
        compiler_params=pltpu.CompilerParams(vmem_limit_bytes=BIG),
        cost_estimate=QUICK,
        name="feed",
    )(place, sigma, *late, early, state0, mixed, pool, pull, inverse, noisy, target, lat, level)


def unmix_kernel(first, probs_ref, query_ref, keys_ref, values_ref, grad_mixed_ref, grad_scaled_ref, inner_ref, inverse_ref,
                 grad_query_ref, grad_pair_ref, grad_scores):
    scale = HEAD_DIM ** (-0.5)
    row = pl.ds(first + pl.program_id(0), 1)
    inner = inner_ref[row, :]
    factor = inverse_ref[row, :] * scale
    pieces = ((0, 256, 0, 256), (256, 768, 0, 512), (768, 1280, 0, 512), (1280, 1536, 256, 512))
    for low_row, high_row, low_column, high_column in pieces:
        rows, columns = slice(low_row, high_row), slice(low_column, high_column)
        probs = probs_ref[0, rows, columns]
        grad_probs = mm_nt(values_ref[0, rows, :], grad_mixed_ref[columns, :])
        low = (probs.astype(F32) * ((grad_probs - inner[:, columns]) * factor[:, columns])).astype(BF)
        grad_scores[rows, columns] = low
        grad_pair_ref[rows, 0:HEAD_DIM] = mm(low, query_ref[columns, :]).astype(BF)
        grad_pair_ref[rows, HEAD_DIM : 2 * HEAD_DIM] = mm(probs, grad_scaled_ref[columns, :]).astype(BF)
    for at in (0, BAND):
        grad_query_ref[at : at + BAND, :] = mm_tn(
            grad_scores[at : at + WINDOW, at : at + BAND], keys_ref[0, at : at + WINDOW, :]
        ).astype(BF)


def unmix(first, heads, probs, query, pair, grad_mixed, grad_scaled, inner, inverse):
    nodes = query.shape[0]
    part = pl.BlockSpec((nodes, HEAD_DIM), lambda i: (0, first + i))
    whole = pl.BlockSpec((8, nodes), lambda i: (0, 0))
    return pl.pallas_call(
        functools.partial(unmix_kernel, first),
        grid=(heads,),
        in_specs=[
            pl.BlockSpec((1, NEAR, nodes), lambda i: (first + i, 0, 0)),
            part,
            pl.BlockSpec((1, NEAR, HEAD_DIM), lambda i: (first + i, 0, 0)),
            pl.BlockSpec((1, NEAR, HEAD_DIM), lambda i: (first + i, 0, 1)),
            part,
            part,
            whole,
            whole,
        ],
        out_specs=(
            pl.BlockSpec((nodes, HEAD_DIM), lambda i: (0, i)),
            pl.BlockSpec((NEAR, 2 * HEAD_DIM), lambda i: (0, i)),
        ),
        out_shape=(
            jax.ShapeDtypeStruct((nodes, heads * HEAD_DIM), BF),
            jax.ShapeDtypeStruct((NEAR, heads * 2 * HEAD_DIM), BF),
        ),
        scratch_shapes=[pltpu.VMEM((NEAR, nodes), BF)],
        compiler_params=pltpu.CompilerParams(vmem_limit_bytes=BIG),
        cost_estimate=QUICK,
        name="unmix",
    )(probs, query, pair, pair, grad_mixed, grad_scaled, inner, inverse)


def return_kernel(
    place_ref, early_ref, query_in_a, query_in_b, pair_in_a, pair_in_b,
    grad_state_in, rows_in, normed_in, before_ref, sums_ref, after_ref, grad_dec_ref,
    keep_0, keep_1, send_0, send_1,
    early, normed_ref, rows_ref, grad_state_ref, query_g, pair_g, sems,
):
    pairs = (
        (normed_in, normed_ref),
        (query_in_a, query_g.at[:, 0:128]), (query_in_b, query_g.at[:, 128:512]),
        (pair_in_a, pair_g.at[:, 0:256]), (pair_in_b, pair_g.at[:, 256:1024]),
        (early_ref, early), (rows_in, rows_ref), (grad_state_in, grad_state_ref),
    )
    copies = [pltpu.make_async_copy(source, there, sems.at[i]) for i, (source, there) in enumerate(pairs)]
    for copy in copies:
        copy.start()
    own_wide, own_narrow = place_ref[0], place_ref[1]
    def put(n, colour, column, value, low):
        lines = value.shape[0] // 8
        for side, out_refs in ((1, (send_0, send_1)), (0, (keep_0, keep_1))):

            @pl.when(((n ^ own_narrow) & 1) == side)
            def _():
                part = (n ^ own_narrow) >> 1
                for w in range(8):
                    out_refs[colour][block_at(DIMS[colour], part, w ^ own_wide), low : low + lines, column : column + 128] = value[
                        w * lines : (w + 1) * lines, :
                    ]

    copies[0].wait()
    turned = normed_ref[...].astype(F32).T.astype(BF)
    for copy in copies[1:5]:
        copy.wait()
    weight_query = mm(turned[:, 512:1024], query_g[...]).astype(BF)
    weight_pair = mm(turned, pair_g[...]).astype(BF)
    for n in range(GROUPS):
        put(n, 0, 0, weight_query[:, n * 128 : n * 128 + 128], 0)
        put(n, 0, 128, weight_pair[:, n * 256 : n * 256 + 128], 0)
        put(n, 1, 0, weight_pair[:, n * 256 + 128 : n * 256 + 256], 0)
    for copy in copies[5:]:
        copy.wait()
    gain = dec_of(early).astype(F32).T[OUT : OUT + 1, :]
    pair_weights = pair_of(early)
    grad_enc = jnp.zeros((IN, D), F32)
    gain_grad = jnp.zeros((1, D), F32)
    for block, sums in enumerate((before_ref, sums_ref, after_ref)):
        at = block * 512
        grad_block = mm_nt(pair_g[at : at + 512, :], pair_weights)
        if block == 1:
            grad_block = grad_block + mm_nt(query_g[...], query_of(early))
        normal, inverse = norm_parts(rows_ref[at : at + 512, :])
        back, gain_part = norm_pull(grad_block, normal, inverse, gain)
        gain_grad = gain_grad + gain_part
        if block == 1:
            back = back + grad_state_ref[...]
        back_low = (back * (1.0 / KG)).astype(BF)
        grad_enc = grad_enc + mm(sums[...].astype(BF), back_low)
    grad_enc = grad_enc.astype(BF)
    rows = lax.broadcasted_iota(jnp.int32, (128, 1), 0)
    grad_dec = jnp.where(rows == OUT, gain_grad, grad_dec_ref[...]).T.astype(BF)
    for n in range(GROUPS):
        put(n, 1, 128, grad_enc[:, n * 128 : n * 128 + 128], 0)
        put(n, 1, 128, grad_dec[n * 128 : n * 128 + 128, :], 32)
        put(n, 1, 128, jnp.zeros((128, 128), BF), 48)


def give_back(place, early, first, second, grad_state, rows, normed, before, sums, after, grad_dec):
    vmem = pl.BlockSpec(memory_space=pltpu.VMEM)
    outside = pl.BlockSpec(memory_space=pltpu.HBM)
    return pl.pallas_call(
        return_kernel,
        in_specs=[pl.BlockSpec(memory_space=pltpu.SMEM), outside] + [outside] * 7 + [vmem] * 4,
        out_specs=[vmem] * 4,
        out_shape=[jax.ShapeDtypeStruct((16, LINES, 256), BF)] * 4,
        scratch_shapes=[
            pltpu.VMEM((8, GROUPS, LINES, EARLY), BF),
            pltpu.VMEM((NEAR, D), BF),
            pltpu.VMEM((NEAR, D), BF),
            pltpu.VMEM((512, D), F32),
            pltpu.VMEM((512, D), BF),
            pltpu.VMEM((NEAR, 2 * D), BF),
            pltpu.SemaphoreType.DMA((14,)),
        ],
        compiler_params=pltpu.CompilerParams(vmem_limit_bytes=36 * MIB),
        cost_estimate=QUICK,
        name="give_back",
    )(
        place,
        *(
            pltpu.with_memory_space_constraint(array, pltpu.HBM)
            for array in (early, first[0], second[0], first[1], second[1], grad_state, rows, normed)
        ),
        before, sums, after, grad_dec,
    )


def adam_kernel(row_ref, early_ref, late_ref, *refs):
    total = row_ref[0:1, 2:3] * MB
    norm_value = jnp.sqrt(row_ref[0:1, 0:1]) / total
    factor = jnp.minimum(1.0, clip_norm / norm_value) / total
    lanes = lax.broadcasted_iota(jnp.int32, (8, 128), 1)
    refs[36][...] = jnp.where(lanes == 0, row_ref[0:1, 1:2] / total, norm_value)
    fix_one = 1.0 - beta_one**STEPS_DONE
    fix_two = 1.0 - beta_two**STEPS_DONE
    enc_rows, read_rows = refs[0].shape[0], refs[12].shape[0]
    shares = (
        ((early_ref, slice(0, enc_rows), slice(384, 512), slice(None)),),
        ((early_ref, slice(None), slice(0, 384), slice(0, 384)), (late_ref, slice(None), slice(0, 512), slice(384, 896))),
        ((late_ref, slice(None), slice(512, 1152), slice(None)),),
        ((early_ref, slice(enc_rows, enc_rows + read_rows), slice(384, 384 + OUT + 2), slice(None)),),
    )
    for i, pieces in enumerate(shares):
        weight_ref, moment_ref, second_ref, average_ref = refs[4 * i : 4 * i + 4]
        outs = refs[16 + 5 * i : 21 + 5 * i]
        for share_ref, rows, columns, there in pieces:
            grad = share_ref[rows, columns] * factor
            weight = weight_ref[:, there]
            moment = beta_one * moment_ref[:, there] + (1.0 - beta_one) * grad
            second = beta_two * second_ref[:, there] + (1.0 - beta_two) * grad * grad
            weight = weight - learn_rate * (
                moment / fix_one / (jnp.sqrt(second / fix_two) + epsilon) + weight_decay * weight
            )
            outs[0][:, there] = moment
            outs[1][:, there] = second
            outs[2][:, there] = weight
            outs[3][:, there] = average_decay * average_ref[:, there] + (1.0 - average_decay) * weight
            outs[4][:, there] = weight.astype(BF)


def adam(row, early, late, states):
    arrays = [array for state in states for array in state]
    shapes = []
    for state in states:
        shapes += [jax.ShapeDtypeStruct(state[0].shape, F32)] * 4 + [jax.ShapeDtypeStruct(state[0].shape, BF)]
    shapes.append(jax.ShapeDtypeStruct((8, 128), F32))
    vmem = pl.BlockSpec(memory_space=pltpu.VMEM)
    return pl.pallas_call(
        adam_kernel,
        in_specs=[vmem] * 19,
        out_specs=[vmem] * 21,
        out_shape=shapes,
        compiler_params=pltpu.CompilerParams(vmem_limit_bytes=16 * MIB),
        cost_estimate=QUICK,
        name="adam",
    )(row, early, late, *arrays)


def pack_kernel(encoder_in, up_in, down_in, readout_in, early_ref, late_ref, encoder_ref, up_ref, down_ref, readout_ref, sems):
    pairs = ((up_in, up_ref), (encoder_in, encoder_ref), (readout_in, readout_ref), (down_in, down_ref))
    copies = [pltpu.make_async_copy(source, there, sems.at[i]) for i, (source, there) in enumerate(pairs)]
    for copy in copies:
        copy.start()
    for copy in copies:
        copy.wait()
    enc_rows, read_rows = encoder_ref.shape[0], readout_ref.shape[0]
    early_ref[:, 0:384] = up_ref[:, 0:384].astype(BF)
    side = jnp.zeros((early_ref.shape[0] - enc_rows, 128), F32)
    early_ref[enc_rows:, 384:512] = side.astype(BF)
    early_ref[0:enc_rows, 384:512] = encoder_ref[...].astype(BF)
    early_ref[enc_rows : enc_rows + read_rows, 384 : 384 + OUT + 2] = readout_ref[...].astype(BF)
    late_ref[:, 0:512] = up_ref[:, 384:896].astype(BF)
    late_ref[:, 512:1152] = down_ref[...].astype(BF)


def pack(encoder, up_proj, down_turned, readout):
    lines = up_proj.shape[0]
    vmem = pl.BlockSpec(memory_space=pltpu.VMEM)
    outside = pl.BlockSpec(memory_space=pltpu.HBM)
    return pl.pallas_call(
        pack_kernel,
        in_specs=[outside] * 4,
        out_specs=[vmem] * 2,
        out_shape=(jax.ShapeDtypeStruct((lines, EARLY), BF), jax.ShapeDtypeStruct((lines, LATE), BF)),
        scratch_shapes=[pltpu.VMEM(array.shape, F32) for array in (encoder, up_proj, down_turned, readout)]
        + [pltpu.SemaphoreType.DMA((4,))],
        compiler_params=pltpu.CompilerParams(vmem_limit_bytes=BIG),
        cost_estimate=QUICK,
        name="pack",
    )(encoder, up_proj, down_turned, readout)


def to_lines(array, wide):
    if wide == 8:
        return array
    lines, width = array.shape[2:]
    return jnp.moveaxis(jnp.moveaxis(array, 1, 0).reshape(GROUPS, 8, LINES, width), 0, 1)


def side_to_lines(side, wide):
    if wide == 8:
        return side
    enc_rows, read_rows = IN // wide, D // (GROUPS * wide)
    enc = to_rows(side[:, :, :enc_rows], 32)
    read = to_rows(side[:, :, enc_rows : enc_rows + read_rows], 16)
    return jnp.concatenate([enc, read, jnp.zeros((8, GROUPS, 16, 128), side.dtype)], axis=2)


def to_rows(array, rows):
    return jnp.moveaxis(jnp.moveaxis(array, 1, 0).reshape(GROUPS, 8, rows, array.shape[3]), 0, 1)


def from_rows(array, wide):
    rows, width = array.shape[2:]
    return jnp.moveaxis(jnp.moveaxis(array, 1, 0).reshape(GROUPS, wide, 8 * rows // wide, width), 0, 1)


def early_from_lines(array, wide):
    if wide == 8:
        return array
    main = from_rows(array[..., :384], wide)
    enc = from_rows(array[:, :, :32, 384:], wide)
    read = from_rows(array[:, :, 32:48, 384:], wide)
    spare = main.shape[2] - enc.shape[2] - read.shape[2]
    side = jnp.concatenate([enc, read, jnp.zeros((wide, GROUPS, spare, 128), array.dtype)], axis=2)
    return jnp.concatenate([main, side], axis=3)


ORDERS = ((1, 2, 3, 4), (2, 3, 1, 4), (3, 1, 2, 4))
DIMS = ((1, 2, 3, 4), (2, 1, 3, 4))
CUTS = (640, 512)


def by_relative(array, dims):
    array = array.reshape(2, 2, 2, 2, 2, *array.shape[2:])
    axes = {4: 0, 3: 1, 2: 2, 1: 3}
    turned = jnp.transpose(array, (4, *(axes[bit] for bit in dims), 5, 6))
    turned = turned.reshape(4, 8, *turned.shape[5:])
    return [turned[i] for i in range(4)]


def gather_plain(early, late, wide):
    def gathered(array):
        full = lax.all_gather(array, ("wide", "narrow"), axis=0, tiled=False)
        return full.reshape(wide, GROUPS, *array.shape)

    full = gathered(early)
    full = jnp.concatenate([to_lines(full[..., :384], wide), side_to_lines(full[..., 384:], wide)], axis=3)
    first = by_relative(full, DIMS[0])
    full = to_lines(gathered(late), wide)
    second = [by_relative(part, DIMS[i]) for i, part in enumerate(jnp.split(full, [CUTS[0]], axis=3))]
    return first, sum(second, [])


def joined(array, other):
    return jnp.concatenate([array[None], other[None]], axis=0)


def swap(array, bit):
    count = lax.axis_size("wide") * lax.axis_size("narrow")
    return lax.ppermute(array, ("wide", "narrow"), [(i, i ^ (1 << bit)) for i in range(count)])


def cube(array):
    return array.reshape(2, 2, 2, 2, *array.shape[1:])


def flat(array):
    return array.reshape(8, *array.shape[3:])


def halve_kernel(groups, keep, *refs):
    count = len(groups)
    total = sum(groups)
    flat_refs, refs = refs[:total], refs[total:]
    outs, refs = refs[: count * (1 + keep)], refs[count * (1 + keep) :]
    flat_there, refs = refs[:total], refs[total:]
    held, (in_sems, out_sems) = refs[:-2], refs[-2:]
    starts = [sum(groups[:i]) for i in range(count)]
    order = [(i, side) for side in ((1, 0) if keep else (1,)) for i in range(count)]

    def fetch(i, side):
        half = held[i].shape[0]
        here = pl.ds(side * half, half)
        return [
            pltpu.make_async_copy(
                flat_refs[starts[i] + k].at[here],
                flat_there[starts[i] + k].at[here if keep else pl.ds(0, half)],
                in_sems.at[starts[i] + k, side],
            )
            for k in range(groups[i])
        ]

    def leave(i, side):
        at = i if side else count + i
        return pltpu.make_async_copy(held[at], outs[at], out_sems.at[at])

    fetches = {at: fetch(*at) for at in order}
    for at in order:
        for copy in fetches[at]:
            copy.start()
    for i, side in order:
        for copy in fetches[i, side]:
            copy.wait()
        half = held[i].shape[0]
        here = pl.ds(side * half if keep else 0, half)
        added = sum(ref[here].astype(F32) for ref in flat_there[starts[i] : starts[i] + groups[i]])
        at = i if side else count + i
        held[at][...] = added.astype(held[at].dtype)
        leave(i, side).start()
    for i, side in order:
        leave(i, side).wait()


def halve_far(lists, keep):
    groups = [len(arrays) for arrays in lists]
    sizes = [min(array.shape[0] for array in arrays) for arrays in lists]
    halves = [(size // 2, *arrays[0].shape[1:]) for size, arrays in zip(sizes, lists)]
    kinds = (BF, F32)[: 1 + keep]
    outside = pl.BlockSpec(memory_space=pl.ANY)
    there = [
        pltpu.VMEM((size if keep else size // 2, *array.shape[1:]), array.dtype)
        for size, arrays in zip(sizes, lists)
        for array in arrays
    ]
    outs = pl.pallas_call(
        functools.partial(halve_kernel, groups, keep),
        in_specs=[outside] * sum(groups),
        out_specs=[outside] * (len(kinds) * len(lists)),
        out_shape=[jax.ShapeDtypeStruct(shape, kind) for kind in kinds for shape in halves],
        scratch_shapes=there
        + [pltpu.VMEM(shape, kind) for kind in kinds for shape in halves]
        + [pltpu.SemaphoreType.DMA((sum(groups), 2)), pltpu.SemaphoreType.DMA((len(kinds) * len(lists),))],
        compiler_params=pltpu.CompilerParams(vmem_limit_bytes=20 * MIB),
        cost_estimate=QUICK,
        name="halve_far",
    )(*(array for arrays in lists for array in arrays))
    return outs[: len(lists)], outs[len(lists) :]


def halve_near_kernel(joint, count, *refs):
    column = 0
    for i in range(count):
        first, second = refs[2 * i], refs[2 * i + 1]
        half, width = first.shape[0] // 2, first.shape[2]
        sent, kept = (refs[2 * count], refs[2 * count + 1]) if joint else refs[2 * count + 2 * i : 2 * count + 2 * i + 2]
        there = slice(column, column + width) if joint else slice(None)
        sent[:, :, there] = (first[half:].astype(F32) + second[half:].astype(F32)).astype(BF)
        kept[:, :, there] = first[:half].astype(F32) + second[:half].astype(F32)
        column += width


def halve_near(pairs, joint=False):
    count = len(pairs)
    vmem = pl.BlockSpec(memory_space=pltpu.VMEM)
    halves = [(pair[0].shape[0] // 2, *pair[0].shape[1:]) for pair in pairs]
    if joint:
        halves = [(*halves[0][:2], sum(shape[2] for shape in halves))]
    outs = pl.pallas_call(
        functools.partial(halve_near_kernel, joint, count),
        in_specs=[vmem] * (2 * count),
        out_specs=[vmem] * (2 * len(halves)),
        out_shape=[jax.ShapeDtypeStruct(shape, kind) for shape in halves for kind in (BF, F32)],
        compiler_params=pltpu.CompilerParams(vmem_limit_bytes=12 * MIB),
        cost_estimate=QUICK,
        name="halve_near",
    )(*(array for pair in pairs for array in pair))
    return outs[0::2], outs[1::2]


class Sums:
    def __init__(self, keep, send, orders):
        self.pairs = [(mine, swap(other, 0)) for mine, other in zip(keep, send)]
        self.orders = orders

    def far_step(self, phase, values):
        sent, kept = halve_far(self.pairs, keep=phase > 0)
        sent, values = lax.optimization_barrier((sent, values))
        came = [swap(out, order[phase]) for out, order in zip(sent, self.orders)]
        self.pairs = [(*(pair if phase == 0 else (kept[i],)), came[i]) for i, pair in enumerate(self.pairs)]
        return values

    def step(self, phase, values=(), **how):
        sent, kept = halve_near(self.pairs, **how)
        sent, values = lax.optimization_barrier((sent, values))
        self.pairs = [(mine, swap(out, order[phase])) for mine, out, order in zip(kept, sent, self.orders)]
        return values

    def came(self, values):
        others, values = lax.optimization_barrier(([other for _, other in self.pairs], values))
        self.pairs = [(mine, other) for (mine, _), other in zip(self.pairs, others)]
        return values


def shares_kernel(loss_ref, early_a, early_b, late_a, late_b, early_ref, late_ref, row_ref):
    early = early_a[0] + early_b[0].astype(F32)
    early_ref[...] = early
    late = late_a[0] + late_b[0].astype(F32)
    late_ref[...] = late
    total = jnp.sum(early * early) + jnp.sum(late * late)
    lanes = lax.broadcasted_iota(jnp.int32, (1, 128), 1)
    row_ref[...] = loss_ref[...] + jnp.where(lanes == 0, total, 0.0)


def shares(loss_part, early, late):
    lines = early[0].shape[1]
    vmem = pl.BlockSpec(memory_space=pltpu.VMEM)
    return pl.pallas_call(
        shares_kernel,
        in_specs=[vmem] * 5,
        out_specs=[vmem] * 3,
        out_shape=(
            jax.ShapeDtypeStruct((lines, EARLY), F32),
            jax.ShapeDtypeStruct((lines, LATE), F32),
            jax.ShapeDtypeStruct((1, 128), F32),
        ),
        compiler_params=pltpu.CompilerParams(vmem_limit_bytes=8 * MIB),
        cost_estimate=QUICK,
        name="shares",
    )(loss_part, *early, *late)


def in_order(keep, send, dims):
    both = jnp.stack([keep, send]).reshape(2, 2, 2, 2, 2, *keep.shape[1:])
    turned = jnp.transpose(both, (*(1 + dims.index(bit) for bit in (4, 3, 2, 1)), 0, 5, 6))
    return turned.reshape(8, 4, *keep.shape[1:])


def scatter_sum(blocks):
    return lax.psum_scatter(
        blocks.astype(F32).reshape(-1, blocks.shape[3]), ("wide", "narrow"), scatter_dimension=0, tiled=True
    )


def sum_all(row):
    count = lax.axis_size("wide") * lax.axis_size("narrow")
    bit = 0
    while 1 << bit < count:
        masks = (1, 2, 3) if bit == 1 else (1,)
        others = [lax.ppermute(row, ("wide", "narrow"), [(i, i ^ (mask << bit)) for i in range(count)]) for mask in masks]
        row = sum(others, row)
        bit += len(masks) // 2 + 1
    return row


def body(
    cond_fields,
    target,
    noise_draw,
    noise_sigma,
    grid_to_mesh,
    mesh_edges,
    mesh_to_grid,
    latitude_row,
    level_index,
    encoder,
    up_proj,
    down_proj,
    readout,
    encoder_moment,
    up_moment,
    down_moment,
    readout_moment,
    encoder_second,
    up_second,
    down_second,
    readout_second,
    encoder_average,
    up_average,
    down_average,
    readout_average,
):
    wide_index = lax.axis_index("wide")
    wide = lax.axis_size("wide")
    globe = lax.axis_index("narrow")
    nodes = mesh_edges.shape[0]
    pixels = cond_fields.shape[1]
    all_nodes = nodes * wide
    width = -(-pixels // 128) * 128

    own_place = [wide_index, globe] if wide == 8 else [0, 0]
    place = jnp.stack([*own_place, globe]).astype(jnp.int32)
    early, late = pack(encoder, up_proj, down_proj.T, readout)
    moving = wide == 8
    tie = lax.optimization_barrier
    if moving:
        early_4 = swap(early, 4)

    across = jnp.pad(mesh_to_grid.T - wide_index * nodes, ((0, 0), (0, width - pixels)), constant_values=-1)
    pool, pull = pull_counts(across, nodes)
    if moving:
        early_4, pull = tie((early_4, pull))
        early_1 = joined(early, early_4)
        early_3 = swap(early_1, 3)

    def own(array):
        return lax.dynamic_index_in_dim(jnp.transpose(array, (2, 0, 1)), globe, 1, keepdims=False)

    goal, noise = own(target), own(noise_draw)
    sigma = lax.dynamic_index_in_dim(noise_sigma, globe, 0, keepdims=False)
    square = sigma * sigma
    c_in = lax.rsqrt(square + 1.0)
    if moving:
        early_3, goal, noise = tie((early_3, goal, noise))
        both = joined(early_1, early_3)
        both, goal, noise = tie((both, goal, noise))
        early_2 = swap(both, 2)
    noisy = goal + sigma * noise
    if moving:
        noisy, late = tie((noisy, late))
        late_4 = swap(late, 4)
    grid = jnp.concatenate([own(cond_fields), (c_in * noisy).astype(BF)], axis=0)
    grid = jnp.pad(grid, ((0, 0), (0, width - pixels)))
    edges = mesh_edges.T
    slot_rows = jnp.where(edges >= 0, (edges - wide_index * nodes + nodes + all_nodes) % all_nodes, -1)

    def halo(sums):
        low = sums.astype(BF)
        ring = [(i, (i + 1) % wide) for i in range(wide)]
        return lax.ppermute(low, "wide", ring), lax.ppermute(low, "wide", [(j, i) for i, j in ring])

    if moving:
        sums = grid_sums(grid, grid_to_mesh.T - wide_index * pixels)
        before, after = halo(sums)
        early_2, sums = tie((early_2, sums))
        quad, late_1 = joined(both, early_2), joined(late, late_4)
        quad, late_1, slot_rows = tie((quad, late_1, slot_rows))
        early_0 = swap(quad, 1)
        late_3 = swap(late_1, 3)
        bias = counts(slot_rows)
        bias, late_3 = tie((bias, late_3))
        both = joined(late_1, late_3)
        parts = [both[..., : CUTS[0]], both[..., CUTS[0] :]]
        parts, early_0, before, after = tie((parts, early_0, before, after))
        got = [swap(parts[0], 2), swap(parts[1], 1)]
        halves = [flat(quad), flat(early_0)]
        gathered = halves + [swap(half, 0) for half in halves]
    else:
        gathered, late_full = gather_plain(early, late, wide)
        sums = grid_sums(grid, grid_to_mesh.T - wide_index * pixels)
        bias = counts(slot_rows)
        before, after = halo(sums)

    state0, rows, normed, early_full = encode(place, gathered, before, sums, after)
    if moving:
        got, normed = tie((got, normed))
        parts = [joined(part, one) for part, one in zip(parts, got)]
        parts, normed = tie((parts, normed))
        got = [swap(parts[0], 1), swap(parts[1], 2)]
        halves = [flat(part) for part in parts]
        others = [swap(half, 0) for half in halves]
    mixed, probs, query, pair, inverse = attend(normed, early_full, bias)
    if moving:
        mixed, got, others = tie((mixed, got, others))
        late_full = []
        for half, one, other in zip(halves, got, others):
            late_full += [half, flat(one), other, swap(flat(one), 0)]
    *blocks, grad_state, grad_mixed, grad_scaled, inner, grad_dec, loss_part = feed(
        place, noise_sigma,
        late_full, early_full, state0, mixed, pool, pull, inverse, noisy, goal, latitude_row[None, :], level_index[:, None],
    )
    keep_late, send_late = blocks[:3], blocks[3:]
    if moving:
        late_sum = Sums(keep_late, send_late, ORDERS)
    first_heads = unmix(0, 1, probs, query, pair, grad_mixed, grad_scaled, inner, inverse)
    if moving:
        query, first_heads = late_sum.far_step(0, (query, first_heads))
    last_heads = unmix(1, 3, probs, query, pair, grad_mixed, grad_scaled, inner, inverse)
    if moving:
        grad_state, last_heads = late_sum.far_step(1, (grad_state, last_heads))
    *blocks, = give_back(
        place, early_full, first_heads, last_heads, grad_state, rows, normed, before, sums, after, grad_dec
    )
    keep_early, send_early = blocks[:2], blocks[2:]
    if moving:
        keep_early, send_early = late_sum.came((keep_early, send_early))
        early_sum = Sums(keep_early, send_early, DIMS)
        late_sum.pairs = early_sum.step(0, late_sum.pairs)
        late_sum.step(2)
        late_sum.pairs = early_sum.step(1, late_sum.pairs)
        late_sum.step(3, joint=True)
        early_sum.step(2, joint=True)
        early_sum.step(3)
        share_early, share_late, row = shares(loss_part, early_sum.pairs[0], late_sum.pairs[0])
    else:
        late_lines = jnp.concatenate([in_order(keep_late[i], send_late[i], ORDERS[i]) for i in range(3)], axis=3)
        early_lines = jnp.concatenate([in_order(keep_early[i], send_early[i], DIMS[i]) for i in range(2)], axis=3)
        share_late = scatter_sum(from_rows(late_lines, wide))
        share_early = scatter_sum(early_from_lines(early_lines, wide))
        squares = jnp.sum(share_early * share_early) + jnp.sum(share_late * share_late)
        row = loss_part + jnp.where(lax.broadcasted_iota(jnp.int32, (1, 128), 1) == 0, squares, 0.0)
    row = sum_all(row)
    states = [
        (encoder, encoder_moment, encoder_second, encoder_average),
        (up_proj, up_moment, up_second, up_average),
        (down_proj.T, down_moment.T, down_second.T, down_average.T),
        (readout, readout_moment, readout_second, readout_average),
    ]
    news = list(adam(row, share_early, share_late, states))
    news[10:15] = [array.T for array in news[10:15]]
    return (news[20][0, 0], news[20][0, 1], *news[:20])


def solution(mesh):
    if mesh.shape["narrow"] != GROUPS or MB != GROUPS:
        raise ValueError("narrow size")
    by_pixel = P(None, "wide", None)
    pair = P("wide", "narrow")
    weights = (pair, pair, P("narrow", "wide"), P(("narrow", "wide"), None))
    placed = (by_pixel, by_pixel, by_pixel, P()) + (P("wide", None),) * 3 + (P("wide"), P()) + weights * 4
    given = (P(), P())
    for spec in weights:
        given = given + (spec,) * 5
    return jax.shard_map(body, mesh=mesh, in_specs=placed, out_specs=given, check_vma=False)
```

```python
import functools
import math

import jax
import jax.numpy as jnp
from jax import lax
from jax.experimental import pallas as pl
from jax.experimental.pallas import tpu as pltpu
from jax.sharding import PartitionSpec as P

D = 512
HEADS = 4
HEAD_DIM = 128
OUT = 84
IN = 256
LEVELS = 13
KM = 16
KG = 8
KD = 3
STEPS_DONE = 7
MB = 4
GROUPS = 4
HID = 512
ROWS = 8
LINES = 64
EARLY = 512
LATE = 1152
BAND = 256
WINDOW = 1280
NEAR = 1536

clip_norm = 0.001
beta_one = 0.9
beta_two = 0.999
epsilon = 1e-08
learn_rate = 0.04
weight_decay = 0.1
average_decay = 0.9

BF = jnp.bfloat16
F32 = jnp.float32
MIB = 1024 * 1024
QUICK = pl.CostEstimate(flops=1000, bytes_accessed=1000, transcendentals=0)
BIG = 60 * MIB


def mm(left, right):
    return jnp.dot(left, right, preferred_element_type=F32)


def mm_nt(left, right):
    return lax.dot_general(left, right, (((1,), (1,)), ((), ())), preferred_element_type=F32)


def mm_tn(left, right):
    return lax.dot_general(left, right, (((0,), (0,)), ((), ())), preferred_element_type=F32)


def split_two(value):
    high = value.astype(BF)
    return high, (value - high.astype(F32)).astype(BF)


def norm_parts(rows_low):
    values = rows_low.astype(F32)
    center = values - jnp.mean(values, axis=-1, keepdims=True)
    inverse = lax.rsqrt(jnp.mean(center * center, axis=-1, keepdims=True) + 1e-05)
    return center * inverse, inverse


def norm_pull(grad_out, normal, inverse, gain):
    scaled = grad_out * gain
    inner = (
        scaled
        - jnp.mean(scaled, axis=-1, keepdims=True)
        - normal * jnp.mean(scaled * normal, axis=-1, keepdims=True)
    )
    return inner * inverse, jnp.sum(grad_out * normal, axis=0, keepdims=True)


class Leaving:
    def __init__(self, sems):
        self.sems, self.copies = sems, []

    def __call__(self, source, there):
        self.copies.append(pltpu.make_async_copy(source, there, self.sems.at[len(self.copies)]))
        self.copies[-1].start()

    def wait(self):
        for copy in self.copies:
            copy.wait()


def sums_kernel(grid_ref, pixels_ref, sums_ref, count_ref):
    width, nodes = count_ref.shape
    step = 32
    picks = [jnp.broadcast_to(pixels_ref[k : k + 1, :], (step, nodes)) for k in range(KG)]
    rows = lax.broadcasted_iota(jnp.int32, (step, nodes), 0)

    def count(i, _):
        at = pl.multiple_of(i * step, step)
        total = jnp.zeros((step, nodes), F32)
        for pick in picks:
            total = total + jnp.where(pick - at == rows, 1.0, 0.0)
        count_ref[pl.ds(at, step), :] = total.astype(BF)
        return 0

    lax.fori_loop(0, width // step, count, 0)
    sums_ref[...] = mm(grid_ref[...], count_ref[...])


def grid_sums(grid, pixel_rows):
    nodes, width = pixel_rows.shape[1], grid.shape[1]
    return pl.pallas_call(
        sums_kernel,
        out_shape=jax.ShapeDtypeStruct((IN, nodes), F32),
        scratch_shapes=[pltpu.VMEM((width, nodes), BF)],
        compiler_params=pltpu.CompilerParams(vmem_limit_bytes=16 * 1024 * 1024),
        cost_estimate=QUICK,
        name="grid_sums",
    )(grid, pixel_rows)


def pull_kernel(across_ref, pool_ref, pull_ref):
    nodes, width = pull_ref.shape
    across = across_ref[...]

    def count_across(i, _):
        at = pl.multiple_of(i * 128, 128)
        rows = lax.broadcasted_iota(jnp.int32, (128, width), 0) + at
        total = jnp.zeros((128, width), F32)
        for k in range(KD):
            total = total + jnp.where(across[k : k + 1, :] == rows, 1.0, 0.0)
        pull_ref[pl.ds(at, 128), :] = total.astype(BF)
        pool_ref[:, pl.ds(at, 128)] = total.T.astype(BF)
        return 0

    lax.fori_loop(0, nodes // 128, count_across, 0)


def pull_counts(across_rows, nodes):
    width = across_rows.shape[1]
    return pl.pallas_call(
        pull_kernel,
        out_shape=(jax.ShapeDtypeStruct((width, nodes), BF), jax.ShapeDtypeStruct((nodes, width), BF)),
        compiler_params=pltpu.CompilerParams(vmem_limit_bytes=BIG),
        cost_estimate=QUICK,
        name="pull_counts",
    )(across_rows)


def counts_kernel(slots_ref, bias_out, bias_ref, sems):
    nodes = slots_ref.shape[1]
    step = 64
    leave = Leaving(sems)
    for band in range(nodes // BAND):
        low = band * BAND
        picks = slots_ref[:, low : low + BAND] - low
        rows = lax.broadcasted_iota(jnp.int32, (step, BAND), 0)
        alike = jnp.zeros((KM, BAND), F32)
        for k in range(KM):
            alike = alike + jnp.where(picks == picks[k : k + 1, :], 1.0, 0.0)
        weight = jnp.log2(alike)

        def count_slots(i, _):
            at = pl.multiple_of(i * step, step)
            value = jnp.full((step, BAND), -1e30, F32)
            for k in range(KM):
                value = jnp.where(picks[k : k + 1, :] - at == rows, weight[k : k + 1, :], value)
            bias_ref[band, pl.ds(at, step), :] = value
            return 0

        for part in range(2):
            half = WINDOW // step // 2
            lax.fori_loop(part * half, (part + 1) * half, count_slots, 0)
            here = slice(part * half * step, (part + 1) * half * step)
            leave(bias_ref.at[band, here], bias_out.at[band, here])
    leave.wait()


def counts(slot_rows):
    nodes = slot_rows.shape[1]
    shape = jax.ShapeDtypeStruct((nodes // BAND, WINDOW, BAND), F32)
    return pl.pallas_call(
        counts_kernel,
        out_specs=pl.BlockSpec(memory_space=pltpu.HBM),
        out_shape=shape,
        scratch_shapes=[pltpu.VMEM(shape.shape, shape.dtype), pltpu.SemaphoreType.DMA((4,))],
        compiler_params=pltpu.CompilerParams(vmem_limit_bytes=BIG),
        cost_estimate=QUICK,
        name="counts",
    )(slot_rows)


def blocks_of(place_ref, dims, refs):
    own_wide, own_narrow = place_ref[0], place_ref[1]
    found = []
    for side in range(2):
        for j in range(16):
            bits = dict(zip(dims, ((j >> 3) & 1, (j >> 2) & 1, (j >> 1) & 1, j & 1)))
            wide = own_wide ^ (bits[4] * 4 + bits[3] * 2 + bits[2])
            narrow = own_narrow ^ (bits[1] * 2 + side)
            found.append((wide, narrow, refs[2 * side + (j >> 3)].at[j & 7]))
    return found


def block_at(dims, part, wide):
    bits = {1: part, 2: wide & 1, 3: (wide >> 1) & 1, 4: wide >> 2}
    return ((bits[dims[0]] * 2 + bits[dims[1]]) * 2 + bits[dims[2]]) * 2 + bits[dims[3]]


def fetch_early(place_ref, refs, early, sems):
    return [
        pltpu.make_async_copy(source, early.at[wide, narrow], sems.at[i])
        for i, (wide, narrow, source) in enumerate(blocks_of(place_ref, DIMS[0], refs))
    ]


def enc_of(early):
    return jnp.concatenate([early[:, n, 0:32, 384:512].reshape(IN, 128) for n in range(GROUPS)], axis=1)


def dec_of(early):
    return jnp.concatenate([early[:, n, 32:48, 384:512].reshape(128, 128) for n in range(GROUPS)], axis=0)


def query_of(early):
    return jnp.concatenate([early[:, n, :, 0:128].reshape(D, 128) for n in range(GROUPS)], axis=1)


def pair_of(early):
    return jnp.concatenate([early[:, n, :, 128:384].reshape(D, 256) for n in range(GROUPS)], axis=1)


def encode_kernel(
    place_ref, a_0, a_1, a_2, a_3, before_ref, sums_ref, after_ref,
    state_ref, rows_ref, normed_ref, early_ref,
    early, state, rows_all, normed_all, sems, out_sems,
):
    copies = fetch_early(place_ref, (a_0, a_1, a_2, a_3), early, sems)
    for copy in copies:
        copy.start()
    for copy in copies:
        copy.wait()
    leave = Leaving(out_sems)
    leave(early, early_ref)
    gain = dec_of(early).astype(F32).T[OUT : OUT + 1, :]
    enc = enc_of(early)
    for block, ref in enumerate((before_ref, sums_ref, after_ref)):
        here = slice(block * 512, block * 512 + 512)
        if block == 1:
            high, low = split_two(ref[...])
            embedded = (mm_tn(high, enc) + mm_tn(low, enc)) * (1.0 / KG)
            state[...] = embedded
            leave(state, state_ref)
        else:
            embedded = mm_tn(ref[...], enc) * (1.0 / KG)
        rows = embedded.astype(BF)
        rows_all[here, :] = rows
        leave(rows_all.at[here], rows_ref.at[here])
        normal, _inverse = norm_parts(rows)
        normed_all[here, :] = (normal * gain).astype(BF)
        leave(normed_all.at[here], normed_ref.at[here])
    leave.wait()


def encode(place, gathered, before, sums, after):
    nodes = sums.shape[1]
    vmem = pl.BlockSpec(memory_space=pltpu.VMEM)
    outside = pl.BlockSpec(memory_space=pltpu.HBM)
    shapes = (
        jax.ShapeDtypeStruct((nodes, D), F32),
        jax.ShapeDtypeStruct((NEAR, D), BF),
        jax.ShapeDtypeStruct((NEAR, D), BF),
        jax.ShapeDtypeStruct((8, GROUPS, LINES, EARLY), BF),
    )
    return pl.pallas_call(
        encode_kernel,
        in_specs=[pl.BlockSpec(memory_space=pltpu.SMEM)] + [outside] * 4 + [vmem] * 3,
        out_specs=[outside] * 4,
        out_shape=shapes,
        scratch_shapes=[pltpu.VMEM((8, GROUPS, LINES, EARLY), BF)]
        + [pltpu.VMEM(shape.shape, shape.dtype) for shape in shapes[:3]]
        + [pltpu.SemaphoreType.DMA((32,)), pltpu.SemaphoreType.DMA((8,))],
        compiler_params=pltpu.CompilerParams(vmem_limit_bytes=BIG),
        cost_estimate=QUICK,
        name="encode",
    )(place, *gathered, before, sums, after)


def attend_kernel(
    normed_in, early_in, bias_in, mixed_ref, probs_ref, query_ref, pair_ref, inverse_ref,
    normed, early, bias, query_all, pair_all, mixed_all, probs, inverse_all, sems, out_sems,
):
    def weight_copy(h):
        return pltpu.make_async_copy(early_in.at[:, h, :, 0:384], early.at[h], sems.at[h])

    normed_copy = pltpu.make_async_copy(normed_in, normed, sems.at[4])
    bias_copies = [pltpu.make_async_copy(bias_in.at[i], bias.at[i], sems.at[5 + i]) for i in range(2)]
    weight_copy(0).start()
    normed_copy.start()
    bias_copies[0].start()
    bias_copies[1].start()
    for h in range(1, HEADS):
        weight_copy(h).start()
    normed_copy.wait()
    factor = HEAD_DIM ** (-0.5) * math.log2(math.e)

    def pair_leave(h):
        return pltpu.make_async_copy(pair_all.at[h], pair_ref.at[h], out_sems.at[8 + h])

    def probs_leave(h):
        return pltpu.make_async_copy(probs.at[h], probs_ref.at[h], out_sems.at[4 + h])

    for h in range(HEADS):
        lanes = slice(h * HEAD_DIM, h * HEAD_DIM + HEAD_DIM)
        weight_copy(h).wait()
        weights = early[h].reshape(D, 384)
        pair_all[h] = mm(normed[...], weights[:, 128:384]).astype(BF)
        query_all[:, lanes] = mm(normed[512:1024, :], weights[:, 0:128]).astype(BF)
        if h == 0:
            bias_copies[0].wait()
            bias_copies[1].wait()
        for band in range(2):
            at = band * BAND
            near, here = slice(at, at + WINDOW), slice(at, at + BAND)
            part = mm_nt(pair_all[h, near, :HEAD_DIM], query_all[here, lanes]) * factor + bias[band]
            expo = jnp.exp2(part - jnp.max(part, axis=0, keepdims=True))
            inverse = 1.0 / jnp.sum(expo, axis=0, keepdims=True)
            low = expo.astype(BF)
            probs[h, near, here] = low
            inverse_all[h : h + 1, here] = inverse
            column = jnp.broadcast_to(inverse, (8, BAND)).T[:, 0:1]
            mixed_all[here, lanes] = mm_tn(low, pair_all[h, near, HEAD_DIM:]) * column
        probs_leave(h).start()
        pair_leave(h).start()
    inverse_all[HEADS:8, :] = jnp.zeros((8 - HEADS, inverse_all.shape[1]), F32)
    leave = Leaving(out_sems)
    leave(mixed_all, mixed_ref)
    leave(query_all, query_ref)
    leave(inverse_all, inverse_ref)
    leave.wait()
    for h in range(HEADS):
        pair_leave(h).wait()
        probs_leave(h).wait()


def attend(normed, early, bias):
    nodes = normed.shape[0] // 3
    outside = pl.BlockSpec(memory_space=pltpu.HBM)
    return pl.pallas_call(
        attend_kernel,
        in_specs=[outside] * 3,
        out_specs=[outside] * 5,
        out_shape=(
            jax.ShapeDtypeStruct((nodes, D), F32),
            jax.ShapeDtypeStruct((HEADS, NEAR, nodes), BF),
            jax.ShapeDtypeStruct((nodes, D), BF),
            jax.ShapeDtypeStruct((HEADS, NEAR, 2 * HEAD_DIM), BF),
            jax.ShapeDtypeStruct((8, nodes), F32),
        ),
        scratch_shapes=[
            pltpu.VMEM((NEAR, D), BF),
            pltpu.VMEM((GROUPS, 8, LINES, 384), BF),
            pltpu.VMEM((2, WINDOW, BAND), F32),
            pltpu.VMEM((nodes, D), BF),
            pltpu.VMEM((HEADS, NEAR, 2 * HEAD_DIM), BF),
            pltpu.VMEM((nodes, D), F32),
            pltpu.VMEM((HEADS, NEAR, nodes), BF),
            pltpu.VMEM((8, nodes), F32),
            pltpu.SemaphoreType.DMA((7,)),
            pltpu.SemaphoreType.DMA((12,)),
        ],
        compiler_params=pltpu.CompilerParams(vmem_limit_bytes=BIG),
        cost_estimate=QUICK,
        name="attend",
    )(normed, early, bias)


def feed_kernel(
    place_ref, sigma_ref, a_0, a_1, a_2, a_3, b_0, b_1, b_2, b_3, early_ref, state_in, mixed_in, pool_in, pull_in, inverse_ref, noisy_ref, target_ref, lat_ref, level_ref,
    keep_0, keep_1, keep_2, send_0, send_1, send_2, grad_state_out, grad_mixed_out, grad_scaled_out, inner_ref, grad_dec_ref, loss_ref,
    late, dec, pre_ref, act_ref, grad_pred_ref,
    state_ref, mixed_ref, pool_ref, pull_ref, keep_ref, send_ref, grad_state_ref, grad_mixed_ref, grad_scaled_ref, sems, group_sems, out_sems,
):
    own_wide, own_narrow = place_ref[0], place_ref[1]

    refs = (a_0, a_1, a_2, a_3), (b_0, b_1, b_2, b_3)

    def fetch(colour, columns, first, sem):
        there = slice(first, first + columns.stop - columns.start)
        return [
            pltpu.make_async_copy(source.at[:, columns], late.at[wide, narrow, :, there], sem(narrow, i))
            for i, (wide, narrow, source) in enumerate(blocks_of(place_ref, DIMS[colour], refs[colour]))
        ]

    def group(n, columns, row):
        return pltpu.make_async_copy(late.at[:, n, :, columns], late.at[:, n, :, columns], group_sems.at[row, n])

    hidden, outer, lower = slice(0, 512), slice(512, 640), slice(640, 1152)
    pairs = [(state_in, state_ref), (mixed_in, mixed_ref), (early_ref.at[:, :, 32:48, 384:512], dec)]
    small = [pltpu.make_async_copy(source, there, sems.at[32 + i]) for i, (source, there) in enumerate(pairs)]
    small += fetch(0, outer, 512, lambda n, i: sems.at[i])
    pool_copy = pltpu.make_async_copy(pool_in, pool_ref, sems.at[35])
    pull_copy = pltpu.make_async_copy(pull_in, pull_ref, sems.at[36])
    first = fetch(0, hidden, 0, lambda n, i: group_sems.at[0, n])
    second = fetch(1, slice(0, 512), 640, lambda n, i: group_sems.at[1, n])
    for copy in (*small, *first, *second, pool_copy, pull_copy):
        copy.start()
    for copy in small:
        copy.wait()
    dec_turned = jnp.concatenate([dec[:, n].reshape(128, 128) for n in range(GROUPS)], axis=0).astype(F32).T
    gain = dec_turned[OUT + 1 : OUT + 2, :]
    rows = lax.broadcasted_iota(jnp.int32, (128, 1), 0)
    dec_only = jnp.where(rows < OUT, dec_turned, 0.0).astype(BF)
    out_full = jnp.concatenate([late[:, n, :, 512:640].reshape(D, 128) for n in range(GROUPS)], axis=1)
    mixed = mixed_ref[...].astype(BF)
    state1 = state_ref[...] + mm_nt(mixed, out_full)
    normal, inverse = norm_parts(state1.astype(BF))
    normed = (normal * gain).astype(BF)

    def forward(i, state):
        n = i ^ own_narrow
        group(n, hidden, 0).wait()
        pre = mm(normed, late[:, n, :, 0:512].reshape(D, HID))
        pre_ref[n] = pre
        act = (pre / (1.0 + jnp.exp(-pre))).astype(BF)
        act_ref[n] = act
        group(n, lower, 1).wait()
        return state + mm_nt(act, late[:, n, :, 640:1152].reshape(D, HID))

    state2 = state1
    for i in range(GROUPS):
        state2 = forward(i, state2)
    high, low = split_two(state2)
    pool_copy.wait()
    pull_copy.wait()
    pool = pool_ref[...]
    pooled = ((mm(pool, high) + mm(pool, low)) / KD).astype(BF)
    pixels = noisy_ref.shape[1]
    pred = mm_nt(dec_only, pooled)[:OUT, :pixels]
    sigma = jnp.full((1, 1), sigma_ref[place_ref[2]], F32)
    square = sigma * sigma
    c_skip = 1.0 / (square + 1.0)
    c_out = sigma * lax.rsqrt(square + 1.0)
    lam = (square + 1.0) / square
    error = c_skip * noisy_ref[...] + c_out * pred - target_ref[...]
    weight = jnp.cos((lat_ref[...].astype(F32) - 90.0) * (math.pi / 180.0)) * ((jnp.broadcast_to(level_ref[...].astype(F32), (8, OUT)).T[:, 0:1] + 1.0) / LEVELS)
    weighted = lam * weight
    first_globe = (jnp.full((1, 1), place_ref[2], jnp.int32) == 0).astype(F32)
    lanes = lax.broadcasted_iota(jnp.int32, (1, 128), 1)
    loss_ref[...] = jnp.where(lanes == 1, jnp.sum(weighted * error * error), 0.0) + jnp.where(
        lanes == 2, jnp.sum(weight) * first_globe, 0.0
    )
    grad_pred_ref[...] = jnp.zeros_like(grad_pred_ref)
    grad_pred_ref[:OUT, :pixels] = 2.0 * c_out * weighted * error
    grad_pred = grad_pred_ref[...].astype(BF)
    grad_dec_ref[...] = mm(grad_pred, pooled)
    up_high, up_low = split_two(mm_nt(pull_ref[...], grad_pred))
    grad_state2 = (mm(up_high, dec_only) + mm(up_low, dec_only)) / KD
    grad_low = grad_state2.astype(BF)
    grad_turned = grad_state2.T.astype(BF)
    normed_turned = normed.astype(F32).T.astype(BF)

    def put(out_ref, side, part, first, value):
        done = 0
        while done < value.shape[1]:
            colour, column = divmod(first + done, 384)
            count = min(384 - column, value.shape[1] - done)
            for w in range(8):
                out_ref[colour, block_at(ORDERS[colour], part, w ^ own_wide), :, column : column + count] = value[
                    w * LINES : (w + 1) * LINES, done : done + count
                ]
            done += count

    def backward(part, grad_n, out_ref, side):
        n = (part * 2 + side) ^ own_narrow
        act = act_ref[n]
        pre = pre_ref[n]
        put(out_ref, side, part, 640, mm(grad_turned, act).astype(BF))
        grad_act = mm(grad_low, late[:, n, :, 640:1152].reshape(D, HID))
        logistic = 1.0 / (1.0 + jnp.exp(-pre))
        grad_pre = (grad_act * logistic * (1.0 + pre * (1.0 - logistic))).astype(BF)
        put(out_ref, side, part, 0, mm(normed_turned, grad_pre).astype(BF))
        return grad_n + mm_nt(grad_pre, late[:, n, :, 0:512].reshape(D, HID))

    grad_n = jnp.zeros((D, D), F32)
    leaving = []

    def leave(source, there):
        leaving.append(pltpu.make_async_copy(source, there, out_sems.at[len(leaving)]))
        leaving[-1].start()

    sides = ((1, send_ref, (send_0, send_1, send_2)), (0, keep_ref, (keep_0, keep_1, keep_2)))
    for side, out_ref, there in sides:
        for part in range(2):
            grad_n = backward(part, grad_n, out_ref, side)
        leave(out_ref.at[0], there[0])
        leave(out_ref.at[2], there[2])
    back, gain_grad = norm_pull(grad_n, normal, inverse, gain)
    grad_dec_ref[OUT + 1 : OUT + 2, :] = gain_grad
    grad_state1 = grad_state2 + back
    grad_state_ref[...] = grad_state1
    leave(grad_state_ref, grad_state_out)
    grad_low1 = grad_state1.astype(BF)
    act_ref[0] = mixed
    grad_turned1 = grad_state1.T.astype(BF)
    for side, out_ref, there in sides:
        for part in range(2):
            lane = pl.multiple_of(((part * 2 + side) ^ own_narrow) * 128, 128)
            put(out_ref, side, part, 512, mm(grad_turned1, act_ref[0, :, pl.ds(lane, 128)]).astype(BF))
        leave(out_ref.at[1], there[1])
    grad_mixed = mm(grad_low1, out_full)
    grad_mixed_ref[...] = grad_mixed.astype(BF)
    leave(grad_mixed_ref, grad_mixed_out)
    columns = inverse_ref[...].T
    lanes = lax.broadcasted_iota(jnp.int32, (1, 128), 1)
    inner = jnp.zeros((grad_mixed.shape[0], 128), F32)
    for h in range(HEADS):
        here = slice(h * HEAD_DIM, h * HEAD_DIM + HEAD_DIM)
        grad = grad_mixed[:, here]
        grad_scaled_ref[:, here] = (grad * columns[:, h : h + 1]).astype(BF)
        inner = jnp.where(lanes == h, jnp.sum(grad * mixed_ref[:, here], axis=1, keepdims=True), inner)
    leave(grad_scaled_ref, grad_scaled_out)
    inner_ref[...] = inner.T[0:8, :]
    for copy in leaving:
        copy.wait()


def feed(place, sigma, late, early, state0, mixed, pool, pull, inverse, noisy, target, lat, level):
    nodes = state0.shape[0]
    width = pool.shape[0]
    vmem = pl.BlockSpec(memory_space=pltpu.VMEM)
    outside = pl.BlockSpec(memory_space=pltpu.HBM)
    return pl.pallas_call(
        feed_kernel,
        in_specs=[pl.BlockSpec(memory_space=pltpu.SMEM)] * 2 + [outside] * 13 + [vmem] * 5,
        out_specs=[outside] * 9 + [vmem] * 3,
        out_shape=(
            *([jax.ShapeDtypeStruct((16, LINES, 384), BF)] * 6),
            jax.ShapeDtypeStruct((nodes, D), F32),
            jax.ShapeDtypeStruct((nodes, D), BF),
            jax.ShapeDtypeStruct((nodes, D), BF),
            jax.ShapeDtypeStruct((8, nodes), F32),
            jax.ShapeDtypeStruct((128, D), F32),
            jax.ShapeDtypeStruct((1, 128), F32),
        ),
        scratch_shapes=[
            pltpu.VMEM((8, GROUPS, LINES, LATE), BF),
            pltpu.VMEM((8, GROUPS, 16, 128), BF),
            pltpu.VMEM((GROUPS, nodes, HID), F32),
            pltpu.VMEM((GROUPS, nodes, HID), BF),
            pltpu.VMEM((128, width), F32),
            pltpu.VMEM((nodes, D), F32),
            pltpu.VMEM((nodes, D), F32),
            pltpu.VMEM((width, nodes), BF),
            pltpu.VMEM((nodes, width), BF),
            pltpu.VMEM((3, 16, LINES, 384), BF),
            pltpu.VMEM((3, 16, LINES, 384), BF),
            pltpu.VMEM((nodes, D), F32),
            pltpu.VMEM((nodes, D), BF),
            pltpu.VMEM((nodes, D), BF),
            pltpu.SemaphoreType.DMA((37,)),
            pltpu.SemaphoreType.DMA((2, GROUPS)),
            pltpu.SemaphoreType.DMA((9,)),
        ],
        compiler_params=pltpu.CompilerParams(vmem_limit_bytes=BIG),
        cost_estimate=QUICK,
        name="feed",
    )(place, sigma, *late, early, state0, mixed, pool, pull, inverse, noisy, target, lat, level)


def unmix_kernel(probs_ref, query_ref, keys_ref, values_ref, grad_mixed_ref, grad_scaled_ref, inner_ref, inverse_ref,
                 grad_query_ref, grad_pair_ref, grad_scores):
    scale = HEAD_DIM ** (-0.5)
    row = pl.ds(pl.program_id(0), 1)
    inner = inner_ref[row, :]
    factor = inverse_ref[row, :] * scale
    pieces = ((0, 256, 0, 256), (256, 768, 0, 512), (768, 1280, 0, 512), (1280, 1536, 256, 512))
    for low_row, high_row, low_column, high_column in pieces:
        rows, columns = slice(low_row, high_row), slice(low_column, high_column)
        probs = probs_ref[0, rows, columns]
        grad_probs = mm_nt(values_ref[0, rows, :], grad_mixed_ref[columns, :])
        low = (probs.astype(F32) * ((grad_probs - inner[:, columns]) * factor[:, columns])).astype(BF)
        grad_scores[rows, columns] = low
        grad_pair_ref[rows, 0:HEAD_DIM] = mm(low, query_ref[columns, :]).astype(BF)
        grad_pair_ref[rows, HEAD_DIM : 2 * HEAD_DIM] = mm(probs, grad_scaled_ref[columns, :]).astype(BF)
    for at in (0, BAND):
        grad_query_ref[at : at + BAND, :] = mm_tn(
            grad_scores[at : at + WINDOW, at : at + BAND], keys_ref[0, at : at + WINDOW, :]
        ).astype(BF)


def unmix(probs, query, pair, grad_mixed, grad_scaled, inner, inverse):
    nodes = query.shape[0]
    part = pl.BlockSpec((nodes, HEAD_DIM), lambda i: (0, i))
    whole = pl.BlockSpec((8, nodes), lambda i: (0, 0))
    return pl.pallas_call(
        unmix_kernel,
        grid=(HEADS,),
        in_specs=[
            pl.BlockSpec((1, NEAR, nodes), lambda i: (i, 0, 0)),
            part,
            pl.BlockSpec((1, NEAR, HEAD_DIM), lambda i: (i, 0, 0)),
            pl.BlockSpec((1, NEAR, HEAD_DIM), lambda i: (i, 0, 1)),
            part,
            part,
            whole,
            whole,
        ],
        out_specs=(
            pl.BlockSpec((nodes, HEAD_DIM), lambda i: (0, i)),
            pl.BlockSpec((NEAR, 2 * HEAD_DIM), lambda i: (0, i)),
        ),
        out_shape=(
            jax.ShapeDtypeStruct((nodes, HEADS * HEAD_DIM), BF),
            jax.ShapeDtypeStruct((NEAR, HEADS * 2 * HEAD_DIM), BF),
        ),
        scratch_shapes=[pltpu.VMEM((NEAR, nodes), BF)],
        compiler_params=pltpu.CompilerParams(vmem_limit_bytes=BIG),
        cost_estimate=QUICK,
        name="unmix",
    )(probs, query, pair, pair, grad_mixed, grad_scaled, inner, inverse)


def return_kernel(
    place_ref, early_ref, query_in, pair_in,
    grad_state_in, rows_in, normed_in, before_ref, sums_ref, after_ref, grad_dec_ref,
    keep_0, keep_1, send_0, send_1,
    early, normed_ref, rows_ref, grad_state_ref, query_g, pair_g, sems,
):
    pairs = (
        (normed_in, normed_ref),
        (query_in, query_g),
        (pair_in, pair_g),
        (early_ref, early), (rows_in, rows_ref), (grad_state_in, grad_state_ref),
    )
    copies = [pltpu.make_async_copy(source, there, sems.at[i]) for i, (source, there) in enumerate(pairs)]
    for copy in copies:
        copy.start()
    own_wide, own_narrow = place_ref[0], place_ref[1]
    def put(n, colour, column, value, low):
        lines = value.shape[0] // 8
        for side, out_refs in ((1, (send_0, send_1)), (0, (keep_0, keep_1))):

            @pl.when(((n ^ own_narrow) & 1) == side)
            def _():
                part = (n ^ own_narrow) >> 1
                for w in range(8):
                    out_refs[colour][block_at(DIMS[colour], part, w ^ own_wide), low : low + lines, column : column + 128] = value[
                        w * lines : (w + 1) * lines, :
                    ]

    copies[0].wait()
    turned = normed_ref[...].astype(F32).T.astype(BF)
    for copy in copies[1:3]:
        copy.wait()
    weight_query = mm(turned[:, 512:1024], query_g[...]).astype(BF)
    weight_pair = mm(turned, pair_g[...]).astype(BF)
    for n in range(GROUPS):
        put(n, 0, 0, weight_query[:, n * 128 : n * 128 + 128], 0)
        put(n, 0, 128, weight_pair[:, n * 256 : n * 256 + 128], 0)
        put(n, 1, 0, weight_pair[:, n * 256 + 128 : n * 256 + 256], 0)
    for copy in copies[3:]:
        copy.wait()
    gain = dec_of(early).astype(F32).T[OUT : OUT + 1, :]
    pair_weights = pair_of(early)
    grad_enc = jnp.zeros((IN, D), F32)
    gain_grad = jnp.zeros((1, D), F32)
    for block, sums in enumerate((before_ref, sums_ref, after_ref)):
        at = block * 512
        grad_block = mm_nt(pair_g[at : at + 512, :], pair_weights)
        if block == 1:
            grad_block = grad_block + mm_nt(query_g[...], query_of(early))
        normal, inverse = norm_parts(rows_ref[at : at + 512, :])
        back, gain_part = norm_pull(grad_block, normal, inverse, gain)
        gain_grad = gain_grad + gain_part
        if block == 1:
            back = back + grad_state_ref[...]
        back_low = (back * (1.0 / KG)).astype(BF)
        grad_enc = grad_enc + mm(sums[...].astype(BF), back_low)
    grad_enc = grad_enc.astype(BF)
    rows = lax.broadcasted_iota(jnp.int32, (128, 1), 0)
    grad_dec = jnp.where(rows == OUT, gain_grad, grad_dec_ref[...]).T.astype(BF)
    for n in range(GROUPS):
        put(n, 1, 128, grad_enc[:, n * 128 : n * 128 + 128], 0)
        put(n, 1, 128, grad_dec[n * 128 : n * 128 + 128, :], 32)
        put(n, 1, 128, jnp.zeros((128, 128), BF), 48)


def give_back(place, early, heads, grad_state, rows, normed, before, sums, after, grad_dec):
    vmem = pl.BlockSpec(memory_space=pltpu.VMEM)
    outside = pl.BlockSpec(memory_space=pltpu.HBM)
    return pl.pallas_call(
        return_kernel,
        in_specs=[pl.BlockSpec(memory_space=pltpu.SMEM), outside] + [outside] * 5 + [vmem] * 4,
        out_specs=[vmem] * 4,
        out_shape=[jax.ShapeDtypeStruct((16, LINES, 256), BF)] * 4,
        scratch_shapes=[
            pltpu.VMEM((8, GROUPS, LINES, EARLY), BF),
            pltpu.VMEM((NEAR, D), BF),
            pltpu.VMEM((NEAR, D), BF),
            pltpu.VMEM((512, D), F32),
            pltpu.VMEM((512, D), BF),
            pltpu.VMEM((NEAR, 2 * D), BF),
            pltpu.SemaphoreType.DMA((14,)),
        ],
        compiler_params=pltpu.CompilerParams(vmem_limit_bytes=36 * MIB),
        cost_estimate=QUICK,
        name="give_back",
    )(
        place,
        *(
            pltpu.with_memory_space_constraint(array, pltpu.HBM)
            for array in (early, *heads, grad_state, rows, normed)
        ),
        before, sums, after, grad_dec,
    )


def adam_kernel(row_ref, early_ref, late_ref, *refs):
    total = row_ref[0:1, 2:3] * MB
    norm_value = jnp.sqrt(row_ref[0:1, 0:1]) / total
    factor = jnp.minimum(1.0, clip_norm / norm_value) / total
    lanes = lax.broadcasted_iota(jnp.int32, (8, 128), 1)
    refs[36][...] = jnp.where(lanes == 0, row_ref[0:1, 1:2] / total, norm_value)
    fix_one = 1.0 - beta_one**STEPS_DONE
    fix_two = 1.0 - beta_two**STEPS_DONE
    enc_rows, read_rows = refs[0].shape[0], refs[12].shape[0]
    shares = (
        ((early_ref, slice(0, enc_rows), slice(384, 512), slice(None)),),
        ((early_ref, slice(None), slice(0, 384), slice(0, 384)), (late_ref, slice(None), slice(0, 512), slice(384, 896))),
        ((late_ref, slice(None), slice(512, 1152), slice(None)),),
        ((early_ref, slice(enc_rows, enc_rows + read_rows), slice(384, 384 + OUT + 2), slice(None)),),
    )
    for i, pieces in enumerate(shares):
        weight_ref, moment_ref, second_ref, average_ref = refs[4 * i : 4 * i + 4]
        outs = refs[16 + 5 * i : 21 + 5 * i]
        for share_ref, rows, columns, there in pieces:
            grad = share_ref[rows, columns] * factor
            weight = weight_ref[:, there]
            moment = beta_one * moment_ref[:, there] + (1.0 - beta_one) * grad
            second = beta_two * second_ref[:, there] + (1.0 - beta_two) * grad * grad
            weight = weight - learn_rate * (
                moment / fix_one / (jnp.sqrt(second / fix_two) + epsilon) + weight_decay * weight
            )
            outs[0][:, there] = moment
            outs[1][:, there] = second
            outs[2][:, there] = weight
            outs[3][:, there] = average_decay * average_ref[:, there] + (1.0 - average_decay) * weight
            outs[4][:, there] = weight.astype(BF)


def adam(row, early, late, states):
    arrays = [array for state in states for array in state]
    shapes = []
    for state in states:
        shapes += [jax.ShapeDtypeStruct(state[0].shape, F32)] * 4 + [jax.ShapeDtypeStruct(state[0].shape, BF)]
    shapes.append(jax.ShapeDtypeStruct((8, 128), F32))
    vmem = pl.BlockSpec(memory_space=pltpu.VMEM)
    return pl.pallas_call(
        adam_kernel,
        in_specs=[vmem] * 19,
        out_specs=[vmem] * 21,
        out_shape=shapes,
        compiler_params=pltpu.CompilerParams(vmem_limit_bytes=16 * MIB),
        cost_estimate=QUICK,
        name="adam",
    )(row, early, late, *arrays)


def pack_kernel(encoder_in, up_in, down_in, readout_in, early_ref, late_ref, encoder_ref, up_ref, down_ref, readout_ref, sems):
    pairs = ((up_in, up_ref), (encoder_in, encoder_ref), (readout_in, readout_ref), (down_in, down_ref))
    copies = [pltpu.make_async_copy(source, there, sems.at[i]) for i, (source, there) in enumerate(pairs)]
    for copy in copies:
        copy.start()
    for copy in copies:
        copy.wait()
    enc_rows, read_rows = encoder_ref.shape[0], readout_ref.shape[0]
    early_ref[:, 0:384] = up_ref[:, 0:384].astype(BF)
    side = jnp.zeros((early_ref.shape[0] - enc_rows, 128), F32)
    early_ref[enc_rows:, 384:512] = side.astype(BF)
    early_ref[0:enc_rows, 384:512] = encoder_ref[...].astype(BF)
    early_ref[enc_rows : enc_rows + read_rows, 384 : 384 + OUT + 2] = readout_ref[...].astype(BF)
    late_ref[:, 0:512] = up_ref[:, 384:896].astype(BF)
    late_ref[:, 512:1152] = down_ref[...].astype(BF)


def pack(encoder, up_proj, down_turned, readout):
    lines = up_proj.shape[0]
    vmem = pl.BlockSpec(memory_space=pltpu.VMEM)
    outside = pl.BlockSpec(memory_space=pltpu.HBM)
    return pl.pallas_call(
        pack_kernel,
        in_specs=[outside] * 4,
        out_specs=[vmem] * 2,
        out_shape=(jax.ShapeDtypeStruct((lines, EARLY), BF), jax.ShapeDtypeStruct((lines, LATE), BF)),
        scratch_shapes=[pltpu.VMEM(array.shape, F32) for array in (encoder, up_proj, down_turned, readout)]
        + [pltpu.SemaphoreType.DMA((4,))],
        compiler_params=pltpu.CompilerParams(vmem_limit_bytes=BIG),
        cost_estimate=QUICK,
        name="pack",
    )(encoder, up_proj, down_turned, readout)


def to_lines(array, wide):
    if wide == 8:
        return array
    lines, width = array.shape[2:]
    return jnp.moveaxis(jnp.moveaxis(array, 1, 0).reshape(GROUPS, 8, LINES, width), 0, 1)


def side_to_lines(side, wide):
    if wide == 8:
        return side
    enc_rows, read_rows = IN // wide, D // (GROUPS * wide)
    enc = to_rows(side[:, :, :enc_rows], 32)
    read = to_rows(side[:, :, enc_rows : enc_rows + read_rows], 16)
    return jnp.concatenate([enc, read, jnp.zeros((8, GROUPS, 16, 128), side.dtype)], axis=2)


def to_rows(array, rows):
    return jnp.moveaxis(jnp.moveaxis(array, 1, 0).reshape(GROUPS, 8, rows, array.shape[3]), 0, 1)


def from_rows(array, wide):
    rows, width = array.shape[2:]
    return jnp.moveaxis(jnp.moveaxis(array, 1, 0).reshape(GROUPS, wide, 8 * rows // wide, width), 0, 1)


def early_from_lines(array, wide):
    if wide == 8:
        return array
    main = from_rows(array[..., :384], wide)
    enc = from_rows(array[:, :, :32, 384:], wide)
    read = from_rows(array[:, :, 32:48, 384:], wide)
    spare = main.shape[2] - enc.shape[2] - read.shape[2]
    side = jnp.concatenate([enc, read, jnp.zeros((wide, GROUPS, spare, 128), array.dtype)], axis=2)
    return jnp.concatenate([main, side], axis=3)


ORDERS = ((1, 2, 3, 4), (2, 3, 1, 4), (3, 1, 2, 4))
DIMS = ((1, 2, 3, 4), (2, 1, 3, 4))
CUTS = (640, 512)


def by_relative(array, dims):
    array = array.reshape(2, 2, 2, 2, 2, *array.shape[2:])
    axes = {4: 0, 3: 1, 2: 2, 1: 3}
    turned = jnp.transpose(array, (4, *(axes[bit] for bit in dims), 5, 6))
    turned = turned.reshape(4, 8, *turned.shape[5:])
    return [turned[i] for i in range(4)]


def gather_plain(early, late, wide):
    def gathered(array):
        full = lax.all_gather(array, ("wide", "narrow"), axis=0, tiled=False)
        return full.reshape(wide, GROUPS, *array.shape)

    full = gathered(early)
    full = jnp.concatenate([to_lines(full[..., :384], wide), side_to_lines(full[..., 384:], wide)], axis=3)
    first = by_relative(full, DIMS[0])
    full = to_lines(gathered(late), wide)
    second = [by_relative(part, DIMS[i]) for i, part in enumerate(jnp.split(full, [CUTS[0]], axis=3))]
    return first, sum(second, [])


def joined(array, other):
    return jnp.concatenate([array[None], other[None]], axis=0)


def swap(array, bit):
    count = lax.axis_size("wide") * lax.axis_size("narrow")
    return lax.ppermute(array, ("wide", "narrow"), [(i, i ^ (1 << bit)) for i in range(count)])


def cube(array):
    return array.reshape(2, 2, 2, 2, *array.shape[1:])


def flat(array):
    return array.reshape(8, *array.shape[3:])


def halve_kernel(groups, keep, *refs):
    count = len(groups)
    total = sum(groups)
    flat_refs, refs = refs[:total], refs[total:]
    outs, refs = refs[: count * (1 + keep)], refs[count * (1 + keep) :]
    flat_there, refs = refs[:total], refs[total:]
    held, (in_sems, out_sems) = refs[:-2], refs[-2:]
    starts = [sum(groups[:i]) for i in range(count)]
    order = [(i, side) for side in ((1, 0) if keep else (1,)) for i in range(count)]

    def fetch(i, side):
        half = held[i].shape[0]
        here = pl.ds(side * half, half)
        return [
            pltpu.make_async_copy(
                flat_refs[starts[i] + k].at[here],
                flat_there[starts[i] + k].at[here if keep else pl.ds(0, half)],
                in_sems.at[starts[i] + k, side],
            )
            for k in range(groups[i])
        ]

    def leave(i, side):
        at = i if side else count + i
        return pltpu.make_async_copy(held[at], outs[at], out_sems.at[at])

    fetches = {at: fetch(*at) for at in order}
    for at in order:
        for copy in fetches[at]:
            copy.start()
    for i, side in order:
        for copy in fetches[i, side]:
            copy.wait()
        half = held[i].shape[0]
        here = pl.ds(side * half if keep else 0, half)
        added = sum(ref[here].astype(F32) for ref in flat_there[starts[i] : starts[i] + groups[i]])
        at = i if side else count + i
        held[at][...] = added.astype(held[at].dtype)
        leave(i, side).start()
    for i, side in order:
        leave(i, side).wait()


def halve_far(lists, keep):
    groups = [len(arrays) for arrays in lists]
    sizes = [min(array.shape[0] for array in arrays) for arrays in lists]
    halves = [(size // 2, *arrays[0].shape[1:]) for size, arrays in zip(sizes, lists)]
    kinds = (BF, F32)[: 1 + keep]
    outside = pl.BlockSpec(memory_space=pl.ANY)
    there = [
        pltpu.VMEM((size if keep else size // 2, *array.shape[1:]), array.dtype)
        for size, arrays in zip(sizes, lists)
        for array in arrays
    ]
    outs = pl.pallas_call(
        functools.partial(halve_kernel, groups, keep),
        in_specs=[outside] * sum(groups),
        out_specs=[outside] * (len(kinds) * len(lists)),
        out_shape=[jax.ShapeDtypeStruct(shape, kind) for kind in kinds for shape in halves],
        scratch_shapes=there
        + [pltpu.VMEM(shape, kind) for kind in kinds for shape in halves]
        + [pltpu.SemaphoreType.DMA((sum(groups), 2)), pltpu.SemaphoreType.DMA((len(kinds) * len(lists),))],
        compiler_params=pltpu.CompilerParams(vmem_limit_bytes=20 * MIB),
        cost_estimate=QUICK,
        name="halve_far",
    )(*(array for arrays in lists for array in arrays))
    return outs[: len(lists)], outs[len(lists) :]


def halve_near_kernel(joint, count, *refs):
    column = 0
    for i in range(count):
        first, second = refs[2 * i], refs[2 * i + 1]
        half, width = first.shape[0] // 2, first.shape[2]
        sent, kept = (refs[2 * count], refs[2 * count + 1]) if joint else refs[2 * count + 2 * i : 2 * count + 2 * i + 2]
        there = slice(column, column + width) if joint else slice(None)
        sent[:, :, there] = (first[half:].astype(F32) + second[half:].astype(F32)).astype(BF)
        kept[:, :, there] = first[:half].astype(F32) + second[:half].astype(F32)
        column += width


def halve_near(pairs, joint=False):
    count = len(pairs)
    vmem = pl.BlockSpec(memory_space=pltpu.VMEM)
    halves = [(pair[0].shape[0] // 2, *pair[0].shape[1:]) for pair in pairs]
    if joint:
        halves = [(*halves[0][:2], sum(shape[2] for shape in halves))]
    outs = pl.pallas_call(
        functools.partial(halve_near_kernel, joint, count),
        in_specs=[vmem] * (2 * count),
        out_specs=[vmem] * (2 * len(halves)),
        out_shape=[jax.ShapeDtypeStruct(shape, kind) for shape in halves for kind in (BF, F32)],
        compiler_params=pltpu.CompilerParams(vmem_limit_bytes=12 * MIB),
        cost_estimate=QUICK,
        name="halve_near",
    )(*(array for pair in pairs for array in pair))
    return outs[0::2], outs[1::2]


class Sums:
    def __init__(self, keep, send, orders):
        self.pairs = [(mine, swap(other, 0)) for mine, other in zip(keep, send)]
        self.orders = orders

    def far_step(self, phase, values=(), keep=False):
        pairs = [(pltpu.with_memory_space_constraint(pair[0], pltpu.HBM), *pair[1:]) for pair in self.pairs]
        sent, kept = halve_far(pairs, keep)
        sent, values = lax.optimization_barrier((sent, values))
        came = [swap(out, order[phase]) for out, order in zip(sent, self.orders)]
        self.pairs = [(*((kept[i],) if keep else pair), came[i]) for i, pair in enumerate(self.pairs)]
        return values

    def step(self, phase, values=(), **how):
        sent, kept = halve_near(self.pairs, **how)
        sent, values = lax.optimization_barrier((sent, values))
        self.pairs = [(mine, swap(out, order[phase])) for mine, out, order in zip(kept, sent, self.orders)]
        return values

    def came(self, values):
        others, values = lax.optimization_barrier(([pair[-1] for pair in self.pairs], values))
        self.pairs = [(*pair[:-1], other) for pair, other in zip(self.pairs, others)]
        return values


def shares_kernel(loss_ref, early_a, early_b, late_a, late_b, early_ref, late_ref, row_ref):
    early = early_a[0] + early_b[0].astype(F32)
    early_ref[...] = early
    late = late_a[0] + late_b[0].astype(F32)
    late_ref[...] = late
    total = jnp.sum(early * early) + jnp.sum(late * late)
    lanes = lax.broadcasted_iota(jnp.int32, (1, 128), 1)
    row_ref[...] = loss_ref[...] + jnp.where(lanes == 0, total, 0.0)


def shares(loss_part, early, late):
    lines = early[0].shape[1]
    vmem = pl.BlockSpec(memory_space=pltpu.VMEM)
    return pl.pallas_call(
        shares_kernel,
        in_specs=[vmem] * 5,
        out_specs=[vmem] * 3,
        out_shape=(
            jax.ShapeDtypeStruct((lines, EARLY), F32),
            jax.ShapeDtypeStruct((lines, LATE), F32),
            jax.ShapeDtypeStruct((1, 128), F32),
        ),
        compiler_params=pltpu.CompilerParams(vmem_limit_bytes=8 * MIB),
        cost_estimate=QUICK,
        name="shares",
    )(loss_part, *early, *late)


def in_order(keep, send, dims):
    both = jnp.stack([keep, send]).reshape(2, 2, 2, 2, 2, *keep.shape[1:])
    turned = jnp.transpose(both, (*(1 + dims.index(bit) for bit in (4, 3, 2, 1)), 0, 5, 6))
    return turned.reshape(8, 4, *keep.shape[1:])


def scatter_sum(blocks):
    return lax.psum_scatter(
        blocks.astype(F32).reshape(-1, blocks.shape[3]), ("wide", "narrow"), scatter_dimension=0, tiled=True
    )


def sum_all(row):
    count = lax.axis_size("wide") * lax.axis_size("narrow")
    bit = 0
    while 1 << bit < count:
        masks = (1, 2, 3) if bit == 1 else (1,)
        others = [lax.ppermute(row, ("wide", "narrow"), [(i, i ^ (mask << bit)) for i in range(count)]) for mask in masks]
        row = sum(others, row)
        bit += len(masks) // 2 + 1
    return row


def body(
    cond_fields,
    target,
    noise_draw,
    noise_sigma,
    grid_to_mesh,
    mesh_edges,
    mesh_to_grid,
    latitude_row,
    level_index,
    encoder,
    up_proj,
    down_proj,
    readout,
    encoder_moment,
    up_moment,
    down_moment,
    readout_moment,
    encoder_second,
    up_second,
    down_second,
    readout_second,
    encoder_average,
    up_average,
    down_average,
    readout_average,
):
    wide_index = lax.axis_index("wide")
    wide = lax.axis_size("wide")
    globe = lax.axis_index("narrow")
    nodes = mesh_edges.shape[0]
    pixels = cond_fields.shape[1]
    all_nodes = nodes * wide
    width = -(-pixels // 128) * 128

    own_place = [wide_index, globe] if wide == 8 else [0, 0]
    place = jnp.stack([*own_place, globe]).astype(jnp.int32)
    early, late = pack(encoder, up_proj, down_proj.T, readout)
    moving = wide == 8
    tie = lax.optimization_barrier
    if moving:
        early_4 = swap(early, 4)

    latitude, level = latitude_row[None, :], level_index[None, :]
    across = jnp.pad(mesh_to_grid.T - wide_index * nodes, ((0, 0), (0, width - pixels)), constant_values=-1)
    pool, pull = pull_counts(across, nodes)
    if moving:
        early_4, pull, latitude, level = tie((early_4, pull, latitude, level))
        early_1 = joined(early, early_4)
        early_3 = swap(early_1, 3)

    def own(array):
        return lax.dynamic_index_in_dim(jnp.transpose(array, (2, 0, 1)), globe, 1, keepdims=False)

    goal, noise = own(target), own(noise_draw)
    sigma = lax.dynamic_index_in_dim(noise_sigma, globe, 0, keepdims=False)
    square = sigma * sigma
    c_in = lax.rsqrt(square + 1.0)
    if moving:
        early_3, goal, noise = tie((early_3, goal, noise))
        both = joined(early_1, early_3)
        both, goal, noise = tie((both, goal, noise))
        early_2 = swap(both, 2)
    noisy = goal + sigma * noise
    if moving:
        noisy, late = tie((noisy, late))
        late_4 = swap(late, 4)
    grid = jnp.concatenate([own(cond_fields), (c_in * noisy).astype(BF)], axis=0)
    grid = jnp.pad(grid, ((0, 0), (0, width - pixels)))
    edges = mesh_edges.T
    slot_rows = jnp.where(edges >= 0, (edges - wide_index * nodes + nodes + all_nodes) % all_nodes, -1)

    def halo(sums):
        low = sums.astype(BF)
        ring = [(i, (i + 1) % wide) for i in range(wide)]
        return lax.ppermute(low, "wide", ring), lax.ppermute(low, "wide", [(j, i) for i, j in ring])

    if moving:
        sums = grid_sums(grid, grid_to_mesh.T - wide_index * pixels)
        before, after = halo(sums)
        early_2, sums = tie((early_2, sums))
        quad, late_1 = joined(both, early_2), joined(late, late_4)
        quad, late_1, slot_rows = tie((quad, late_1, slot_rows))
        early_0 = swap(quad, 1)
        late_3 = swap(late_1, 3)
        bias = counts(slot_rows)
        bias, late_3 = tie((bias, late_3))
        both = joined(late_1, late_3)
        parts = [both[..., : CUTS[0]], both[..., CUTS[0] :]]
        parts, early_0, before, after = tie((parts, early_0, before, after))
        got = [swap(parts[0], 2), swap(parts[1], 1)]
        halves = [flat(quad), flat(early_0)]
        gathered = halves + [swap(half, 0) for half in halves]
    else:
        gathered, late_full = gather_plain(early, late, wide)
        sums = grid_sums(grid, grid_to_mesh.T - wide_index * pixels)
        bias = counts(slot_rows)
        before, after = halo(sums)

    state0, rows, normed, early_full = encode(place, gathered, before, sums, after)
    if moving:
        got, normed = tie((got, normed))
        parts = [joined(part, one) for part, one in zip(parts, got)]
        parts, normed = tie((parts, normed))
        got = [swap(parts[0], 1), swap(parts[1], 2)]
        halves = [flat(part) for part in parts]
        others = [swap(half, 0) for half in halves]
    mixed, probs, query, pair, inverse = attend(normed, early_full, bias)
    if moving:
        mixed, got, others = tie((mixed, got, others))
        late_full = []
        for half, one, other in zip(halves, got, others):
            late_full += [half, flat(one), other, swap(flat(one), 0)]
    *blocks, grad_state, grad_mixed, grad_scaled, inner, grad_dec, loss_part = feed(
        place, noise_sigma,
        late_full, early_full, state0, mixed, pool, pull, inverse, noisy, goal, latitude, level,
    )
    keep_late, send_late = blocks[:3], blocks[3:]
    if moving:
        late_sum = Sums(keep_late, send_late, ORDERS)
    if moving:
        query, inner = late_sum.far_step(0, (query, inner))
    heads = unmix(probs, query, pair, grad_mixed, grad_scaled, inner, inverse)
    if moving:
        grad_state, heads = late_sum.far_step(1, (grad_state, heads))
    *blocks, = give_back(
        place, early_full, heads, grad_state, rows, normed, before, sums, after, grad_dec
    )
    keep_early, send_early = blocks[:2], blocks[2:]
    if moving:
        keep_early, send_early = late_sum.came((keep_early, send_early))
        early_sum = Sums(keep_early, send_early, DIMS)
        late_sum.pairs = early_sum.step(0, late_sum.pairs)
        late_sum.far_step(2, keep=True)
        late_sum.pairs = early_sum.step(1, late_sum.pairs)
        late_sum.step(3, joint=True)
        early_sum.step(2, joint=True)
        early_sum.step(3)
        share_early, share_late, row = shares(loss_part, early_sum.pairs[0], late_sum.pairs[0])
    else:
        late_lines = jnp.concatenate([in_order(keep_late[i], send_late[i], ORDERS[i]) for i in range(3)], axis=3)
        early_lines = jnp.concatenate([in_order(keep_early[i], send_early[i], DIMS[i]) for i in range(2)], axis=3)
        share_late = scatter_sum(from_rows(late_lines, wide))
        share_early = scatter_sum(early_from_lines(early_lines, wide))
        squares = jnp.sum(share_early * share_early) + jnp.sum(share_late * share_late)
        row = loss_part + jnp.where(lax.broadcasted_iota(jnp.int32, (1, 128), 1) == 0, squares, 0.0)
    row = sum_all(row)
    states = [
        (encoder, encoder_moment, encoder_second, encoder_average),
        (up_proj, up_moment, up_second, up_average),
        (down_proj.T, down_moment.T, down_second.T, down_average.T),
        (readout, readout_moment, readout_second, readout_average),
    ]
    news = list(adam(row, share_early, share_late, states))
    news[10:15] = [array.T for array in news[10:15]]
    return (news[20][0, 0], news[20][0, 1], *news[:20])


def solution(mesh):
    if mesh.shape["narrow"] != GROUPS or MB != GROUPS:
        raise ValueError("narrow size")
    by_pixel = P(None, "wide", None)
    pair = P("wide", "narrow")
    weights = (pair, pair, P("narrow", "wide"), P(("narrow", "wide"), None))
    placed = (by_pixel, by_pixel, by_pixel, P()) + (P("wide", None),) * 3 + (P("wide"), P()) + weights * 4
    given = (P(), P())
    for spec in weights:
        given = given + (spec,) * 5
    return jax.shard_map(body, mesh=mesh, in_specs=placed, out_specs=given, check_vma=False)
```
